32 devices in a mesh: dp: 8 (over y, x, core), heads: 4 (over z).
Axes of the slice: x: 2, y: 2, z: 4, core: 2. Of those that a mesh axis runs over, the one named last changes fastest.
Arguments:
- block_input: bfloat16 [8192, 2048], P(('dp', 'heads')), may hold values from -6 to 6
- doc_ids: int32 [8192], P('dp'), may hold values from 0 to 15, as said below
- pad_mask: int32 [8192], P('dp'), may hold values from 0 to 1, as said below
- first_gain: bfloat16 [2048], replicated, may hold values from 0.5 to 1.5
- qkv_weight: bfloat16 [3, 2048, 2048], P(None, None, 'heads'), may hold values from -0.125 to 0.125
- beta_weight: bfloat16 [2048, 16], P(None, 'heads'), may hold values from -0.125 to 0.125
- conv_weight: bfloat16 [3, 4, 2048], P(None, None, 'heads'), may hold values from -3 to 3
- out_gain: bfloat16 [128], replicated, may hold values from 0.5 to 1.5
- out_weight: bfloat16 [2048, 2048], P('heads'), may hold values from -0.125 to 0.125
- second_gain: bfloat16 [2048], replicated, may hold values from 0.5 to 1.5
- gate_up_weight: bfloat16 [2, 2048, 5632], P(None, None, 'heads'), may hold values from -0.125 to 0.125
- down_weight: bfloat16 [5632, 2048], P('heads'), may hold values from -0.078125 to 0.078125
- cotangent: bfloat16 [8192, 2048], P(('dp', 'heads')), may hold values from -6 to 6
Outputs:
- block_output: bfloat16 [8192, 2048], P(('dp', 'heads'))
- input_grad: float32 [8192, 2048], P(('dp', 'heads'))
- first_gain_grad: float32 [2048], replicated
- qkv_grad: float32 [3, 2048, 2048], P(None, None, 'heads')
- beta_grad: float32 [2048, 16], P(None, 'heads')
- conv_grad: float32 [3, 4, 2048], P(None, None, 'heads')
- out_gain_grad: float32 [128], replicated
- out_grad: float32 [2048, 2048], P('heads')
- second_gain_grad: float32 [2048], replicated
- gate_up_grad: float32 [2, 2048, 5632], P(None, None, 'heads')
- down_grad: float32 [5632, 2048], P('heads')
The draws below stay inside these ranges and needn't reach their ends.
Inputs may be any that keep to these rules, and one draw needn't show every extreme that they name: `doc_ids`: within each group of 1024 tokens the document number starts at 0, never falls, rises by at most one and changes only at multiples of 64; in one group all tokens belong to a single document, and in another every block of 64 tokens begins a new document. `pad_mask`: padding lies only at the end of a document, fewer than 64 tokens of it.
All inputs are finite; a program needn't handle non-finite values.
Results may differ from the reference program's by a relative error of at most 0.02.
Values may be sent and summed in bfloat16 or wider, within the bound.
No kernel may reach another device: no remote copies, remote signals or barrier semaphores. Data moves between devices by JAX's collectives and lax.ppermute only.
A program may use at most 320 MiB of HBM per device.

```python
import jax
import jax.numpy as jnp
from jax import lax

D = 2048
HEADS = 16
HEAD_DIM = 128
FF = 5632
SPAN = 64
CONV = 4
GROUP_TOK = 1024
TOKENS = 8192
N_DP = 8


def layout(key):
    groups = TOKENS // GROUP_TOK
    blocks = GROUP_TOK // SPAN
    base_key = jax.random.fold_in(key, 11)
    first_key, second_key, third_key = jax.random.split(base_key, 3)
    column = jnp.arange(blocks)
    begins = (jax.random.randint(first_key, (groups, blocks), 0, 4) == 0).astype(jnp.int32)
    begins = jnp.where(column[None, :] == 0, 1, begins)
    whole_group = jax.random.randint(second_key, (), 0, groups)
    single = jnp.arange(groups)[:, None] == whole_group
    every_group = (whole_group + 1) % groups
    every = jnp.arange(groups)[:, None] == every_group
    begins = jnp.where(every, jnp.ones_like(begins), begins)
    begins = jnp.where(single, (column[None, :] == 0).astype(jnp.int32), begins)
    numbers = jnp.cumsum(begins, axis=1) - 1
    ending = jnp.concatenate([begins[:, 1:], jnp.ones((groups, 1), jnp.int32)], axis=1) == 1
    spare_count = jax.random.randint(third_key, (groups, blocks), 0, SPAN)
    spare_count = jnp.where(ending & jnp.logical_not(single), spare_count, 0)
    position = jnp.arange(SPAN)
    keep_mask = (position[None, None, :] < SPAN - spare_count[:, :, None]).astype(jnp.int32)
    doc_numbers = jnp.broadcast_to(numbers[:, :, None], (groups, blocks, SPAN)).astype(jnp.int32)
    return (doc_numbers.reshape(TOKENS), keep_mask.reshape(TOKENS))


def draw_doc_ids(key, part):
    return layout(key)[0]


def draw_pad_mask(key, part):
    return layout(key)[1]


def steps_of(key, extent, shards, low, largest):
    gain = 1.0
    for dim, blocks in shards:
        heights = jax.random.uniform(jax.random.fold_in(jax.random.fold_in(key, 6), dim), (blocks,), jnp.float32, low / len(shards), largest / len(shards))
        gain = gain * jnp.repeat(jnp.exp(heights), extent[dim] // blocks).reshape((-1,) + (1,) * (len(extent) - 1 - dim))
    return gain


def bell_draw(stream_key, dims, scale, most, cuts=(), held_as=jnp.bfloat16):
    gain = steps_of(stream_key, dims, cuts, -0.22, 0.18) if cuts else 1.0
    drawn = jax.random.normal(stream_key, dims, jnp.float32) * scale * gain
    return jnp.minimum(jnp.maximum(drawn, -most), most).astype(held_as)


def setup_inputs(seed: int = 0) -> dict:
    arg_keys = jax.random.split(jax.random.key(seed), 14)
    block_input = bell_draw(arg_keys[0], (TOKENS, D), 1.0, 6.0, ((0, 32),))
    doc_ids = draw_doc_ids(jax.random.fold_in(arg_keys[13], 71), 0)
    pad_mask = draw_pad_mask(jax.random.fold_in(arg_keys[13], 71), 0)
    first_gain = jnp.clip(1.0 + 0.1 * jax.random.normal(arg_keys[3], (D,), jnp.float32), 0.5, 1.5).astype(jnp.bfloat16)
    qkv_weight = bell_draw(arg_keys[4], (3, D, HEADS * HEAD_DIM), D ** -0.5, 0.125, ((2, 4),))
    beta_weight = bell_draw(arg_keys[5], (D, HEADS), D ** -0.5, 0.125, ((1, 4),))
    conv_weight = bell_draw(arg_keys[6], (3, CONV, HEADS * HEAD_DIM), 0.5, 3.0, ((2, 4),))
    out_gain = jnp.clip(1.0 + 0.1 * jax.random.normal(arg_keys[7], (HEAD_DIM,), jnp.float32), 0.5, 1.5).astype(jnp.bfloat16)
    out_weight = bell_draw(arg_keys[8], (HEADS * HEAD_DIM, D), (HEADS * HEAD_DIM) ** -0.5, 0.125, ((0, 4),))
    second_gain = jnp.clip(1.0 + 0.1 * jax.random.normal(arg_keys[9], (D,), jnp.float32), 0.5, 1.5).astype(jnp.bfloat16)
    gate_up_weight = bell_draw(arg_keys[10], (2, D, FF), D ** -0.5, 0.125, ((2, 4),))
    down_weight = bell_draw(arg_keys[11], (FF, D), FF ** -0.5, 0.078125, ((0, 4),))
    cotangent = bell_draw(arg_keys[12], (TOKENS, D), 1.0, 6.0, ((0, 32),))
    return dict(block_input=block_input, doc_ids=doc_ids, pad_mask=pad_mask, first_gain=first_gain, qkv_weight=qkv_weight, beta_weight=beta_weight, conv_weight=conv_weight, out_gain=out_gain, out_weight=out_weight, second_gain=second_gain, gate_up_weight=gate_up_weight, down_weight=down_weight, cotangent=cotangent)


@jax.custom_vjp
def low(v):
    return lax.optimization_barrier(v.astype(jnp.bfloat16)).astype(jnp.float32)

@jax.custom_vjp
def low_back(v):
    return v

def low_keep(v):
    return (low(v), None)

def low_pass(kept, grad):
    return (grad,)

def back_keep(v):
    return (v, None)

def back_low(kept, grad):
    return (low(grad),)
low.defvjp(low_keep, low_pass)
low_back.defvjp(back_keep, back_low)
highest = lax.Precision.HIGHEST

def rms_scale(rows, epsilon):
    return rows * lax.rsqrt(lax.optimization_barrier(jnp.mean(rows * rows, axis=-1, keepdims=True)) + epsilon)

def lower_solve(matrix, right):
    return jax.scipy.linalg.solve_triangular(matrix, right, lower=True, unit_diagonal=True)

def delta_rule(queries, keys, values, betas, resets):
    length, heads, width = queries.shape
    blocks = length // SPAN

    def split_blocks(array):
        return array.reshape(blocks, SPAN, heads, width).transpose(0, 2, 1, 3)
    below = jnp.tril(jnp.ones((SPAN, SPAN), jnp.float32), -1)
    upto = jnp.tril(jnp.ones((SPAN, SPAN), jnp.float32))
    unit_eye = jnp.eye(SPAN, dtype=jnp.float32)
    factor = width ** (-0.5)
    query_all = split_blocks(queries)
    key_all = split_blocks(keys)
    value_all = split_blocks(values)
    beta_all = betas.reshape(blocks, SPAN, heads).transpose(0, 2, 1)
    key_beta = key_all * beta_all[..., None]
    value_beta = value_all * beta_all[..., None]
    inner = jnp.einsum('bhcd,bhed->bhce', key_beta, key_all, precision=highest) * below
    joined = jnp.concatenate([key_beta, value_beta], axis=3)
    system = (unit_eye[None, None] + inner).reshape(blocks * heads, SPAN, SPAN)
    solved = jax.vmap(lower_solve)(system, joined.reshape(blocks * heads, SPAN, 2 * width))
    solved = solved.reshape(blocks, heads, SPAN, 2 * width)
    wy_keys_all = solved[..., :width]
    wy_values_all = solved[..., width:]

    def block_step(state, inputs):
        query_blk, key_blk, wy_keys, wy_values, flag = inputs
        state = state * (1.0 - flag)
        fresh = wy_values - jnp.einsum('hcd,hde->hce', wy_keys, state, precision=highest)
        scores = jnp.einsum('hcd,hed->hce', query_blk, key_blk, precision=highest) * upto
        result = factor * (jnp.einsum('hcd,hde->hce', query_blk, state, precision=highest) + jnp.einsum('hce,hed->hcd', scores, fresh, precision=highest))
        state = state + jnp.einsum('hcd,hce->hde', key_blk, fresh, precision=highest)
        return (state, result)
    start_state = jnp.zeros((heads, width, width), jnp.float32)
    _, results = lax.scan(jax.checkpoint(block_step), start_state, (query_all, key_all, wy_keys_all, wy_values_all, resets))
    return results.transpose(0, 2, 1, 3).reshape(length, heads, width)

def mixer(pre_conv, beta_logit, conv_weight, out_gain, doc_ids, pad_float):
    length = pre_conv.shape[0]
    width = conv_weight.shape[2]
    heads = width // HEAD_DIM
    stacked = pre_conv.reshape(length, 3, width)
    summed = stacked * conv_weight[:, 0][None]
    for shift_by in range(1, CONV):
        earlier = jnp.concatenate([jnp.full((shift_by,), -1, jnp.int32), doc_ids[:length - shift_by]])
        same_doc = (earlier == doc_ids).astype(jnp.float32)
        moved = jnp.concatenate([jnp.zeros((shift_by, 3, width), jnp.float32), stacked[:length - shift_by]], axis=0)
        summed = summed + moved * conv_weight[:, shift_by][None] * same_doc[:, None, None]
    active = jax.nn.silu(summed)

    def unit_rows(block):
        split_rows = block.reshape(length, heads, HEAD_DIM)
        return split_rows * lax.rsqrt(lax.optimization_barrier(jnp.sum(split_rows * split_rows, axis=-1, keepdims=True)) + 1e-06)
    queries = unit_rows(active[:, 0])
    keys = unit_rows(active[:, 1]) * pad_float[:, None, None]
    values = active[:, 2].reshape(length, heads, HEAD_DIM)
    betas = jax.nn.sigmoid(beta_logit) * pad_float[:, None]
    firsts = doc_ids[::SPAN]
    lasts = doc_ids[SPAN - 1::SPAN]
    before = jnp.concatenate([jnp.full((1,), -1, jnp.int32), lasts[:-1]])
    resets = (firsts != before).astype(jnp.float32)
    outputs = delta_rule(queries, keys, values, betas, resets)
    normed = outputs * lax.rsqrt(lax.optimization_barrier(jnp.mean(outputs * outputs, axis=-1, keepdims=True)) + 1e-05) * out_gain
    return normed.reshape(length, width)

def block_forward(rows, params, doc_ids, pad_float):
    first_gain, qkv_weight, beta_weight, conv_weight, out_gain, out_weight, second_gain, gate_up_weight, down_weight = params
    width = qkv_weight.shape[2]
    xn_first = low(rms_scale(rows, 1e-06) * first_gain)
    weight_cat = jnp.concatenate([qkv_weight[0], qkv_weight[1], qkv_weight[2], beta_weight], axis=1)
    projected = low_back(jnp.dot(xn_first.astype(jnp.float32), weight_cat.astype(jnp.float32), precision=highest, preferred_element_type=jnp.float32))
    normed_out = mixer(projected[:, :3 * width], projected[:, 3 * width:], conv_weight, out_gain, doc_ids, pad_float)
    mixed = low_back(jnp.dot(low(normed_out).astype(jnp.float32), out_weight.astype(jnp.float32), precision=highest, preferred_element_type=jnp.float32))
    hidden_one = rows + mixed
    xn_second = low(rms_scale(hidden_one, 1e-06) * second_gain)
    gate_value = low_back(jnp.dot(xn_second.astype(jnp.float32), gate_up_weight[0].astype(jnp.float32), precision=highest, preferred_element_type=jnp.float32))
    up_value = low_back(jnp.dot(xn_second.astype(jnp.float32), gate_up_weight[1].astype(jnp.float32), precision=highest, preferred_element_type=jnp.float32))
    hidden = low(jax.nn.silu(gate_value) * up_value)
    return hidden_one + low_back(jnp.dot(hidden.astype(jnp.float32), down_weight.astype(jnp.float32), precision=highest, preferred_element_type=jnp.float32))

def reference(block_input, doc_ids, pad_mask, first_gain, qkv_weight, beta_weight, conv_weight, out_gain, out_weight, second_gain, gate_up_weight, down_weight, cotangent):
    params = tuple((array.astype(jnp.float32) for array in (first_gain, qkv_weight, beta_weight, conv_weight, out_gain, out_weight, second_gain, gate_up_weight, down_weight)))
    groups = N_DP
    inputs = (block_input.astype(jnp.float32).reshape(groups, GROUP_TOK, D), cotangent.astype(jnp.float32).reshape(groups, GROUP_TOK, D), doc_ids.reshape(groups, GROUP_TOK), pad_mask.astype(jnp.float32).reshape(groups, GROUP_TOK))

    def group_step(totals, item):
        rows, grad_rows, seg_ids, pad_float = item

        def forward(values, *weights):
            return block_forward(values, weights, seg_ids, pad_float)
        output, backward = jax.vjp(forward, rows, *params)
        grads = backward(grad_rows * pad_float[:, None])
        totals = tuple((total + grad for total, grad in zip(totals, grads[1:])))
        return (totals, (output.astype(jnp.bfloat16), grads[0]))
    zeros_init = tuple((jnp.zeros_like(param) for param in params))
    totals, (outputs, input_grads) = lax.scan(group_step, zeros_init, inputs)
    return (outputs.reshape(TOKENS, D), input_grads.reshape(TOKENS, D), totals[0], totals[1], totals[2], totals[3], totals[4], totals[5], totals[6], totals[7], totals[8])
```

```python
import functools
import jax
import jax.numpy as jnp
from jax import lax
from jax.experimental import pallas as pl
from jax.experimental.pallas import tpu as pltpu

HEAD_DIM = 128
CONV = 4
TILE = 256
HALO = 8
f32 = jnp.float32
bf16 = jnp.bfloat16


def mm(a, b):
    return jnp.dot(a.astype(bf16), b.astype(bf16), preferred_element_type=f32)


def mm_nt(a, b):
    return lax.dot_general(
        a.astype(bf16), b.astype(bf16), (((1,), (1,)), ((), ())), preferred_element_type=f32
    )


def mm_tn(a, b):
    return lax.dot_general(
        a.astype(bf16), b.astype(bf16), (((0,), (0,)), ((), ())), preferred_element_type=f32
    )


def token_table(doc_ids, pad_float, tile):
    length = doc_ids.shape[0]
    minus = jnp.full((tile,), -1, jnp.int32)
    padded = jnp.concatenate([minus, doc_ids, minus])

    def same(shift):
        moved = lax.slice_in_dim(padded, tile - shift, tile - shift + length, axis=0)
        return (moved == doc_ids).astype(f32)

    tiles = doc_ids.reshape(length // tile, tile)
    ends = tiles[:, -1]
    before = jnp.concatenate([jnp.full((1,), -1, jnp.int32), ends[:-1]])
    from_start = (tiles == before[:, None]).astype(f32).reshape(length)
    to_end = (tiles == ends[:, None]).astype(f32).reshape(length)
    columns = [same(1), same(2), same(3), pad_float, from_start, to_end, same(-1), same(-2), same(-3)]
    columns += [jnp.zeros((length,), f32)] * (16 - len(columns))
    return jnp.stack(columns, axis=1)


def sigmoid(x):
    return 1.0 / (1.0 + jnp.exp(-x))


def split_dot(a_hi, a_lo, b_hi, b_lo):
    return (
        jnp.dot(a_hi, b_hi, preferred_element_type=f32)
        + jnp.dot(a_lo, b_hi, preferred_element_type=f32)
        + jnp.dot(a_hi, b_lo, preferred_element_type=f32)
    )


def halves(a):
    hi = a.astype(bf16)
    return hi, (a - hi.astype(f32)).astype(bf16)


def unit_inverse(strict, row, col):
    size = strict.shape[0]
    apart = row ^ col
    eye = (row == col).astype(f32)
    zero = jnp.zeros_like(strict)
    inverse = eye - jnp.where(apart == 1, strict, zero)
    step = 2
    while step < size:
        part = jnp.where((apart >= step) & (apart < 2 * step), strict, zero)
        low = inverse.astype(bf16)
        inverse = inverse - mm(low, mm(part, low))
        step *= 2
    a_hi, a_lo = halves(strict)
    x_hi, x_lo = halves(inverse)
    rest = eye - inverse - split_dot(a_hi, a_lo, x_hi, x_lo)
    return inverse + mm(x_hi, rest)


def conv_sum(ext_ref, part, lanes, taps, same):
    total = ext_ref[part, pl.ds(HALO, TILE), lanes] * taps[0]
    for shift in range(1, CONV):
        total = total + ext_ref[part, pl.ds(HALO - shift, TILE), lanes] * taps[shift] * same[shift - 1]
    return total


def forward_kernel(
    heads, q_ref, k_ref, v_ref, beta_ref, table_ref, doc_col_ref, doc_row_ref, conv_ref, gain_ref,
    normed_ref, out_ref, fresh_ref, inv_ref, start_ref, ext_ref, state_ref,
):
    tile = pl.program_id(0)
    factor = HEAD_DIM ** (-0.5)

    @pl.when(tile == 0)
    def _():
        state_ref[...] = jnp.zeros_like(state_ref)
        ext_ref[:, pl.ds(0, HALO), :] = jnp.zeros((3, HALO, ext_ref.shape[2]), f32)

    @pl.when(tile > 0)
    def _():
        ext_ref[:, pl.ds(0, HALO), :] = ext_ref[:, pl.ds(TILE, HALO), :]

    for part, ref in enumerate((q_ref, k_ref, v_ref)):
        ext_ref[part, pl.ds(HALO, TILE), :] = ref[...].astype(f32)
    wide = (TILE, HEAD_DIM)
    same = [jnp.broadcast_to(table_ref[:, j : j + 1], wide) for j in range(3)]
    pad = table_ref[:, 3:4]
    from_start = jnp.broadcast_to(table_ref[:, 4:5], wide)
    to_end = jnp.broadcast_to(table_ref[:, 5:6], wide)
    carry = table_ref[TILE - 1 : TILE, 4:5]
    row = lax.broadcasted_iota(jnp.int32, (TILE, TILE), 0)
    col = lax.broadcasted_iota(jnp.int32, (TILE, TILE), 1)
    together = doc_col_ref[...] == doc_row_ref[...]
    below = together & (row > col)
    upto = together & (row >= col)
    gain = gain_ref[...]
    for head in range(heads):
        lanes = pl.ds(head * HEAD_DIM, HEAD_DIM)
        acts = []
        for part in range(3):
            taps = [conv_ref[part * CONV + j : part * CONV + j + 1, lanes] for j in range(CONV)]
            total = conv_sum(ext_ref, part, lanes, taps, same)
            acts.append(total * sigmoid(total))
        query = acts[0] * lax.rsqrt(jnp.sum(acts[0] * acts[0], axis=1, keepdims=True) + 1e-06)
        key = acts[1] * (lax.rsqrt(jnp.sum(acts[1] * acts[1], axis=1, keepdims=True) + 1e-06) * pad)
        beta = sigmoid(beta_ref[:, head : head + 1]) * pad
        key = key.astype(bf16)
        query = query.astype(bf16)
        inner = mm_nt(key, key)
        strict = jnp.where(below, inner * beta, 0.0)
        inverse = unit_inverse(strict, row, col).astype(bf16)
        inv_ref[head] = inverse
        state = state_ref[head]
        low_state = state.astype(bf16)
        start_ref[0, head] = low_state
        right = beta * (acts[2] - from_start * mm(key, low_state))
        fresh = mm(inverse, right).astype(bf16)
        fresh_ref[:, lanes] = fresh
        scores = jnp.where(upto, mm_nt(query, key), 0.0)
        out = factor * (from_start * mm(query, low_state) + mm(scores, fresh))
        state_ref[head] = carry * state + mm_tn(key.astype(f32) * to_end, fresh)
        out_ref[:, lanes] = out
        scale = lax.rsqrt(jnp.mean(out * out, axis=1, keepdims=True) + 1e-05)
        normed_ref[:, lanes] = (out * scale * gain).astype(bf16)


def mixer_forward(q_pre, k_pre, v_pre, beta_logit, table, doc_ids, conv, gain):
    length, width = q_pre.shape
    heads = width // HEAD_DIM
    tiles = length // TILE
    wide = pl.BlockSpec((TILE, width), lambda i: (i, 0))
    flops = 2 * tiles * heads * TILE * TILE * (TILE * 18 + HEAD_DIM * 6)
    return pl.pallas_call(
        functools.partial(forward_kernel, heads),
        grid=(tiles,),
        in_specs=[
            wide, wide, wide,
            pl.BlockSpec((TILE, heads), lambda i: (i, 0)),
            pl.BlockSpec((TILE, 16), lambda i: (i, 0)),
            pl.BlockSpec((TILE, 1), lambda i: (i, 0)),
            pl.BlockSpec((1, TILE), lambda i: (0, i)),
            pl.BlockSpec((3 * CONV, width), lambda i: (0, 0)),
            pl.BlockSpec((1, HEAD_DIM), lambda i: (0, 0)),
        ],
        out_specs=[
            wide, wide, wide,
            pl.BlockSpec((heads, TILE, TILE), lambda i: (0, i, 0)),
            pl.BlockSpec((1, heads, HEAD_DIM, HEAD_DIM), lambda i: (i, 0, 0, 0)),
        ],
        out_shape=[
            jax.ShapeDtypeStruct((length, width), bf16),
            jax.ShapeDtypeStruct((length, width), f32),
            jax.ShapeDtypeStruct((length, width), bf16),
            jax.ShapeDtypeStruct((heads, length, TILE), bf16),
            jax.ShapeDtypeStruct((tiles, heads, HEAD_DIM, HEAD_DIM), bf16),
        ],
        scratch_shapes=[
            pltpu.VMEM((3, TILE + HALO, width), f32),
            pltpu.VMEM((heads, HEAD_DIM, HEAD_DIM), f32),
        ],
        compiler_params=pltpu.CompilerParams(vmem_limit_bytes=48 * 1024 * 1024),
        cost_estimate=pl.CostEstimate(
            flops=flops, bytes_accessed=length * width * 24, transcendentals=length * width * 6
        ),
        name="mixer_forward",
    )(
        q_pre, k_pre, v_pre, beta_logit, table,
        doc_ids.reshape(length, 1), doc_ids.reshape(1, length), conv, gain.reshape(1, HEAD_DIM),
    )


def backward_kernel(
    heads, q_ref, k_ref, v_ref, q_halo_ref, k_halo_ref, v_halo_ref,
    beta_ref, table_ref, doc_col_ref, doc_row_ref, conv_ref, gain_ref,
    out_ref, fresh_ref, inv_ref, start_ref, cot_ref,
    dq_ref, dk_ref, dv_ref, dbeta_ref, dconv_ref, dgain_ref, ext_ref, back_ref, state_ref,
):
    step = pl.program_id(0)
    factor = HEAD_DIM ** (-0.5)
    width = q_ref.shape[1]

    @pl.when(step == 0)
    def _():
        state_ref[...] = jnp.zeros_like(state_ref)
        back_ref[:, pl.ds(TILE, HALO), :] = jnp.zeros((3, HALO, width), f32)
        dconv_ref[...] = jnp.zeros_like(dconv_ref)
        dgain_ref[...] = jnp.zeros_like(dgain_ref)

    @pl.when(step > 0)
    def _():
        back_ref[:, pl.ds(TILE, HALO), :] = back_ref[:, pl.ds(0, HALO), :]

    for part, (ref, halo) in enumerate(
        ((q_ref, q_halo_ref), (k_ref, k_halo_ref), (v_ref, v_halo_ref))
    ):
        ext_ref[part, pl.ds(0, HALO), :] = halo[...].astype(f32)
        ext_ref[part, pl.ds(HALO, TILE), :] = ref[...].astype(f32)
    wide = (TILE, HEAD_DIM)
    same = [jnp.broadcast_to(table_ref[:, j : j + 1], wide) for j in range(3)]
    after = [jnp.broadcast_to(table_ref[:, 6 + j : 7 + j], wide) for j in range(3)]
    pad = table_ref[:, 3:4]
    from_start = jnp.broadcast_to(table_ref[:, 4:5], wide)
    to_end = jnp.broadcast_to(table_ref[:, 5:6], wide)
    carry = table_ref[TILE - 1 : TILE, 4:5]
    row = lax.broadcasted_iota(jnp.int32, (TILE, TILE), 0)
    col = lax.broadcasted_iota(jnp.int32, (TILE, TILE), 1)
    together = doc_col_ref[...] == doc_row_ref[...]
    below = together & (row > col)
    upto = together & (row >= col)
    gain = gain_ref[...]
    dgain = jnp.zeros((1, HEAD_DIM), f32)
    for head in range(heads):
        lanes = pl.ds(head * HEAD_DIM, HEAD_DIM)
        sums, sigs, acts = [], [], []
        for part in range(3):
            taps = [conv_ref[part * CONV + j : part * CONV + j + 1, lanes] for j in range(CONV)]
            total = conv_sum(ext_ref, part, lanes, taps, same)
            sig = sigmoid(total)
            sums.append(total)
            sigs.append(sig)
            acts.append(total * sig)
        q_scale = lax.rsqrt(jnp.sum(acts[0] * acts[0], axis=1, keepdims=True) + 1e-06)
        k_scale = lax.rsqrt(jnp.sum(acts[1] * acts[1], axis=1, keepdims=True) + 1e-06)
        query_full = acts[0] * q_scale
        key_unit = acts[1] * k_scale
        beta_sig = sigmoid(beta_ref[:, head : head + 1])
        beta = beta_sig * pad
        key_full = key_unit * pad
        key = key_full.astype(bf16)
        query = query_full.astype(bf16)
        value = acts[2]
        out = out_ref[:, lanes]
        cot = cot_ref[:, lanes].astype(f32)
        scale = lax.rsqrt(jnp.mean(out * out, axis=1, keepdims=True) + 1e-05)
        unit = out * scale
        dgain = dgain + jnp.sum(cot * unit, axis=0, keepdims=True)
        gained = cot * gain
        dout = (factor * scale) * (gained - unit * jnp.mean(unit * gained, axis=1, keepdims=True))
        dout_low = dout.astype(bf16)
        dout_first = (dout * from_start).astype(bf16)
        fresh = fresh_ref[:, lanes]
        start = start_ref[0, head]
        dstate = state_ref[head]
        dstate_low = dstate.astype(bf16)
        inverse = inv_ref[head]
        key_end = (key_full * to_end).astype(bf16)
        scores = jnp.where(upto, mm_nt(query, key), 0.0).astype(bf16)
        dfresh = mm_tn(scores, dout_low) + mm(key_end, dstate_low)
        dright = mm_tn(inverse, dfresh)
        dright_low = dright.astype(bf16)
        dscores = jnp.where(upto, mm_nt(dout_low, fresh), 0.0).astype(bf16)
        dquery = mm_nt(dout_first, start) + mm(dscores, key)
        dstrict = jnp.where(below, -mm_nt(dright_low, fresh), 0.0)
        scaled = (dstrict * beta).astype(bf16)
        weighted = (dright * (beta * from_start)).astype(bf16)
        inner_key = mm(dstrict, key)
        start_key = from_start * mm_nt(dright_low, start)
        dkey = (
            mm_tn(dscores, query)
            + to_end * mm_nt(fresh, dstate_low)
            + beta * (inner_key - start_key)
            + mm_tn(scaled, key)
        )
        dbeta = jnp.sum(
            dright * value + (inner_key - start_key) * key_full, axis=1, keepdims=True
        )
        dvalue = beta * dright
        state_ref[head] = (
            carry * dstate + mm_tn(query, dout_first) - mm_tn(key, weighted)
        )
        dbeta_ref[:, head : head + 1] = dbeta * pad * beta_sig * (1.0 - beta_sig)
        dkey = dkey * pad
        dacts = (
            q_scale * (dquery - query_full * jnp.sum(query_full * dquery, axis=1, keepdims=True)),
            k_scale * (dkey - key_unit * jnp.sum(key_unit * dkey, axis=1, keepdims=True)),
            dvalue,
        )
        for part, target in enumerate((dq_ref, dk_ref, dv_ref)):
            sig = sigs[part]
            dsum = dacts[part] * (sig * (1.0 + sums[part] * (1.0 - sig)))
            back_ref[part, pl.ds(0, TILE), lanes] = dsum
            taps = [conv_ref[part * CONV + j : part * CONV + j + 1, lanes] for j in range(CONV)]
            dpre = dsum * taps[0]
            dtaps = [jnp.sum(dsum * ext_ref[part, pl.ds(HALO, TILE), lanes], axis=0, keepdims=True)]
            for shift in range(1, CONV):
                dpre = dpre + back_ref[part, pl.ds(shift, TILE), lanes] * (after[shift - 1] * taps[shift])
                moved = ext_ref[part, pl.ds(HALO - shift, TILE), lanes]
                dtaps.append(jnp.sum(dsum * moved * same[shift - 1], axis=0, keepdims=True))
            target[:, lanes] = dpre.astype(bf16)
            for j in range(CONV):
                spot = slice(part * CONV + j, part * CONV + j + 1)
                dconv_ref[spot, lanes] = dconv_ref[spot, lanes] + dtaps[j]
    dgain_ref[...] = dgain_ref[...] + dgain


def mixer_backward(q_pre, k_pre, v_pre, beta_logit, table, doc_ids, conv, gain, saved, cot):
    out, fresh, inverse, start = saved
    length, width = q_pre.shape
    heads = width // HEAD_DIM
    tiles = length // TILE
    last = tiles - 1
    wide = pl.BlockSpec((TILE, width), lambda i: (last - i, 0))
    per = TILE // HALO
    halo = pl.BlockSpec((HALO, width), lambda i: (jnp.maximum((last - i) * per - 1, 0), 0))
    flops = 2 * tiles * heads * TILE * HEAD_DIM * (TILE * 9 + HEAD_DIM * 6)
    return pl.pallas_call(
        functools.partial(backward_kernel, heads),
        grid=(tiles,),
        in_specs=[
            wide, wide, wide, halo, halo, halo,
            pl.BlockSpec((TILE, heads), lambda i: (last - i, 0)),
            pl.BlockSpec((TILE, 16), lambda i: (last - i, 0)),
            pl.BlockSpec((TILE, 1), lambda i: (last - i, 0)),
            pl.BlockSpec((1, TILE), lambda i: (0, last - i)),
            pl.BlockSpec((3 * CONV, width), lambda i: (0, 0)),
            pl.BlockSpec((1, HEAD_DIM), lambda i: (0, 0)),
            wide, wide,
            pl.BlockSpec((heads, TILE, TILE), lambda i: (0, last - i, 0)),
            pl.BlockSpec((1, heads, HEAD_DIM, HEAD_DIM), lambda i: (last - i, 0, 0, 0)),
            wide,
        ],
        out_specs=[
            wide, wide, wide,
            pl.BlockSpec((TILE, heads), lambda i: (last - i, 0)),
            pl.BlockSpec((3 * CONV, width), lambda i: (0, 0)),
            pl.BlockSpec((1, HEAD_DIM), lambda i: (0, 0)),
        ],
        out_shape=[
            jax.ShapeDtypeStruct((length, width), bf16),
            jax.ShapeDtypeStruct((length, width), bf16),
            jax.ShapeDtypeStruct((length, width), bf16),
            jax.ShapeDtypeStruct((length, heads), f32),
            jax.ShapeDtypeStruct((3 * CONV, width), f32),
            jax.ShapeDtypeStruct((1, HEAD_DIM), f32),
        ],
        scratch_shapes=[
            pltpu.VMEM((3, TILE + HALO, width), f32),
            pltpu.VMEM((3, TILE + HALO, width), f32),
            pltpu.VMEM((heads, HEAD_DIM, HEAD_DIM), f32),
        ],
        compiler_params=pltpu.CompilerParams(vmem_limit_bytes=48 * 1024 * 1024),
        cost_estimate=pl.CostEstimate(
            flops=flops, bytes_accessed=length * width * 30, transcendentals=length * width * 6
        ),
        name="mixer_backward",
    )(
        q_pre, k_pre, v_pre, q_pre, k_pre, v_pre, beta_logit, table,
        doc_ids.reshape(length, 1), doc_ids.reshape(1, length), conv, gain.reshape(1, HEAD_DIM),
        out, fresh, inverse, start, cot,
    )


from jax.sharding import PartitionSpec as P


def dot_f32(a, b):
    return jnp.dot(a, b, preferred_element_type=f32)


def rms_forward(rows, gain):
    scale = lax.rsqrt(jnp.mean(rows * rows, axis=-1, keepdims=True) + 1e-06)
    return (rows * scale * gain).astype(bf16), scale


def rms_backward(rows, scale, gain, grad):
    scaled = grad * gain
    mean = jnp.mean(scaled * rows, axis=-1, keepdims=True)
    gain_grad = jnp.sum(grad * rows * scale, axis=0)
    return scale * scaled - (scale * scale * scale) * rows * mean, gain_grad


def gather_rows(rows):
    return lax.all_gather(rows, "heads", axis=0, tiled=True)


def scatter_rows(partial):
    return lax.psum_scatter(
        partial.astype(bf16), "heads", scatter_dimension=0, tiled=True
    ).astype(f32)


def shards(
    block_input,
    doc_ids,
    pad_mask,
    first_gain,
    qkv_weight,
    beta_weight,
    conv_weight,
    out_gain,
    out_weight,
    second_gain,
    gate_up_weight,
    down_weight,
    cotangent,
):
    local_rows, model_width = block_input.shape
    width = qkv_weight.shape[2]
    pad_float = pad_mask.astype(f32)
    row_offset = lax.axis_index("heads") * local_rows
    pad_rows = lax.dynamic_slice_in_dim(pad_float, row_offset, local_rows, 0)
    rows_float = block_input.astype(f32)
    first_float = first_gain.astype(f32)
    second_float = second_gain.astype(f32)
    conv_float = conv_weight.astype(f32).reshape(3 * CONV, width)
    gain_float = out_gain.astype(f32)
    table = token_table(doc_ids, pad_float, TILE)

    xn_first, first_scale = rms_forward(rows_float, first_float)
    full_first = gather_rows(xn_first)
    pres = [dot_f32(full_first, qkv_weight[i]) for i in range(3)]
    beta_logit = dot_f32(full_first, beta_weight)
    mixer_low, *saved = mixer_forward(*pres, beta_logit, table, doc_ids, conv_float, gain_float)
    mixed = scatter_rows(dot_f32(mixer_low, out_weight))
    hidden_one = rows_float + mixed
    xn_second, second_scale = rms_forward(hidden_one, second_float)
    full_second = gather_rows(xn_second)
    gate_value = dot_f32(full_second, gate_up_weight[0])
    up_value = dot_f32(full_second, gate_up_weight[1])
    gate_sig = jax.nn.sigmoid(gate_value)
    swish = gate_value * gate_sig
    hidden = (swish * up_value).astype(bf16)
    output = hidden_one + scatter_rows(dot_f32(hidden, down_weight))
    block_output = output.astype(bf16)
    grad_rows = cotangent.astype(f32) * pad_rows[:, None]
    full_grad = gather_rows(grad_rows.astype(bf16))
    down_grad = jnp.einsum("tf,td->fd", hidden, full_grad, preferred_element_type=f32)
    grad_hidden = jnp.einsum("td,fd->tf", full_grad, down_weight, preferred_element_type=f32)
    grad_gate = (grad_hidden * up_value * gate_sig * (1.0 + gate_value * (1.0 - gate_sig))).astype(bf16)
    grad_up = (grad_hidden * swish).astype(bf16)
    gate_up_grad = jnp.stack(
        [
            jnp.einsum("td,tf->df", full_second, grad_gate, preferred_element_type=f32),
            jnp.einsum("td,tf->df", full_second, grad_up, preferred_element_type=f32),
        ]
    )
    grad_xn_second = scatter_rows(
        jnp.einsum("tf,df->td", grad_gate, gate_up_weight[0], preferred_element_type=f32)
        + jnp.einsum("tf,df->td", grad_up, gate_up_weight[1], preferred_element_type=f32)
    )
    grad_part, second_gain_grad = rms_backward(hidden_one, second_scale, second_float, grad_xn_second)
    grad_h1 = grad_rows + grad_part
    full_mid = gather_rows(grad_h1.astype(bf16))
    out_grad = jnp.einsum("tc,td->cd", mixer_low, full_mid, preferred_element_type=f32)
    grad_normed = jnp.einsum("td,cd->tc", full_mid, out_weight, preferred_element_type=f32)
    *grad_pres, grad_logit, conv_grad, out_gain_grad = mixer_backward(
        *pres, beta_logit, table, doc_ids, conv_float, gain_float, saved, grad_normed
    )
    grad_logit = grad_logit.astype(bf16)
    qkv_grad = jnp.stack(
        [jnp.einsum("td,tc->dc", full_first, g, preferred_element_type=f32).astype(bf16) for g in grad_pres]
    )
    beta_grad = jnp.einsum("td,tc->dc", full_first, grad_logit, preferred_element_type=f32)
    grad_xn = jnp.einsum("tc,dc->td", grad_logit, beta_weight, preferred_element_type=f32)
    for i in range(3):
        grad_xn = grad_xn + jnp.einsum(
            "tc,dc->td", grad_pres[i], qkv_weight[i], preferred_element_type=f32
        )
    grad_x_part, first_gain_grad = rms_backward(
        rows_float, first_scale, first_float, scatter_rows(grad_xn)
    )
    input_grad = grad_h1 + grad_x_part
    first_gain_grad, second_gain_grad, out_gain_grad = lax.psum(
        (first_gain_grad, second_gain_grad, out_gain_grad.reshape(-1)), ("dp", "heads")
    )
    qkv_grad, beta_grad, conv_grad, out_grad, gate_up_grad, down_grad = (
        lax.psum(g.astype(bf16), "dp").astype(f32)
        for g in (qkv_grad, beta_grad, conv_grad.reshape(3, CONV, width), out_grad, gate_up_grad, down_grad)
    )
    return (
        block_output,
        input_grad,
        first_gain_grad,
        qkv_grad,
        beta_grad,
        conv_grad,
        out_gain_grad,
        out_grad,
        second_gain_grad,
        gate_up_grad,
        down_grad,
    )


def solution(mesh):
    return jax.shard_map(
        shards,
        mesh=mesh,
        in_specs=(
            P(("dp", "heads"), None),
            P("dp"),
            P("dp"),
            P(),
            P(None, None, "heads"),
            P(None, "heads"),
            P(None, None, "heads"),
            P(),
            P("heads", None),
            P(),
            P(None, None, "heads"),
            P("heads", None),
            P(("dp", "heads"), None),
        ),
        out_specs=(
            P(("dp", "heads"), None),
            P(("dp", "heads"), None),
            P(),
            P(None, None, "heads"),
            P(None, "heads"),
            P(None, None, "heads"),
            P(),
            P("heads", None),
            P(),
            P(None, None, "heads"),
            P("heads", None),
        ),
        check_vma=False,
    )
```

```python
import functools
import jax
import jax.numpy as jnp
from jax import lax
from jax.experimental import pallas as pl
from jax.experimental.pallas import tpu as pltpu
from jax.sharding import PartitionSpec as P

HEAD_DIM = 128
CONV = 4
HALO = 8
f32 = jnp.float32
bf16 = jnp.bfloat16


def mm(a, b):
    return jnp.dot(a.astype(bf16), b.astype(bf16), preferred_element_type=f32)


def mm_nt(a, b):
    return lax.dot_general(
        a.astype(bf16), b.astype(bf16), (((1,), (1,)), ((), ())), preferred_element_type=f32
    )


def mm_tn(a, b):
    return lax.dot_general(
        a.astype(bf16), b.astype(bf16), (((0,), (0,)), ((), ())), preferred_element_type=f32
    )


def token_table(doc_ids, pad_float, tile):
    length = doc_ids.shape[0]
    minus = jnp.full((tile,), -1, jnp.int32)
    padded = jnp.concatenate([minus, doc_ids, minus])

    def same(shift):
        moved = lax.slice_in_dim(padded, tile - shift, tile - shift + length, axis=0)
        return (moved == doc_ids).astype(f32)

    tiles = doc_ids.reshape(length // tile, tile)
    ends = tiles[:, -1]
    before = jnp.concatenate([jnp.full((1,), -1, jnp.int32), ends[:-1]])
    from_start = (tiles == before[:, None]).astype(f32).reshape(length)
    to_end = (tiles == ends[:, None]).astype(f32).reshape(length)
    columns = [same(1), same(2), same(3), pad_float, from_start, to_end, same(-1), same(-2), same(-3)]
    columns += [jnp.zeros((length,), f32)] * (16 - len(columns))
    return jnp.stack(columns, axis=1)


def sigmoid(x):
    return 1.0 / (1.0 + jnp.exp(-x))


def split_dot(a_hi, a_lo, b_hi, b_lo):
    return (
        jnp.dot(a_hi, b_hi, preferred_element_type=f32)
        + jnp.dot(a_lo, b_hi, preferred_element_type=f32)
        + jnp.dot(a_hi, b_lo, preferred_element_type=f32)
    )


def halves(a):
    hi = a.astype(bf16)
    return hi, (a - hi.astype(f32)).astype(bf16)


def unit_inverse(strict, row, col):
    size = strict.shape[0]
    apart = row ^ col
    eye = (row == col).astype(f32)
    zero = jnp.zeros_like(strict)
    inverse = eye - jnp.where(apart == 1, strict, zero)
    step = 2
    while step < size:
        part = jnp.where((apart >= step) & (apart < 2 * step), strict, zero)
        low = inverse.astype(bf16)
        inverse = inverse - mm(low, mm(part, low))
        step *= 2
    a_hi, a_lo = halves(strict)
    x_hi, x_lo = halves(inverse)
    rest = eye - inverse - split_dot(a_hi, a_lo, x_hi, x_lo)
    return inverse + mm(x_hi, rest)


def conv_sum(ext_ref, part, rows, lanes, taps, same):
    total = ext_ref[part, pl.ds(HALO, rows), lanes] * taps[0]
    for shift in range(1, CONV):
        total = total + ext_ref[part, pl.ds(HALO - shift, rows), lanes] * taps[shift] * same[shift - 1]
    return total


def rotated(tile, me, ring):
    return lax.rem(tile - me + ring, ring)


def chunk_kernel(
    heads, old, where_ref, q_ref, k_ref, v_ref, q_halo_ref, k_halo_ref, v_halo_ref,
    beta_ref, table_ref, doc_col_ref, doc_row_ref, conv_ref, *rest,
):
    outs = rest[old:]
    (q_pre_ref, k_pre_ref, v_pre_ref, beta_out_ref,
     query_ref, key_ref, value_ref, score_ref, inv_ref, ext_ref) = outs
    group = pl.program_id(0)
    rows = q_ref.shape[0]
    for part, (ref, halo, copy) in enumerate(
        ((q_ref, q_halo_ref, q_pre_ref), (k_ref, k_halo_ref, k_pre_ref), (v_ref, v_halo_ref, v_pre_ref))
    ):
        ext_ref[part, pl.ds(0, HALO), :] = halo[...]
        ext_ref[part, pl.ds(HALO, rows), :] = ref[...]
        copy[...] = ref[...]
    beta_out_ref[...] = beta_ref[...]
    wide = (rows, HEAD_DIM)
    same = [jnp.broadcast_to(table_ref[:, j : j + 1], wide) for j in range(3)]
    pad = table_ref[:, 3:4]
    row = lax.broadcasted_iota(jnp.int32, (rows, rows), 0)
    col = lax.broadcasted_iota(jnp.int32, (rows, rows), 1)
    together = doc_col_ref[...] == doc_row_ref[...]
    below = together & (row > col)
    upto = together & (row >= col)
    betas = sigmoid(beta_ref[...]) * pad
    lane = lax.broadcasted_iota(jnp.int32, betas.shape, 1)
    for head in range(heads):
        lanes = pl.ds(head * HEAD_DIM, HEAD_DIM)
        acts = []
        for part in range(3):
            taps = [conv_ref[part * CONV + j : part * CONV + j + 1, lanes] for j in range(CONV)]
            total = conv_sum(ext_ref, part, rows, lanes, taps, same)
            acts.append(total * sigmoid(total))
        query = acts[0] * lax.rsqrt(jnp.sum(acts[0] * acts[0], axis=1, keepdims=True) + 1e-06)
        key = acts[1] * (lax.rsqrt(jnp.sum(acts[1] * acts[1], axis=1, keepdims=True) + 1e-06) * pad)
        beta = jnp.sum(jnp.where(lane == group * heads + head, betas, 0.0), axis=1, keepdims=True)
        key = key.astype(bf16)
        query = query.astype(bf16)
        query_ref[:, lanes] = query
        key_ref[:, lanes] = key
        value_ref[:, lanes] = acts[2].astype(bf16)
        strict = jnp.where(below, mm_nt(key, key) * beta, 0.0)
        inv_ref[head] = unit_inverse(strict, row, col).astype(bf16)
        score_ref[head] = jnp.where(upto, mm_nt(query, key), 0.0).astype(bf16)


def mixer_chunk(slot, ring, chunk, pres, halos, halo_row, beta_logit, table, doc_ids, conv, old):
    rows, width = pres[0].shape
    heads = width // HEAD_DIM
    length = doc_ids.shape[0]
    per = 2 if heads % 2 == 0 else 1
    lane = per * HEAD_DIM
    wide = pl.BlockSpec((rows, lane), lambda g, c: (0, g))
    halo = pl.BlockSpec((HALO, lane), lambda g, c: (halo_row, g))
    out_wide = pl.BlockSpec((rows, lane), lambda g, c: (slot, g))
    out_square = pl.BlockSpec((per, rows, rows), lambda g, c: (g, slot, 0))
    whole = jax.ShapeDtypeStruct((length, width), f32)
    low = jax.ShapeDtypeStruct((length, width), bf16)
    square = jax.ShapeDtypeStruct((heads, length, rows), bf16)
    flops = 2 * heads * rows * rows * (rows * 18 + HEAD_DIM * 2)
    return pl.pallas_call(
        functools.partial(chunk_kernel, per, len(old)),
        grid_spec=pltpu.PrefetchScalarGridSpec(
            num_scalar_prefetch=1,
            grid=(heads // per,),
            in_specs=[
                wide, wide, wide, halo, halo, halo,
                pl.BlockSpec((rows, heads), lambda g, c: (0, 0)),
                pl.BlockSpec((rows, 16), lambda g, c: (c[0], 0)),
                pl.BlockSpec((rows, 1), lambda g, c: (c[0], 0)),
                pl.BlockSpec((1, rows), lambda g, c: (0, c[0])),
                pl.BlockSpec((3 * CONV, lane), lambda g, c: (0, g)),
            ] + [pl.BlockSpec(memory_space=pl.ANY)] * len(old),
            out_specs=[
                out_wide, out_wide, out_wide,
                pl.BlockSpec((rows, heads), lambda g, c: (slot, 0)),
                out_wide, out_wide, out_wide, out_square, out_square,
            ],
            scratch_shapes=[pltpu.VMEM((3, rows + HALO, lane), f32)],
        ),
        out_shape=[
            whole, whole, whole, jax.ShapeDtypeStruct((length, heads), f32),
            low, low, low, square, square,
        ],
        input_output_aliases={12 + i: i for i in range(len(old))},
        compiler_params=pltpu.CompilerParams(vmem_limit_bytes=40 * 1024 * 1024),
        cost_estimate=pl.CostEstimate(
            flops=flops, bytes_accessed=rows * width * 50, transcendentals=rows * width * 4
        ),
        name="mixer_chunk",
    )(
        chunk, *pres, *halos, beta_logit, table,
        doc_ids.reshape(length, 1), doc_ids.reshape(1, length), conv, *old,
    )


def scan_kernel(
    heads, me_ref, query_ref, key_ref, value_ref, score_ref, inv_ref, beta_ref, table_ref, gain_ref,
    normed_ref, out_ref, fresh_ref, start_ref, state_ref,
):
    tile = pl.program_id(0)
    factor = HEAD_DIM ** (-0.5)
    rows = query_ref.shape[0]

    @pl.when(tile == 0)
    def _():
        state_ref[...] = jnp.zeros_like(state_ref)

    wide = (rows, HEAD_DIM)
    pad = table_ref[:, 3:4]
    from_start = jnp.broadcast_to(table_ref[:, 4:5], wide)
    to_end = jnp.broadcast_to(table_ref[:, 5:6], wide)
    carry = table_ref[rows - 1 : rows, 4:5]
    gain = gain_ref[...]
    for head in range(heads):
        lanes = pl.ds(head * HEAD_DIM, HEAD_DIM)
        beta = sigmoid(beta_ref[:, head : head + 1]) * pad
        query = query_ref[:, lanes]
        key = key_ref[:, lanes]
        state = state_ref[head]
        low_state = state.astype(bf16)
        start_ref[0, head] = low_state
        right = beta * (value_ref[:, lanes].astype(f32) - from_start * mm(key, low_state))
        fresh = mm(inv_ref[head], right).astype(bf16)
        fresh_ref[:, lanes] = fresh
        state_ref[head] = carry * state + mm_tn(key.astype(f32) * to_end, fresh)
        out = factor * (from_start * mm(query, low_state) + mm(score_ref[head], fresh))
        out_ref[:, lanes] = out
        scale = lax.rsqrt(jnp.mean(out * out, axis=1, keepdims=True) + 1e-05)
        normed_ref[:, lanes] = (out * scale * gain).astype(bf16)


def mixer_scan(me, ring, query, key, value, score, inverse, beta_logit, table, gain):
    length, width = query.shape
    heads = width // HEAD_DIM
    rows = length // ring
    wide = pl.BlockSpec((rows, width), lambda i, m: (rotated(i, m[0], ring), 0))
    square = pl.BlockSpec((heads, rows, rows), lambda i, m: (0, rotated(i, m[0], ring), 0))
    flops = 2 * ring * heads * rows * HEAD_DIM * (rows * 2 + HEAD_DIM * 3)
    return pl.pallas_call(
        functools.partial(scan_kernel, heads),
        grid_spec=pltpu.PrefetchScalarGridSpec(
            num_scalar_prefetch=1,
            grid=(ring,),
            in_specs=[
                wide, wide, wide, square, square,
                pl.BlockSpec((rows, heads), lambda i, m: (rotated(i, m[0], ring), 0)),
                pl.BlockSpec((rows, 16), lambda i, m: (i, 0)),
                pl.BlockSpec((1, HEAD_DIM), lambda i, m: (0, 0)),
            ],
            out_specs=[
                wide, wide, wide,
                pl.BlockSpec((1, heads, HEAD_DIM, HEAD_DIM), lambda i, m: (i, 0, 0, 0)),
            ],
            scratch_shapes=[pltpu.VMEM((heads, HEAD_DIM, HEAD_DIM), f32)],
        ),
        out_shape=[
            jax.ShapeDtypeStruct((length, width), bf16),
            jax.ShapeDtypeStruct((length, width), f32),
            jax.ShapeDtypeStruct((length, width), bf16),
            jax.ShapeDtypeStruct((ring, heads, HEAD_DIM, HEAD_DIM), bf16),
        ],
        compiler_params=pltpu.CompilerParams(vmem_limit_bytes=40 * 1024 * 1024),
        cost_estimate=pl.CostEstimate(
            flops=flops, bytes_accessed=length * width * 18, transcendentals=length * heads
        ),
        name="mixer_scan",
    )(me, query, key, value, score, inverse, beta_logit, table, gain.reshape(1, HEAD_DIM))


def backward_kernel(
    heads, me_ref, q_ref, k_ref, v_ref, q_halo_ref, k_halo_ref, v_halo_ref,
    beta_ref, table_ref, doc_col_ref, doc_row_ref, conv_ref, gain_ref,
    out_ref, fresh_ref, score_ref, inv_ref, start_ref, cot_ref,
    dq_ref, dk_ref, dv_ref, dbeta_ref, dconv_ref, dgain_ref, ext_ref, back_ref, state_ref,
):
    step = pl.program_id(0)
    factor = HEAD_DIM ** (-0.5)
    rows, width = q_ref.shape

    @pl.when(step == 0)
    def _():
        state_ref[...] = jnp.zeros_like(state_ref)
        back_ref[:, pl.ds(rows, HALO), :] = jnp.zeros((3, HALO, width), f32)
        dconv_ref[...] = jnp.zeros_like(dconv_ref)
        dgain_ref[...] = jnp.zeros_like(dgain_ref)

    @pl.when(step > 0)
    def _():
        back_ref[:, pl.ds(rows, HALO), :] = back_ref[:, pl.ds(0, HALO), :]

    for part, (ref, halo) in enumerate(
        ((q_ref, q_halo_ref), (k_ref, k_halo_ref), (v_ref, v_halo_ref))
    ):
        ext_ref[part, pl.ds(0, HALO), :] = halo[...].astype(f32)
        ext_ref[part, pl.ds(HALO, rows), :] = ref[...].astype(f32)
    wide = (rows, HEAD_DIM)
    same = [jnp.broadcast_to(table_ref[:, j : j + 1], wide) for j in range(3)]
    after = [jnp.broadcast_to(table_ref[:, 6 + j : 7 + j], wide) for j in range(3)]
    pad = table_ref[:, 3:4]
    from_start = jnp.broadcast_to(table_ref[:, 4:5], wide)
    to_end = jnp.broadcast_to(table_ref[:, 5:6], wide)
    carry = table_ref[rows - 1 : rows, 4:5]
    row = lax.broadcasted_iota(jnp.int32, (rows, rows), 0)
    col = lax.broadcasted_iota(jnp.int32, (rows, rows), 1)
    together = doc_col_ref[...] == doc_row_ref[...]
    below = together & (row > col)
    upto = together & (row >= col)
    gain = gain_ref[...]
    dgain = jnp.zeros((1, HEAD_DIM), f32)
    for head in range(heads):
        lanes = pl.ds(head * HEAD_DIM, HEAD_DIM)
        sums, sigs, acts = [], [], []
        for part in range(3):
            taps = [conv_ref[part * CONV + j : part * CONV + j + 1, lanes] for j in range(CONV)]
            total = conv_sum(ext_ref, part, rows, lanes, taps, same)
            sig = sigmoid(total)
            sums.append(total)
            sigs.append(sig)
            acts.append(total * sig)
        q_scale = lax.rsqrt(jnp.sum(acts[0] * acts[0], axis=1, keepdims=True) + 1e-06)
        k_scale = lax.rsqrt(jnp.sum(acts[1] * acts[1], axis=1, keepdims=True) + 1e-06)
        query_full = acts[0] * q_scale
        key_unit = acts[1] * k_scale
        beta_sig = sigmoid(beta_ref[:, head : head + 1])
        beta = beta_sig * pad
        key_full = key_unit * pad
        key = key_full.astype(bf16)
        query = query_full.astype(bf16)
        value = acts[2]
        out = out_ref[:, lanes]
        cot = cot_ref[:, lanes].astype(f32)
        scale = lax.rsqrt(jnp.mean(out * out, axis=1, keepdims=True) + 1e-05)
        unit = out * scale
        dgain = dgain + jnp.sum(cot * unit, axis=0, keepdims=True)
        gained = cot * gain
        dout = (factor * scale) * (gained - unit * jnp.mean(unit * gained, axis=1, keepdims=True))
        dout_low = dout.astype(bf16)
        dout_first = (dout * from_start).astype(bf16)
        fresh = fresh_ref[:, lanes]
        start = start_ref[0, head]
        dstate = state_ref[head]
        dstate_low = dstate.astype(bf16)
        inverse = inv_ref[head]
        key_end = (key_full * to_end).astype(bf16)
        scores = score_ref[head]
        dfresh = mm_tn(scores, dout_low) + mm(key_end, dstate_low)
        dright = mm_tn(inverse, dfresh)
        dright_low = dright.astype(bf16)
        dscores = jnp.where(upto, mm_nt(dout_low, fresh), 0.0).astype(bf16)
        dquery = mm_nt(dout_first, start) + mm(dscores, key)
        dstrict = jnp.where(below, -mm_nt(dright_low, fresh), 0.0)
        scaled = (dstrict * beta).astype(bf16)
        weighted = (dright * (beta * from_start)).astype(bf16)
        inner_key = mm(dstrict, key)
        start_key = from_start * mm_nt(dright_low, start)
        dkey = (
            mm_tn(dscores, query)
            + to_end * mm_nt(fresh, dstate_low)
            + beta * (inner_key - start_key)
            + mm_tn(scaled, key)
        )
        dbeta = jnp.sum(
            dright * value + (inner_key - start_key) * key_full, axis=1, keepdims=True
        )
        dvalue = beta * dright
        state_ref[head] = (
            carry * dstate + mm_tn(query, dout_first) - mm_tn(key, weighted)
        )
        dbeta_ref[:, head : head + 1] = dbeta * pad * beta_sig * (1.0 - beta_sig)
        dkey = dkey * pad
        dacts = (
            q_scale * (dquery - query_full * jnp.sum(query_full * dquery, axis=1, keepdims=True)),
            k_scale * (dkey - key_unit * jnp.sum(key_unit * dkey, axis=1, keepdims=True)),
            dvalue,
        )
        for part, target in enumerate((dq_ref, dk_ref, dv_ref)):
            sig = sigs[part]
            dsum = dacts[part] * (sig * (1.0 + sums[part] * (1.0 - sig)))
            back_ref[part, pl.ds(0, rows), lanes] = dsum
            taps = [conv_ref[part * CONV + j : part * CONV + j + 1, lanes] for j in range(CONV)]
            dpre = dsum * taps[0]
            dtaps = [jnp.sum(dsum * ext_ref[part, pl.ds(HALO, rows), lanes], axis=0, keepdims=True)]
            for shift in range(1, CONV):
                dpre = dpre + back_ref[part, pl.ds(shift, rows), lanes] * (after[shift - 1] * taps[shift])
                moved = ext_ref[part, pl.ds(HALO - shift, rows), lanes]
                dtaps.append(jnp.sum(dsum * moved * same[shift - 1], axis=0, keepdims=True))
            target[:, lanes] = dpre.astype(bf16)
            for j in range(CONV):
                spot = slice(part * CONV + j, part * CONV + j + 1)
                dconv_ref[spot, lanes] = dconv_ref[spot, lanes] + dtaps[j]
    dgain_ref[...] = dgain_ref[...] + dgain


def mixer_backward(me, ring, pres, beta_logit, table, doc_ids, conv, gain, saved, cot):
    length, width = pres[0].shape
    heads = width // HEAD_DIM
    rows = length // ring
    last = ring - 1

    def spot(i, m):
        return rotated(last - i, m[0], ring)

    def before(i, m):
        return rotated(jnp.maximum(last - i - 1, 0), m[0], ring)

    per = rows // HALO
    wide = pl.BlockSpec((rows, width), lambda i, m: (spot(i, m), 0))
    halo = pl.BlockSpec((HALO, width), lambda i, m: (before(i, m) * per + per - 1, 0))
    square = pl.BlockSpec((heads, rows, rows), lambda i, m: (0, spot(i, m), 0))
    narrow = pl.BlockSpec((rows, heads), lambda i, m: (spot(i, m), 0))
    flops = 2 * ring * heads * rows * HEAD_DIM * (rows * 9 + HEAD_DIM * 6)
    low = jax.ShapeDtypeStruct((length, width), bf16)
    return pl.pallas_call(
        functools.partial(backward_kernel, heads),
        grid_spec=pltpu.PrefetchScalarGridSpec(
            num_scalar_prefetch=1,
            grid=(ring,),
            in_specs=[
                wide, wide, wide, halo, halo, halo, narrow,
                pl.BlockSpec((rows, 16), lambda i, m: (last - i, 0)),
                pl.BlockSpec((rows, 1), lambda i, m: (last - i, 0)),
                pl.BlockSpec((1, rows), lambda i, m: (0, last - i)),
                pl.BlockSpec((3 * CONV, width), lambda i, m: (0, 0)),
                pl.BlockSpec((1, HEAD_DIM), lambda i, m: (0, 0)),
                wide, wide, square, square,
                pl.BlockSpec((1, heads, HEAD_DIM, HEAD_DIM), lambda i, m: (last - i, 0, 0, 0)),
                wide,
            ],
            out_specs=[
                wide, wide, wide, narrow,
                pl.BlockSpec((3 * CONV, width), lambda i, m: (0, 0)),
                pl.BlockSpec((1, HEAD_DIM), lambda i, m: (0, 0)),
            ],
            scratch_shapes=[
                pltpu.VMEM((3, rows + HALO, width), f32),
                pltpu.VMEM((3, rows + HALO, width), f32),
                pltpu.VMEM((heads, HEAD_DIM, HEAD_DIM), f32),
            ],
        ),
        out_shape=[
            low, low, low,
            jax.ShapeDtypeStruct((length, heads), f32),
            jax.ShapeDtypeStruct((3 * CONV, width), f32),
            jax.ShapeDtypeStruct((1, HEAD_DIM), f32),
        ],
        compiler_params=pltpu.CompilerParams(vmem_limit_bytes=40 * 1024 * 1024),
        cost_estimate=pl.CostEstimate(
            flops=flops, bytes_accessed=length * width * 34, transcendentals=length * width * 3
        ),
        name="mixer_backward",
    )(
        me, *pres, *pres, beta_logit, table,
        doc_ids.reshape(length, 1), doc_ids.reshape(1, length), conv, gain.reshape(1, HEAD_DIM),
        *saved, cot,
    )


def dot_f32(a, b):
    return jnp.dot(a, b, preferred_element_type=f32)


def dot_nt(a, b):
    return lax.dot_general(a, b, (((1,), (1,)), ((), ())), preferred_element_type=f32)


def dot_tn(a, b):
    return lax.dot_general(a, b, (((0,), (0,)), ((), ())), preferred_element_type=f32)


def rms_forward(rows, gain):
    scale = lax.rsqrt(jnp.mean(rows * rows, axis=-1, keepdims=True) + 1e-06)
    return (rows * scale * gain).astype(bf16), scale


def rms_backward(rows, scale, gain, grad):
    scaled = grad * gain
    mean = jnp.mean(scaled * rows, axis=-1, keepdims=True)
    gain_grad = jnp.sum(grad * rows * scale, axis=0)
    return scale * scaled - (scale * scale * scale) * rows * mean, gain_grad


def after(value, *others):
    return lax.optimization_barrier((value, *others))[0]


def bits_of(count):
    return [b for b in range(count.bit_length() - 1)]


class Ring:
    def __init__(self, size):
        self.size = size
        self.me = lax.axis_index("heads")

    def back(self, value):
        return lax.ppermute(value, "heads", [(i, (i - 1) % self.size) for i in range(self.size)])

    def shift(self, value, by):
        return lax.ppermute(value, "heads", [(i, (i + by) % self.size) for i in range(self.size)])

    def gather(self, rows):
        slots = [rows]
        for _ in range(self.size - 1):
            slots.append(self.back(slots[-1]))
        return slots

    def scatter(self, partial):
        total = partial(1 % self.size)
        for k in range(2, self.size + 1):
            moved = self.back(total.astype(bf16))
            total = moved.astype(f32) + partial(k % self.size)
        return total


class Groups:
    def __init__(self, size):
        self.size = size
        self.bits = bits_of(size)
        self.me = lax.axis_index("dp")

    def swap(self, value, bit):
        return lax.ppermute(value, "dp", [(i, i ^ (1 << bit)) for i in range(self.size)])

    def mine(self, bit):
        return (self.me >> bit) & 1

    def order(self, color):
        first, rest = self.bits[:1], self.bits[1:]
        return first + (rest if color == 0 else rest[::-1])

    def reduce(self, array, color):
        rows, cols = array.shape
        view = array.reshape((2,) * len(self.bits) + (rows // self.size, cols))
        left = self.bits[::-1]
        for bit in self.order(color):
            axis = left.index(bit)
            keep = lax.dynamic_index_in_dim(view, self.mine(bit), axis, keepdims=False)
            send = lax.dynamic_index_in_dim(view, 1 - self.mine(bit), axis, keepdims=False)
            got = self.swap(send.astype(bf16), bit)
            view = (keep.astype(f32) + got.astype(f32)).astype(bf16)
            left = [b for b in left if b != bit]
        return view

    def gather(self, piece, color):
        view = piece
        have = []
        for bit in self.order(color)[::-1]:
            got = self.swap(view, bit)
            have = sorted(have + [bit], reverse=True)
            axis = have.index(bit)
            shape = view.shape[:axis] + (2,) + view.shape[axis:]
            place = lax.broadcasted_iota(jnp.int32, shape, axis)
            view = jnp.where(
                place == self.mine(bit), jnp.expand_dims(view, axis), jnp.expand_dims(got, axis)
            )
        rows, cols = view.shape[-2:]
        return view.reshape(rows * self.size, cols).astype(f32)

    def total(self, array, color):
        return self.gather(self.reduce(array, color), color)

    def small(self, vector):
        for bit in self.bits:
            vector = vector + self.swap(vector, bit)
        return vector


def shards(
    heads_size,
    dp_size,
    block_input,
    doc_ids,
    pad_mask,
    first_gain,
    qkv_weight,
    beta_weight,
    conv_weight,
    out_gain,
    out_weight,
    second_gain,
    gate_up_weight,
    down_weight,
    cotangent,
):
    ring = Ring(heads_size)
    groups = Groups(dp_size)
    size = heads_size
    local_rows, model_width = block_input.shape
    width = qkv_weight.shape[2]
    me = ring.me.astype(jnp.int32)
    me_one = me.reshape(1)
    pad_float = pad_mask.astype(f32)
    pad_rows = lax.dynamic_slice_in_dim(pad_float, me * local_rows, local_rows, 0)
    rows_float = block_input.astype(f32)
    first_float = first_gain.astype(f32)
    second_float = second_gain.astype(f32)
    conv_float = conv_weight.astype(f32).reshape(3 * CONV, width)
    gain_float = out_gain.astype(f32)

    xn_first, first_scale = rms_forward(rows_float, first_float)
    halo_rows = ring.shift(xn_first[local_rows - HALO :], 1)
    first_slots = ring.gather(xn_first)
    share = out_weight.shape[0] // dp_size
    own_share = lax.dynamic_slice_in_dim(out_weight, groups.me * share, share, 0)
    out_full = lax.all_gather(own_share, ("heads", "dp"), axis=0, tiled=True)
    out_full = out_full.reshape(size, out_weight.shape[0], model_width)
    table = token_table(doc_ids, pad_float, local_rows)
    halos = [dot_f32(halo_rows, qkv_weight[i]) for i in range(3)]
    halo_row = 0
    old = []
    for k in range(size):
        pres = [dot_f32(first_slots[k], qkv_weight[i]) for i in range(3)]
        beta_logit = dot_f32(first_slots[k], beta_weight)
        chunk = lax.rem(me + k, size).reshape(1)
        old = mixer_chunk(
            k, size, chunk, pres, halos, halo_row, beta_logit, table, doc_ids, conv_float, old
        )
        halos, halo_row = pres, local_rows // HALO - 1
    *pre_all, beta_all, query, key, value, score, inverse = old

    grad_rows = cotangent.astype(f32) * pad_rows[:, None]
    grad_slots = ring.gather(after(grad_rows.astype(bf16), first_slots[-1]))

    normed, out_all, fresh, starts = mixer_scan(
        me_one, size, query, key, value, score, inverse, beta_all, table, gain_float
    )
    saved = (out_all, fresh, score, inverse, starts)
    mixed = 0.0
    for k in range(size):
        block = normed[k * local_rows : (k + 1) * local_rows]
        moved = block if k == 0 else ring.shift(block, k)
        source = lax.rem(me - k + size, size)
        mixed = mixed + dot_f32(moved, lax.dynamic_index_in_dim(out_full, source, 0, keepdims=False))
    hidden_one = rows_float + mixed
    xn_second, second_scale = rms_forward(hidden_one, second_float)

    second_slots = ring.gather(xn_second)
    hiddens, gates, ups, backs, downs = [], [], [], [], []
    for k in range(size):
        gate = dot_f32(second_slots[k], gate_up_weight[0])
        up = dot_f32(second_slots[k], gate_up_weight[1])
        grad_hidden = dot_nt(grad_slots[k], down_weight)
        sig = sigmoid(gate)
        swish = gate * sig
        hiddens.append((swish * up).astype(bf16))
        gates.append((grad_hidden * up * sig * (1.0 + gate * (1.0 - sig))).astype(bf16))
        ups.append((grad_hidden * swish).astype(bf16))
        backs.append(dot_nt(gates[k], gate_up_weight[0]) + dot_nt(ups[k], gate_up_weight[1]))
        downs.append(dot_f32(hiddens[k], down_weight))
    grad_xn_second = ring.scatter(lambda k: backs[k])
    full_second = jnp.concatenate(second_slots)
    full_grad = jnp.concatenate(grad_slots)
    full_hidden = jnp.concatenate(hiddens)
    down_part = dot_tn(full_hidden, full_grad).astype(bf16)
    gate_part = dot_tn(full_second, jnp.concatenate(gates)).astype(bf16)
    up_part = dot_tn(full_second, jnp.concatenate(ups)).astype(bf16)
    half = model_width // 2
    gate_grad = groups.total(gate_part, 0)
    up_grad = groups.total(up_part, 1)
    down_grad = jnp.concatenate(
        [groups.total(down_part[:, :half], 0), groups.total(down_part[:, half:], 1)], axis=1
    )
    gate_up_grad = jnp.stack([gate_grad, up_grad])

    grad_part, second_gain_grad = rms_backward(hidden_one, second_scale, second_float, grad_xn_second)
    grad_h1 = grad_rows + grad_part
    mid_slots = ring.gather(grad_h1.astype(bf16))
    grad_normed = jnp.concatenate([dot_nt(rows, out_weight).astype(bf16) for rows in mid_slots])
    output = hidden_one + ring.scatter(lambda k: after(downs[k], mid_slots[-1]) if k == 1 else downs[k])
    block_output = output.astype(bf16)
    out_part = dot_tn(normed, jnp.concatenate(mid_slots)).astype(bf16)
    out_grad = jnp.concatenate(
        [groups.total(out_part[:, :half], 0), groups.total(out_part[:, half:], 1)], axis=1
    )

    *grad_pres, grad_logit, conv_part, out_gain_part = mixer_backward(
        me_one, size, pre_all, beta_all, table, doc_ids, conv_float, gain_float, saved, grad_normed
    )
    grad_logit = grad_logit.astype(bf16)
    full_first = jnp.concatenate(first_slots)
    parts = [dot_tn(full_first, grad_pres[i]) for i in range(3)]
    beta_part = dot_tn(full_first, grad_logit)
    lows = [part.astype(bf16) for part in parts]
    cut = width // 2
    qkv_grad = jnp.stack(
        [
            groups.total(lows[0], 0),
            groups.total(lows[1], 1),
            jnp.concatenate(
                [groups.total(lows[2][:, :cut], 0), groups.total(lows[2][:, cut:], 1)], axis=1
            ),
        ]
    )

    def first_partial(k):
        rows = slice(k * local_rows, (k + 1) * local_rows)
        total = dot_nt(grad_logit[rows], beta_weight)
        for i in range(3):
            total = total + dot_nt(grad_pres[i][rows], qkv_weight[i])
        return total

    grad_xn_first = ring.scatter(first_partial)
    grad_x_part, first_gain_part = rms_backward(rows_float, first_scale, first_float, grad_xn_first)
    input_grad = grad_h1 + grad_x_part

    small = groups.small(jnp.concatenate([beta_part.reshape(-1), conv_part.reshape(-1)]))
    count = beta_part.size
    beta_grad = small[:count].reshape(beta_part.shape)
    conv_grad = small[count:].reshape(3, CONV, width)
    gains = jnp.concatenate([first_gain_part, second_gain_grad, out_gain_part.reshape(-1)])
    gains = groups.small(gains)
    for bit in bits_of(size):
        gains = gains + lax.ppermute(gains, "heads", [(i, i ^ (1 << bit)) for i in range(size)])
    return (
        block_output,
        input_grad,
        gains[:model_width],
        qkv_grad,
        beta_grad,
        conv_grad,
        gains[2 * model_width :],
        out_grad,
        gains[model_width : 2 * model_width],
        gate_up_grad,
        down_grad,
    )


def solution(mesh):
    rows = P(("dp", "heads"), None)
    last = P(None, None, "heads")
    return jax.shard_map(
        functools.partial(shards, mesh.shape["heads"], mesh.shape["dp"]),
        mesh=mesh,
        in_specs=(
            rows, P("dp"), P("dp"), P(), last, P(None, "heads"), last, P(), P("heads", None), P(),
            last, P("heads", None), rows,
        ),
        out_specs=(
            rows, rows, P(), last, P(None, "heads"), last, P(), P("heads", None), P(), last,
            P("heads", None),
        ),
        check_vma=False,
    )
```

```python
import functools
import jax
import jax.numpy as jnp
from jax import lax
from jax.experimental import pallas as pl
from jax.experimental.pallas import tpu as pltpu
from jax.sharding import PartitionSpec as P

HEAD_DIM = 128
CONV = 4
HALO = 16
f32 = jnp.float32
bf16 = jnp.bfloat16


def mm(a, b):
    return jnp.dot(a.astype(bf16), b.astype(bf16), preferred_element_type=f32)


def mm_nt(a, b):
    return lax.dot_general(
        a.astype(bf16), b.astype(bf16), (((1,), (1,)), ((), ())), preferred_element_type=f32
    )


def mm_tn(a, b):
    return lax.dot_general(
        a.astype(bf16), b.astype(bf16), (((0,), (0,)), ((), ())), preferred_element_type=f32
    )


def token_table(doc_ids, pad_float, tile):
    length = doc_ids.shape[0]
    minus = jnp.full((tile,), -1, jnp.int32)
    padded = jnp.concatenate([minus, doc_ids, minus])

    def same(shift):
        moved = lax.slice_in_dim(padded, tile - shift, tile - shift + length, axis=0)
        return (moved == doc_ids).astype(f32)

    tiles = doc_ids.reshape(length // tile, tile)
    ends = tiles[:, -1]
    before = jnp.concatenate([jnp.full((1,), -1, jnp.int32), ends[:-1]])
    from_start = (tiles == before[:, None]).astype(f32).reshape(length)
    to_end = (tiles == ends[:, None]).astype(f32).reshape(length)
    columns = [same(1), same(2), same(3), pad_float, from_start, to_end, same(-1), same(-2), same(-3)]
    columns += [jnp.zeros((length,), f32)] * (16 - len(columns))
    return jnp.stack(columns, axis=1)


def sigmoid(x):
    return 1.0 / (1.0 + jnp.exp(-x))


def block_inverse(strict, apart):
    size = strict.shape[0]
    zero = jnp.zeros_like(strict)
    inverse = jnp.where(apart == 0, 1.0, jnp.where(apart == 1, -strict, zero))
    low = strict.astype(bf16)
    low_zero = jnp.zeros_like(low)
    step = 2
    while step < size:
        part = jnp.where((apart >= step) & (apart < 2 * step), low, low_zero)
        held = inverse.astype(bf16)
        inverse = inverse - mm(held, mm(part, held))
        step *= 2
    return inverse


def unit_inverse(strict):
    size = strict.shape[0]
    half = min(size, 128)
    row = lax.broadcasted_iota(jnp.int32, (half, half), 0)
    col = lax.broadcasted_iota(jnp.int32, (half, half), 1)
    apart = row ^ col
    if size == half:
        return block_inverse(strict, apart)
    top = strict[:half, :half]
    bottom = strict[half:, half:]
    top = block_inverse(top, apart)
    bottom = block_inverse(bottom, apart)
    cross = -mm(bottom, mm(strict[half:, :half], top))
    return jnp.concatenate(
        [jnp.concatenate([top, jnp.zeros_like(top)], axis=1), jnp.concatenate([cross, bottom], axis=1)],
        axis=0,
    )


def conv_sum(ext_ref, part, rows, lanes, taps, same):
    total = ext_ref[part, pl.ds(HALO, rows), lanes] * taps[0]
    for shift in range(1, CONV):
        total = total + ext_ref[part, pl.ds(HALO - shift, rows), lanes] * taps[shift] * same[shift - 1]
    return total


def rotated(tile, me, ring):
    return lax.rem(tile - me + ring, ring)


def chunk_kernel(
    heads, old, where_ref, x_ref, x_halo_ref, weight_ref, beta_weight_ref,
    table_ref, doc_col_ref, doc_row_ref, conv_ref, *rest,
):
    outs = rest[old:]
    (q_pre_ref, k_pre_ref, v_pre_ref, beta_out_ref,
     query_ref, key_ref, value_ref, score_ref, inv_ref, x_ext_ref, ext_ref) = outs
    group = pl.program_id(0)
    rows = x_ref.shape[0]

    @pl.when(group == 0)
    def _():
        x_ext_ref[pl.ds(0, HALO), :] = x_halo_ref[...]
        x_ext_ref[pl.ds(HALO, rows), :] = x_ref[...]
        beta_out_ref[...] = jnp.dot(x_ref[...], beta_weight_ref[...], preferred_element_type=f32)

    for part, copy in enumerate((q_pre_ref, k_pre_ref, v_pre_ref)):
        pre = jnp.dot(x_ext_ref[...], weight_ref[part], preferred_element_type=f32)
        ext_ref[part] = pre
        copy[...] = pre[HALO:]
    wide = (rows, HEAD_DIM)
    same = [jnp.broadcast_to(table_ref[:, j : j + 1], wide) for j in range(3)]
    pad = table_ref[:, 3:4]
    row = lax.broadcasted_iota(jnp.int32, (rows, rows), 0)
    col = lax.broadcasted_iota(jnp.int32, (rows, rows), 1)
    together = doc_col_ref[...] == doc_row_ref[...]
    below = together & (row > col)
    upto = together & (row >= col)
    betas = sigmoid(beta_out_ref[...]) * pad
    lane = lax.broadcasted_iota(jnp.int32, betas.shape, 1)
    for head in range(heads):
        lanes = pl.ds(head * HEAD_DIM, HEAD_DIM)
        acts = []
        for part in range(3):
            taps = [conv_ref[part * CONV + j : part * CONV + j + 1, lanes] for j in range(CONV)]
            total = conv_sum(ext_ref, part, rows, lanes, taps, same)
            acts.append(total * sigmoid(total))
        query = acts[0] * lax.rsqrt(jnp.sum(acts[0] * acts[0], axis=1, keepdims=True) + 1e-06)
        key = acts[1] * (lax.rsqrt(jnp.sum(acts[1] * acts[1], axis=1, keepdims=True) + 1e-06) * pad)
        beta = jnp.sum(jnp.where(lane == group * heads + head, betas, 0.0), axis=1, keepdims=True)
        key = key.astype(bf16)
        query = query.astype(bf16)
        query_ref[:, lanes] = query
        key_ref[:, lanes] = key
        value_ref[:, lanes] = acts[2].astype(bf16)
        strict = jnp.where(below, mm_nt(key, key) * beta, 0.0)
        inv_ref[head] = unit_inverse(strict).astype(bf16)
        score_ref[head] = jnp.where(upto, mm_nt(query, key), 0.0).astype(bf16)


def mixer_chunk(slot, chunk, rows_in, halo, halo_block, weight, beta_weight, table, doc_ids, conv, old):
    rows, depth = rows_in.shape
    width = weight.shape[2]
    heads = width // HEAD_DIM
    length = doc_ids.shape[0]
    per = 2 if heads % 2 == 0 else 1
    lane = per * HEAD_DIM
    out_wide = pl.BlockSpec((rows, lane), lambda g, c: (slot, g))
    out_square = pl.BlockSpec((per, rows, rows), lambda g, c: (g, slot, 0))
    whole = jax.ShapeDtypeStruct((length, width), f32)
    low = jax.ShapeDtypeStruct((length, width), bf16)
    square = jax.ShapeDtypeStruct((heads, length, rows), bf16)
    flops = 16 * heads * rows * (rows * (rows * 8 + HEAD_DIM * 2) + 3 * depth * HEAD_DIM)
    return pl.pallas_call(
        functools.partial(chunk_kernel, per, len(old)),
        grid_spec=pltpu.PrefetchScalarGridSpec(
            num_scalar_prefetch=1,
            grid=(heads // per,),
            in_specs=[
                pl.BlockSpec((rows, depth), lambda g, c: (0, 0)),
                pl.BlockSpec((HALO, depth), lambda g, c: (halo_block, 0)),
                pl.BlockSpec((3, depth, lane), lambda g, c: (0, 0, g)),
                pl.BlockSpec((depth, heads), lambda g, c: (0, 0)),
                pl.BlockSpec((rows, 16), lambda g, c: (c[0], 0)),
                pl.BlockSpec((rows, 1), lambda g, c: (c[0], 0)),
                pl.BlockSpec((1, rows), lambda g, c: (0, c[0])),
                pl.BlockSpec((3 * CONV, lane), lambda g, c: (0, g)),
            ] + [pl.BlockSpec(memory_space=pl.ANY)] * len(old),
            out_specs=[
                out_wide, out_wide, out_wide,
                pl.BlockSpec((rows, heads), lambda g, c: (slot, 0)),
                out_wide, out_wide, out_wide, out_square, out_square,
            ],
            scratch_shapes=[
                pltpu.VMEM((rows + HALO, depth), bf16),
                pltpu.VMEM((3, rows + HALO, lane), f32),
            ],
        ),
        out_shape=[
            whole, whole, whole, jax.ShapeDtypeStruct((length, heads), f32),
            low, low, low, square, square,
        ],
        input_output_aliases={9 + i: i for i in range(len(old))},
        compiler_params=pltpu.CompilerParams(vmem_limit_bytes=60 * 1024 * 1024),
        cost_estimate=pl.CostEstimate(
            flops=flops, bytes_accessed=rows * width * 60, transcendentals=rows * width * 4
        ),
        name="mixer_chunk",
    )(
        chunk, rows_in, halo, weight, beta_weight, table,
        doc_ids.reshape(length, 1), doc_ids.reshape(1, length), conv, *old,
    )


def scan_kernel(
    heads, me_ref, query_ref, key_ref, value_ref, score_ref, inv_ref, beta_ref, table_ref, gain_ref,
    normed_ref, out_ref, fresh_ref, start_ref, state_ref,
):
    tile = pl.program_id(0)
    factor = HEAD_DIM ** (-0.5)
    rows = query_ref.shape[0]

    @pl.when(tile == 0)
    def _():
        state_ref[...] = jnp.zeros_like(state_ref)

    wide = (rows, HEAD_DIM)
    pad = table_ref[:, 3:4]
    from_start = jnp.broadcast_to(table_ref[:, 4:5], wide)
    to_end = jnp.broadcast_to(table_ref[:, 5:6], wide)
    carry = table_ref[rows - 1 : rows, 4:5]
    gain = gain_ref[...]
    for head in range(heads):
        lanes = pl.ds(head * HEAD_DIM, HEAD_DIM)
        beta = sigmoid(beta_ref[:, head : head + 1]) * pad
        query = query_ref[:, lanes]
        key = key_ref[:, lanes]
        state = state_ref[head]
        low_state = state.astype(bf16)
        start_ref[0, head] = low_state
        right = beta * (value_ref[:, lanes].astype(f32) - from_start * mm(key, low_state))
        fresh = mm(inv_ref[head], right).astype(bf16)
        fresh_ref[:, lanes] = fresh
        state_ref[head] = carry * state + mm_tn(key.astype(f32) * to_end, fresh)
        out = factor * (from_start * mm(query, low_state) + mm(score_ref[head], fresh))
        out_ref[:, lanes] = out
        scale = lax.rsqrt(jnp.mean(out * out, axis=1, keepdims=True) + 1e-05)
        normed_ref[:, lanes] = (out * scale * gain).astype(bf16)


def mixer_scan(me, ring, query, key, value, score, inverse, beta_logit, table, gain):
    length, width = query.shape
    heads = width // HEAD_DIM
    rows = length // ring
    wide = pl.BlockSpec((rows, width), lambda i, m: (rotated(i, m[0], ring), 0))
    square = pl.BlockSpec((heads, rows, rows), lambda i, m: (0, rotated(i, m[0], ring), 0))
    flops = 9 * ring * heads * rows * HEAD_DIM * (rows * 2 + HEAD_DIM * 3)
    return pl.pallas_call(
        functools.partial(scan_kernel, heads),
        grid_spec=pltpu.PrefetchScalarGridSpec(
            num_scalar_prefetch=1,
            grid=(ring,),
            in_specs=[
                wide, wide, wide, square, square,
                pl.BlockSpec((rows, heads), lambda i, m: (rotated(i, m[0], ring), 0)),
                pl.BlockSpec((rows, 16), lambda i, m: (i, 0)),
                pl.BlockSpec((1, HEAD_DIM), lambda i, m: (0, 0)),
            ],
            out_specs=[
                wide, wide, wide,
                pl.BlockSpec((1, heads, HEAD_DIM, HEAD_DIM), lambda i, m: (i, 0, 0, 0)),
            ],
            scratch_shapes=[pltpu.VMEM((heads, HEAD_DIM, HEAD_DIM), f32)],
        ),
        out_shape=[
            jax.ShapeDtypeStruct((length, width), bf16),
            jax.ShapeDtypeStruct((length, width), f32),
            jax.ShapeDtypeStruct((length, width), bf16),
            jax.ShapeDtypeStruct((ring, heads, HEAD_DIM, HEAD_DIM), bf16),
        ],
        compiler_params=pltpu.CompilerParams(vmem_limit_bytes=40 * 1024 * 1024),
        cost_estimate=pl.CostEstimate(
            flops=flops, bytes_accessed=length * width * 18, transcendentals=length * heads
        ),
        name="mixer_scan",
    )(me, query, key, value, score, inverse, beta_logit, table, gain.reshape(1, HEAD_DIM))


def backward_kernel(
    heads, me_ref, q_ref, k_ref, v_ref, q_halo_ref, k_halo_ref, v_halo_ref,
    beta_ref, table_ref, doc_col_ref, doc_row_ref, conv_ref, gain_ref,
    out_ref, fresh_ref, score_ref, inv_ref, start_ref, cot_ref,
    dq_ref, dk_ref, dv_ref, dbeta_ref, dconv_ref, dgain_ref, ext_ref, back_ref, state_ref,
):
    step = pl.program_id(0)
    factor = HEAD_DIM ** (-0.5)
    rows, width = q_ref.shape

    @pl.when(step == 0)
    def _():
        state_ref[...] = jnp.zeros_like(state_ref)
        back_ref[:, pl.ds(rows, HALO), :] = jnp.zeros((3, HALO, width), f32)
        dconv_ref[...] = jnp.zeros_like(dconv_ref)
        dgain_ref[...] = jnp.zeros_like(dgain_ref)

    @pl.when(step > 0)
    def _():
        back_ref[:, pl.ds(rows, HALO), :] = back_ref[:, pl.ds(0, HALO), :]

    for part, (ref, halo) in enumerate(
        ((q_ref, q_halo_ref), (k_ref, k_halo_ref), (v_ref, v_halo_ref))
    ):
        ext_ref[part, pl.ds(0, HALO), :] = halo[...].astype(f32)
        ext_ref[part, pl.ds(HALO, rows), :] = ref[...].astype(f32)
    wide = (rows, HEAD_DIM)
    same = [jnp.broadcast_to(table_ref[:, j : j + 1], wide) for j in range(3)]
    after = [jnp.broadcast_to(table_ref[:, 6 + j : 7 + j], wide) for j in range(3)]
    pad = table_ref[:, 3:4]
    from_start = jnp.broadcast_to(table_ref[:, 4:5], wide)
    to_end = jnp.broadcast_to(table_ref[:, 5:6], wide)
    carry = table_ref[rows - 1 : rows, 4:5]
    row = lax.broadcasted_iota(jnp.int32, (rows, rows), 0)
    col = lax.broadcasted_iota(jnp.int32, (rows, rows), 1)
    together = doc_col_ref[...] == doc_row_ref[...]
    below = together & (row > col)
    upto = together & (row >= col)
    gain = gain_ref[...]
    dgain = jnp.zeros((1, HEAD_DIM), f32)
    for head in range(heads):
        lanes = pl.ds(head * HEAD_DIM, HEAD_DIM)
        sums, sigs, acts = [], [], []
        for part in range(3):
            taps = [conv_ref[part * CONV + j : part * CONV + j + 1, lanes] for j in range(CONV)]
            total = conv_sum(ext_ref, part, rows, lanes, taps, same)
            sig = sigmoid(total)
            sums.append(total)
            sigs.append(sig)
            acts.append(total * sig)
        q_scale = lax.rsqrt(jnp.sum(acts[0] * acts[0], axis=1, keepdims=True) + 1e-06)
        k_scale = lax.rsqrt(jnp.sum(acts[1] * acts[1], axis=1, keepdims=True) + 1e-06)
        query_full = acts[0] * q_scale
        key_unit = acts[1] * k_scale
        beta_sig = sigmoid(beta_ref[:, head : head + 1])
        beta = beta_sig * pad
        key_full = key_unit * pad
        key = key_full.astype(bf16)
        query = query_full.astype(bf16)
        value = acts[2]
        out = out_ref[:, lanes]
        cot = cot_ref[:, lanes].astype(f32)
        scale = lax.rsqrt(jnp.mean(out * out, axis=1, keepdims=True) + 1e-05)
        unit = out * scale
        dgain = dgain + jnp.sum(cot * unit, axis=0, keepdims=True)
        gained = cot * gain
        dout = (factor * scale) * (gained - unit * jnp.mean(unit * gained, axis=1, keepdims=True))
        dout_low = dout.astype(bf16)
        dout_first = (dout * from_start).astype(bf16)
        fresh = fresh_ref[:, lanes]
        start = start_ref[0, head]
        dstate = state_ref[head]
        dstate_low = dstate.astype(bf16)
        inverse = inv_ref[head]
        key_end = (key_full * to_end).astype(bf16)
        scores = score_ref[head]
        dfresh = mm_tn(scores, dout_low) + mm(key_end, dstate_low)
        dright = mm_tn(inverse, dfresh)
        dright_low = dright.astype(bf16)
        dscores = jnp.where(upto, mm_nt(dout_low, fresh), 0.0).astype(bf16)
        dquery = mm_nt(dout_first, start) + mm(dscores, key)
        dstrict = jnp.where(below, -mm_nt(dright_low, fresh), 0.0)
        scaled = (dstrict * beta).astype(bf16)
        weighted = (dright * (beta * from_start)).astype(bf16)
        inner_key = mm(dstrict, key)
        start_key = from_start * mm_nt(dright_low, start)
        dkey = (
            mm_tn(dscores, query)
            + to_end * mm_nt(fresh, dstate_low)
            + beta * (inner_key - start_key)
            + mm_tn(scaled, key)
        )
        dbeta = jnp.sum(
            dright * value + (inner_key - start_key) * key_full, axis=1, keepdims=True
        )
        dvalue = beta * dright
        state_ref[head] = (
            carry * dstate + mm_tn(query, dout_first) - mm_tn(key, weighted)
        )
        dbeta_ref[:, head : head + 1] = dbeta * pad * beta_sig * (1.0 - beta_sig)
        dkey = dkey * pad
        dacts = (
            q_scale * (dquery - query_full * jnp.sum(query_full * dquery, axis=1, keepdims=True)),
            k_scale * (dkey - key_unit * jnp.sum(key_unit * dkey, axis=1, keepdims=True)),
            dvalue,
        )
        for part, target in enumerate((dq_ref, dk_ref, dv_ref)):
            sig = sigs[part]
            dsum = dacts[part] * (sig * (1.0 + sums[part] * (1.0 - sig)))
            back_ref[part, pl.ds(0, rows), lanes] = dsum
            taps = [conv_ref[part * CONV + j : part * CONV + j + 1, lanes] for j in range(CONV)]
            dpre = dsum * taps[0]
            dtaps = [jnp.sum(dsum * ext_ref[part, pl.ds(HALO, rows), lanes], axis=0, keepdims=True)]
            for shift in range(1, CONV):
                dpre = dpre + back_ref[part, pl.ds(shift, rows), lanes] * (after[shift - 1] * taps[shift])
                moved = ext_ref[part, pl.ds(HALO - shift, rows), lanes]
                dtaps.append(jnp.sum(dsum * moved * same[shift - 1], axis=0, keepdims=True))
            target[:, lanes] = dpre.astype(bf16)
            for j in range(CONV):
                spot = slice(part * CONV + j, part * CONV + j + 1)
                dconv_ref[spot, lanes] = dconv_ref[spot, lanes] + dtaps[j]
    dgain_ref[...] = dgain_ref[...] + dgain


def mixer_backward(me, ring, pres, beta_logit, table, doc_ids, conv, gain, saved, cot):
    length, width = pres[0].shape
    heads = width // HEAD_DIM
    rows = length // ring
    last = ring - 1

    def spot(i, m):
        return rotated(last - i, m[0], ring)

    def before(i, m):
        return rotated(jnp.maximum(last - i - 1, 0), m[0], ring)

    per = rows // HALO
    wide = pl.BlockSpec((rows, width), lambda i, m: (spot(i, m), 0))
    halo = pl.BlockSpec((HALO, width), lambda i, m: (before(i, m) * per + per - 1, 0))
    square = pl.BlockSpec((heads, rows, rows), lambda i, m: (0, spot(i, m), 0))
    narrow = pl.BlockSpec((rows, heads), lambda i, m: (spot(i, m), 0))
    flops = 10 * ring * heads * rows * HEAD_DIM * (rows * 9 + HEAD_DIM * 6)
    low = jax.ShapeDtypeStruct((length, width), bf16)
    return pl.pallas_call(
        functools.partial(backward_kernel, heads),
        grid_spec=pltpu.PrefetchScalarGridSpec(
            num_scalar_prefetch=1,
            grid=(ring,),
            in_specs=[
                wide, wide, wide, halo, halo, halo, narrow,
                pl.BlockSpec((rows, 16), lambda i, m: (last - i, 0)),
                pl.BlockSpec((rows, 1), lambda i, m: (last - i, 0)),
                pl.BlockSpec((1, rows), lambda i, m: (0, last - i)),
                pl.BlockSpec((3 * CONV, width), lambda i, m: (0, 0)),
                pl.BlockSpec((1, HEAD_DIM), lambda i, m: (0, 0)),
                wide, wide, square, square,
                pl.BlockSpec((1, heads, HEAD_DIM, HEAD_DIM), lambda i, m: (last - i, 0, 0, 0)),
                wide,
            ],
            out_specs=[
                wide, wide, wide, narrow,
                pl.BlockSpec((3 * CONV, width), lambda i, m: (0, 0)),
                pl.BlockSpec((1, HEAD_DIM), lambda i, m: (0, 0)),
            ],
            scratch_shapes=[
                pltpu.VMEM((3, rows + HALO, width), f32),
                pltpu.VMEM((3, rows + HALO, width), f32),
                pltpu.VMEM((heads, HEAD_DIM, HEAD_DIM), f32),
            ],
        ),
        out_shape=[
            low, low, low,
            jax.ShapeDtypeStruct((length, heads), f32),
            jax.ShapeDtypeStruct((3 * CONV, width), f32),
            jax.ShapeDtypeStruct((1, HEAD_DIM), f32),
        ],
        compiler_params=pltpu.CompilerParams(vmem_limit_bytes=40 * 1024 * 1024),
        cost_estimate=pl.CostEstimate(
            flops=flops, bytes_accessed=length * width * 34, transcendentals=length * width * 3
        ),
        name="mixer_backward",
    )(
        me, *pres, *pres, beta_logit, table,
        doc_ids.reshape(length, 1), doc_ids.reshape(1, length), conv, gain.reshape(1, HEAD_DIM),
        *saved, cot,
    )


def spread(place, order):
    mask = 0
    for i, bit in enumerate(order):
        mask = mask | (((place >> (len(order) - 1 - i)) & 1) << bit)
    return mask


def place_of(mask, order):
    place = 0
    for i, bit in enumerate(order):
        place = place | (((mask >> bit) & 1) << (len(order) - 1 - i))
    return place


def pieces_kernel(slots, shared, me_ref, *refs):
    count = 2 + 2 * shared
    lefts = [refs[i * slots : (i + 1) * slots] for i in range(count)]
    at = count * slots
    rights = [refs[at + i * slots : at + (i + 1) * slots] for i in range(2 + shared)]
    outs = refs[at + (2 + shared) * slots :]
    wide = lefts[0][0].shape[1]
    half = wide // 2

    def product(left, right, cols):
        total = None
        for l, r in zip(left, right):
            term = lax.dot_general(
                l[:, cols], r[...], (((0,), (0,)), ((), ())), preferred_element_type=f32
            )
            total = term if total is None else total + term
        return total.astype(bf16)

    for color in range(2):
        out = outs[color]
        out[0, pl.ds(0, wide), :] = product(lefts[color], rights[color], slice(0, wide))
        cols = slice(color * half, (color + 1) * half)
        for i in range(shared):
            spot = pl.ds(wide + i * half, half)
            out[0, spot, :] = product(lefts[2 + 2 * i + color], rights[2 + i], cols)


def grad_pieces(me, orders, first, units):
    slots = len(units[0][0])
    shared = len(units) - 2
    size = 2 ** len(orders[0])
    depth = units[0][0][0][0].shape[1]
    piece = depth // size
    rows = units[0][0][0][1][1]
    cols = units[0][1][0][0].shape[1]

    def left_spec(block, color):
        return pl.BlockSpec(
            (rows, piece), lambda i, m: (block, m[0] ^ spread(i + first, orders[color]))
        )

    def right_spec(block):
        return pl.BlockSpec((rows, cols), lambda i, m: (block, 0), pipeline_mode=pl.Buffered(1))

    arrays, specs = [], []
    for color in range(2):
        for array, (block, _) in units[color][0]:
            arrays.append(array)
            specs.append(left_spec(block, color))
    for unit in units[2:]:
        for color in range(2):
            for array, (block, _) in unit[0]:
                arrays.append(array)
                specs.append(left_spec(block, color))
    for unit in units:
        for array, (block, _) in unit[1]:
            arrays.append(array)
            specs.append(right_spec(block))
    high = piece + shared * (piece // 2)
    out = jax.ShapeDtypeStruct((size // 2, high, cols), bf16)
    flops = 2 * slots * rows * cols * high * size
    return pl.pallas_call(
        functools.partial(pieces_kernel, slots, shared),
        grid_spec=pltpu.PrefetchScalarGridSpec(
            num_scalar_prefetch=1,
            grid=(size // 2,),
            in_specs=specs,
            out_specs=[pl.BlockSpec((1, high, cols), lambda i, m: (i, 0, 0))] * 2,
        ),
        out_shape=[out, out],
        compiler_params=pltpu.CompilerParams(vmem_limit_bytes=40 * 1024 * 1024),
        cost_estimate=pl.CostEstimate(
            flops=flops, bytes_accessed=size * high * cols * 4, transcendentals=0
        ),
        name="grad_pieces",
    )(me, *arrays)


def assemble_kernel(order_core, turned, me_ref, own_a, own_b, got_a, got_b, stack_ref, turned_ref):
    step = pl.program_id(0)
    mine = (((step ^ me_ref[0]) >> order_core) & 1) == 0
    piece = turned_ref.shape[1]
    half = piece // 2
    count = stack_ref.shape[0]

    def pick(own, got, at, high):
        spot = pl.ds(at, high)
        return jnp.where(mine, own[0, spot, :], got[0, spot, :]).astype(f32)

    stack_ref[0] = pick(own_a, got_a, 0, piece)
    stack_ref[1] = pick(own_b, got_b, 0, piece)
    for i in range(count - 2 + 1):
        at = piece + i * half
        top = pick(own_a, got_a, at, half)
        low = pick(own_b, got_b, at, half)
        if i < count - 2:
            stack_ref[2 + i, pl.ds(0, half), :] = top
            stack_ref[2 + i, pl.ds(half, half), :] = low
        else:
            turned_ref[...] = jnp.concatenate([top, low], axis=0).T


def assemble(me, orders, own, got, count):
    places, high, cols = own[0].shape
    size = 2 * places
    piece = 2 * high // (count + 1)
    depth = size * piece

    def spec(color):
        return pl.BlockSpec(
            (1, high, cols), lambda a, m: (place_of(a ^ m[0], orders[color]) & (places - 1), 0, 0)
        )

    return pl.pallas_call(
        functools.partial(assemble_kernel, orders[0][0], True),
        grid_spec=pltpu.PrefetchScalarGridSpec(
            num_scalar_prefetch=1,
            grid=(size,),
            in_specs=[spec(0), spec(1), spec(0), spec(1)],
            out_specs=[
                pl.BlockSpec((count, piece, cols), lambda a, m: (0, a, 0)),
                pl.BlockSpec((cols, piece), lambda a, m: (0, a)),
            ],
        ),
        out_shape=[
            jax.ShapeDtypeStruct((count, depth, cols), f32),
            jax.ShapeDtypeStruct((cols, depth), f32),
        ],
        compiler_params=pltpu.CompilerParams(vmem_limit_bytes=40 * 1024 * 1024),
        cost_estimate=pl.CostEstimate(
            flops=0, bytes_accessed=size * high * cols * 20, transcendentals=0
        ),
        name="assemble",
    )(me, *own, *got)


def dot_f32(a, b):
    return jnp.dot(a, b, preferred_element_type=f32)


def dot_nt(a, b):
    return lax.dot_general(a, b, (((1,), (1,)), ((), ())), preferred_element_type=f32)


def dot_tn(a, b):
    return lax.dot_general(a, b, (((0,), (0,)), ((), ())), preferred_element_type=f32)


def rms_forward(rows, gain):
    scale = lax.rsqrt(jnp.mean(rows * rows, axis=-1, keepdims=True) + 1e-06)
    return (rows * scale * gain).astype(bf16), scale


def rms_backward(rows, scale, gain, grad):
    scaled = grad * gain
    mean = jnp.mean(scaled * rows, axis=-1, keepdims=True)
    gain_grad = jnp.sum(grad * rows * scale, axis=0)
    return scale * scaled - (scale * scale * scale) * rows * mean, gain_grad


def after(value, *others):
    return lax.optimization_barrier((value, *others))[0]


def bits_of(count):
    return [b for b in range(count.bit_length() - 1)]


def add_low(a, b):
    return (a.astype(f32) + b.astype(f32)).astype(bf16)


class Order:
    def __init__(self):
        self.last = []

    def wait(self, *values):
        flat, tree = jax.tree.flatten(values)
        held = lax.optimization_barrier((tuple(flat), tuple(self.last)))[0]
        out = jax.tree.unflatten(tree, held)
        return out if len(out) > 1 else out[0]

    def done(self, *values):
        self.last = jax.tree.leaves(values)
        return values if len(values) > 1 else values[0]


class Ring:
    def __init__(self, size):
        self.size = size
        self.me = lax.axis_index("heads")

    def back(self, value):
        return lax.ppermute(value, "heads", [(i, (i - 1) % self.size) for i in range(self.size)])

    def shift(self, value, by):
        return lax.ppermute(value, "heads", [(i, (i + by) % self.size) for i in range(self.size)])

    def small(self, vector):
        for bit in bits_of(self.size):
            moved = lax.ppermute(vector, "heads", [(i, i ^ (1 << bit)) for i in range(self.size)])
            vector = vector + moved
        return vector

    def gather(self, rows):
        slots = [rows]
        for _ in range(self.size - 1):
            slots.append(self.back(slots[-1]))
        return slots


def spots(arrays):
    return [(array, (0, array.shape[0])) for array in arrays]


def cuts(array, size):
    return [(array, (k, array.shape[0] // size)) for k in range(size)]


class Groups:
    def __init__(self, size):
        self.size = size
        self.bits = bits_of(size)
        self.me = lax.axis_index("dp")

    def swap(self, value, bit):
        return lax.ppermute(value, "dp", [(i, i ^ (1 << bit)) for i in range(self.size)])

    def orders(self):
        first, rest = self.bits[:1], self.bits[1:]
        return first + rest, first + rest[::-1]

    def swap_all(self, values, step):
        return [self.swap(value, self.orders()[color][step]) for color, value in enumerate(values)]

    def narrow(self, keeps, moved):
        half = keeps[0].shape[0] // 2
        if half:
            sends = [add_low(k[half:], m[half:]) for k, m in zip(keeps, moved)]
        else:
            sends, half = [], 1
        return sends, [add_low(k[:half], m[:half]) for k, m in zip(keeps, moved)]

    def widen(self, keeps, moved):
        return [jnp.concatenate([k, m]) for k, m in zip(keeps, moved)]

    def small(self, vector):
        for bit in self.bits:
            vector = vector + self.swap(vector, bit)
        return vector


class Reduction:
    def __init__(self, groups, order, units, count):
        self.groups, self.order, self.count = groups, order, count
        self.me = groups.me.astype(jnp.int32).reshape(1)
        self.units = units
        self.at = 0
        self.steps = len(groups.bits)

    def part(self, first):
        units = [(list(left), list(right)) for left, right in self.units]
        array, spot = units[0][1][0]
        units[0][1][0] = (self.order.wait(array), spot)
        return self.order.done(*grad_pieces(self.me, self.groups.orders(), first, units))

    def send(self):
        self.moved = self.groups.swap_all(self.part(self.groups.size // 2), 0)

    def keep(self):
        self.keeps = list(self.part(0))

    def left(self):
        return 2 * self.steps - 1 - self.at

    def advance(self):
        moved = self.order.wait(self.moved)
        if self.at < self.steps:
            sends, self.keeps = self.groups.narrow(self.keeps, moved)
            self.order.done(self.keeps)
            step = min(self.at + 1, self.steps - 1)
            self.moved = self.groups.swap_all(sends or self.keeps, step)
        else:
            self.keeps = self.groups.widen(self.keeps, moved)
            self.order.done(self.keeps)
            self.moved = self.groups.swap_all(self.keeps, 2 * self.steps - 2 - self.at)
        self.at += 1

    def finish(self):
        while self.left():
            self.advance()
        moved = self.order.wait(self.moved)
        return self.order.done(*assemble(self.me, self.groups.orders(), self.keeps, moved, self.count))


def shards(
    heads_size,
    dp_size,
    block_input,
    doc_ids,
    pad_mask,
    first_gain,
    qkv_weight,
    beta_weight,
    conv_weight,
    out_gain,
    out_weight,
    second_gain,
    gate_up_weight,
    down_weight,
    cotangent,
):
    ring = Ring(heads_size)
    groups = Groups(dp_size)
    order = Order()
    size = heads_size
    steps = len(groups.bits)
    local_rows, model_width = block_input.shape
    width = qkv_weight.shape[2]
    me = ring.me.astype(jnp.int32)
    me_one = me.reshape(1)
    pad_float = pad_mask.astype(f32)
    pad_rows = lax.dynamic_slice_in_dim(pad_float, me * local_rows, local_rows, 0)
    rows_float = block_input.astype(f32)
    first_float = first_gain.astype(f32)
    second_float = second_gain.astype(f32)
    conv_float = conv_weight.astype(f32).reshape(3 * CONV, width)
    gain_float = out_gain.astype(f32)

    share = out_weight.shape[0] // dp_size
    own_share = lax.dynamic_slice_in_dim(out_weight, groups.me * share, share, 0)
    shares = lax.all_gather(own_share, "heads", axis=0)
    halo_raw = ring.shift(block_input[local_rows - HALO :], 1)
    halo_rows, _ = rms_forward(halo_raw.astype(f32), first_float)
    xn_first, first_scale = rms_forward(rows_float, first_float)
    first_slots = ring.gather(after(xn_first, halo_rows))
    grad_rows = cotangent.astype(f32) * pad_rows[:, None]
    grad_low = grad_rows.astype(bf16)
    table = token_table(doc_ids, pad_float, local_rows)
    old = []
    for k in range(size):
        chunk = lax.rem(me + k, size).reshape(1)
        halo, halo_block = (halo_rows, 0) if k == 0 else (first_slots[k - 1], local_rows // HALO - 1)
        old = mixer_chunk(
            k, chunk, first_slots[k], halo, halo_block, qkv_weight, beta_weight, table, doc_ids,
            conv_float, old,
        )
        if k == 1:
            out_all_heads = lax.all_gather(after(shares, old[3]), "dp", axis=1, tiled=True)
        if k == size - 2:
            grad_all = lax.all_gather(after(grad_low, first_slots[-1], old[3]), "heads", axis=0)
    *pre_all, beta_all, query, key, value, score, inverse = old

    normed, out_all, fresh, starts = mixer_scan(
        me_one, size, query, key, value, score, inverse, beta_all, table, gain_float
    )
    saved = (out_all, fresh, score, inverse, starts)
    blocks = [normed[k * local_rows : (k + 1) * local_rows] for k in range(size)]
    moved = [ring.shift(blocks[k], k) for k in range(1, size)]
    mixed = dot_f32(blocks[0], out_weight)
    for k in range(1, size):
        source = lax.rem(me - k + size, size)
        weight = lax.dynamic_index_in_dim(out_all_heads, source, 0, keepdims=False)
        mixed = mixed + dot_f32(moved[k - 1], weight)
    hidden_one = rows_float + mixed
    xn_second, second_scale = rms_forward(hidden_one, second_float)

    second_slots = ring.gather(xn_second)
    grad_slots, hiddens, gates, ups = [], [], [], []
    total = moving_sum = None
    for k in range(size):
        source = lax.rem(me + k, size)
        if k > 2:
            total = add_low(back, moving_sum)
            moving_sum = ring.back(total)
            second_slots[k] = after(second_slots[k], total)
        if k:
            arrived = after(grad_all, second_slots[k])
            grad_slots.append(lax.dynamic_index_in_dim(arrived, source, 0, keepdims=False))
        else:
            grad_slots.append(grad_low)
        gate = dot_f32(second_slots[k], gate_up_weight[0])
        up = dot_f32(second_slots[k], gate_up_weight[1])
        grad_hidden = dot_nt(grad_slots[k], down_weight)
        sig = sigmoid(gate)
        swish = gate * sig
        hiddens.append((swish * up).astype(bf16))
        gates.append((grad_hidden * up * sig * (1.0 + gate * (1.0 - sig))).astype(bf16))
        ups.append((grad_hidden * swish).astype(bf16))
        back = dot_nt(gates[k], gate_up_weight[0]) + dot_nt(ups[k], gate_up_weight[1])
        if k == 0:
            own_back = back
        elif k == 1:
            moving_sum = ring.back(back.astype(bf16))
    total = add_low(back, moving_sum)
    moving_sum = ring.back(total)
    order.done(total)

    ffn_units = [
        (spots(second_slots), spots(gates)),
        (spots(second_slots), spots(ups)),
        (spots(grad_slots), spots(hiddens)),
    ]
    ffn = Reduction(groups, order, ffn_units, 2)
    ffn.send()
    ffn.keep()
    ffn.advance()
    grad_xn_second = own_back + order.wait(moving_sum).astype(f32)
    grad_part, second_gain_grad = rms_backward(hidden_one, second_scale, second_float, grad_xn_second)
    grad_h1 = grad_rows + grad_part
    mid_slots = [order.done(grad_h1.astype(bf16))]
    downs, normeds = [], []
    for k in range(size):
        if k + 1 < size:
            moving = ring.back(mid_slots[k])
        if k == 0:
            downs = [dot_f32(order.wait(hidden), down_weight) for hidden in hiddens]
            order.done(downs)
        if k + 2 == size:
            ffn.advance()
        normeds.append(order.done(dot_nt(order.wait(mid_slots[k]), out_weight).astype(bf16)))
        if k + 1 < size:
            mid_slots.append(order.wait(moving))
            order.done(mid_slots[-1])
    ffn.advance()
    down_moving = ring.back(order.wait(downs[1 % size].astype(bf16)))
    *grad_pres, grad_logit, conv_part, out_gain_part = mixer_backward(
        me_one, size, pre_all, beta_all, table, doc_ids, conv_float, gain_float, saved,
        order.wait(jnp.concatenate(normeds)),
    )
    grad_logit = order.done(grad_logit.astype(bf16), grad_pres[0])[0]

    def first_partial(k):
        rows = slice(k * local_rows, (k + 1) * local_rows)
        total = dot_nt(order.wait(grad_logit[rows]), beta_weight)
        for i in range(3):
            total = total + dot_nt(order.wait(grad_pres[i][rows]), qkv_weight[i])
        return total

    total = order.done(first_partial(1 % size).astype(bf16))
    moving_sum = ring.back(total)
    ffn.advance()
    qkv = Reduction(
        groups,
        order,
        [
            (spots(first_slots), cuts(grad_pres[0], size)),
            (spots(first_slots), cuts(grad_pres[1], size)),
            (spots(first_slots), cuts(grad_pres[2], size)),
            (spots(mid_slots), cuts(normed, size)),
        ],
        3,
    )
    qkv.send()
    down_total = order.done(add_low(downs[2 % size], order.wait(down_moving)))
    qkv.keep()
    qkv.advance()
    partial = order.done(first_partial(2 % size))
    for k in range(2, size):
        total = order.done(add_low(partial, order.wait(moving_sum)))
        moving_sum = ring.back(total)
        partial = order.done(first_partial((k + 1) % size))
        if k == 2:
            while ffn.left():
                ffn.advance()
    qkv.advance()
    grad_xn_first = partial + order.wait(moving_sum).astype(f32)
    grad_x_part, first_gain_part = rms_backward(rows_float, first_scale, first_float, grad_xn_first)
    input_grad = order.done(grad_h1 + grad_x_part)
    down_moving = ring.back(order.wait(down_total))
    qkv.advance()
    gate_up_grad, down_grad = ffn.finish()
    qkv.advance()
    beta_part = 0.0
    for k in range(size):
        beta_part = beta_part + dot_tn(first_slots[k], grad_logit[k * local_rows : (k + 1) * local_rows])
    for k in range(3, size):
        down_total = order.done(add_low(downs[k], order.wait(down_moving)))
        down_moving = ring.back(down_total)
    output = hidden_one + downs[0] + order.wait(down_moving).astype(f32)
    block_output = order.done(output.astype(bf16))
    qkv_grad, out_grad = qkv.finish()

    tiny = (beta_part, conv_part, second_gain_grad, out_gain_part)
    small = groups.small(jnp.concatenate([v.reshape(-1) for v in tiny]))
    count = beta_part.size
    gains_at = count + conv_part.size
    beta_grad = small[:count].reshape(beta_part.shape)
    conv_grad = small[count:gains_at].reshape(3, CONV, width)
    gains = ring.small(small[gains_at:])
    first_gain_grad = ring.small(groups.small(first_gain_part))
    return (
        block_output,
        input_grad,
        first_gain_grad,
        qkv_grad,
        beta_grad,
        conv_grad,
        gains[model_width:],
        out_grad,
        gains[:model_width],
        gate_up_grad,
        down_grad,
    )


def solution(mesh):
    rows = P(("dp", "heads"), None)
    last = P(None, None, "heads")
    return jax.shard_map(
        functools.partial(shards, mesh.shape["heads"], mesh.shape["dp"]),
        mesh=mesh,
        in_specs=(
            rows, P("dp"), P("dp"), P(), last, P(None, "heads"), last, P(), P("heads", None), P(),
            last, P("heads", None), rows,
        ),
        out_specs=(
            rows, rows, P(), last, P(None, "heads"), last, P(), P("heads", None), P(), last,
            P("heads", None),
        ),
        check_vma=False,
    )
```

```python
import functools
import jax
import jax.numpy as jnp
from jax import lax
from jax.experimental import pallas as pl
from jax.experimental.pallas import tpu as pltpu
from jax.sharding import PartitionSpec as P

HEAD_DIM = 128
CONV = 4
HALO = 16
f32 = jnp.float32
bf16 = jnp.bfloat16


def mm(a, b):
    return jnp.dot(a.astype(bf16), b.astype(bf16), preferred_element_type=f32)


def mm_nt(a, b):
    return lax.dot_general(
        a.astype(bf16), b.astype(bf16), (((1,), (1,)), ((), ())), preferred_element_type=f32
    )


def mm_tn(a, b):
    return lax.dot_general(
        a.astype(bf16), b.astype(bf16), (((0,), (0,)), ((), ())), preferred_element_type=f32
    )


def token_table(doc_ids, pad_float, tile):
    length = doc_ids.shape[0]
    minus = jnp.full((tile,), -1, jnp.int32)
    padded = jnp.concatenate([minus, doc_ids, minus])

    def same(shift):
        moved = lax.slice_in_dim(padded, tile - shift, tile - shift + length, axis=0)
        return (moved == doc_ids).astype(f32)

    tiles = doc_ids.reshape(length // tile, tile)
    ends = tiles[:, -1]
    before = jnp.concatenate([jnp.full((1,), -1, jnp.int32), ends[:-1]])
    from_start = (tiles == before[:, None]).astype(f32).reshape(length)
    to_end = (tiles == ends[:, None]).astype(f32).reshape(length)
    columns = [same(1), same(2), same(3), pad_float, from_start, to_end, same(-1), same(-2), same(-3)]
    columns += [jnp.zeros((length,), f32)] * (16 - len(columns))
    return jnp.stack(columns, axis=1)


def sigmoid(x):
    return 1.0 / (1.0 + jnp.exp(-x))


def block_inverse(strict, apart):
    size = strict.shape[0]
    zero = jnp.zeros_like(strict)
    inverse = jnp.where(apart == 0, 1.0, jnp.where(apart == 1, -strict, zero))
    low = strict.astype(bf16)
    low_zero = jnp.zeros_like(low)
    step = 2
    while step < size:
        part = jnp.where((apart >= step) & (apart < 2 * step), low, low_zero)
        held = inverse.astype(bf16)
        inverse = inverse - mm(held, mm(part, held))
        step *= 2
    return inverse


def unit_inverse(strict):
    size = strict.shape[0]
    half = min(size, 128)
    row = lax.broadcasted_iota(jnp.int32, (half, half), 0)
    col = lax.broadcasted_iota(jnp.int32, (half, half), 1)
    apart = row ^ col
    if size == half:
        return block_inverse(strict, apart)
    top = strict[:half, :half]
    bottom = strict[half:, half:]
    top = block_inverse(top, apart)
    bottom = block_inverse(bottom, apart)
    cross = -mm(bottom, mm(strict[half:, :half], top))
    return jnp.concatenate(
        [jnp.concatenate([top, jnp.zeros_like(top)], axis=1), jnp.concatenate([cross, bottom], axis=1)],
        axis=0,
    )


def conv_sum(ext_ref, part, rows, lanes, taps, same):
    total = ext_ref[part, pl.ds(HALO, rows), lanes] * taps[0]
    for shift in range(1, CONV):
        total = total + ext_ref[part, pl.ds(HALO - shift, rows), lanes] * taps[shift] * same[shift - 1]
    return total


def rotated(tile, me, ring):
    return lax.rem(tile - me + ring, ring)


def chunk_kernel(
    heads, old, where_ref, x_ref, x_halo_ref, weight_ref, beta_weight_ref,
    table_ref, doc_col_ref, doc_row_ref, conv_ref, *rest,
):
    outs = rest[old:]
    (q_pre_ref, k_pre_ref, v_pre_ref, beta_out_ref,
     query_ref, key_ref, value_ref, score_ref, inv_ref, x_ext_ref, ext_ref) = outs
    group = pl.program_id(0)
    rows = x_ref.shape[0]

    @pl.when(group == 0)
    def _():
        x_ext_ref[pl.ds(0, HALO), :] = x_halo_ref[...]
        x_ext_ref[pl.ds(HALO, rows), :] = x_ref[...]
        beta_out_ref[...] = jnp.dot(x_ref[...], beta_weight_ref[...], preferred_element_type=f32)

    for part, copy in enumerate((q_pre_ref, k_pre_ref, v_pre_ref)):
        pre = jnp.dot(x_ext_ref[...], weight_ref[part], preferred_element_type=f32)
        ext_ref[part] = pre
        copy[...] = pre[HALO:]
    wide = (rows, HEAD_DIM)
    same = [jnp.broadcast_to(table_ref[:, j : j + 1], wide) for j in range(3)]
    pad = table_ref[:, 3:4]
    row = lax.broadcasted_iota(jnp.int32, (rows, rows), 0)
    col = lax.broadcasted_iota(jnp.int32, (rows, rows), 1)
    together = doc_col_ref[...] == doc_row_ref[...]
    below = together & (row > col)
    upto = together & (row >= col)
    betas = sigmoid(beta_out_ref[...]) * pad
    lane = lax.broadcasted_iota(jnp.int32, betas.shape, 1)
    for head in range(heads):
        lanes = pl.ds(head * HEAD_DIM, HEAD_DIM)
        acts = []
        for part in range(3):
            taps = [conv_ref[part * CONV + j : part * CONV + j + 1, lanes] for j in range(CONV)]
            total = conv_sum(ext_ref, part, rows, lanes, taps, same)
            acts.append(total * sigmoid(total))
        query = acts[0] * lax.rsqrt(jnp.sum(acts[0] * acts[0], axis=1, keepdims=True) + 1e-06)
        key = acts[1] * (lax.rsqrt(jnp.sum(acts[1] * acts[1], axis=1, keepdims=True) + 1e-06) * pad)
        beta = jnp.sum(jnp.where(lane == group * heads + head, betas, 0.0), axis=1, keepdims=True)
        key = key.astype(bf16)
        query = query.astype(bf16)
        query_ref[:, lanes] = query
        key_ref[:, lanes] = key
        value_ref[:, lanes] = acts[2].astype(bf16)
        strict = jnp.where(below, mm_nt(key, key) * beta, 0.0)
        inv_ref[head] = unit_inverse(strict).astype(bf16)
        score_ref[head] = jnp.where(upto, mm_nt(query, key), 0.0).astype(bf16)


def mixer_chunk(slot, chunk, rows_in, halo, halo_block, weight, beta_weight, table, doc_ids, conv, old):
    rows, depth = rows_in.shape
    width = weight.shape[2]
    heads = width // HEAD_DIM
    length = doc_ids.shape[0]
    per = 2 if heads % 2 == 0 else 1
    lane = per * HEAD_DIM
    out_wide = pl.BlockSpec((rows, lane), lambda g, c: (slot, g))
    out_square = pl.BlockSpec((per, rows, rows), lambda g, c: (g, slot, 0))
    whole = jax.ShapeDtypeStruct((length, width), f32)
    low = jax.ShapeDtypeStruct((length, width), bf16)
    square = jax.ShapeDtypeStruct((heads, length, rows), bf16)
    flops = 16 * heads * rows * (rows * (rows * 8 + HEAD_DIM * 2) + 3 * depth * HEAD_DIM)
    return pl.pallas_call(
        functools.partial(chunk_kernel, per, len(old)),
        grid_spec=pltpu.PrefetchScalarGridSpec(
            num_scalar_prefetch=1,
            grid=(heads // per,),
            in_specs=[
                pl.BlockSpec((rows, depth), lambda g, c: (0, 0)),
                pl.BlockSpec((HALO, depth), lambda g, c: (halo_block, 0)),
                pl.BlockSpec((3, depth, lane), lambda g, c: (0, 0, g)),
                pl.BlockSpec((depth, heads), lambda g, c: (0, 0)),
                pl.BlockSpec((rows, 16), lambda g, c: (c[0], 0)),
                pl.BlockSpec((rows, 1), lambda g, c: (c[0], 0)),
                pl.BlockSpec((1, rows), lambda g, c: (0, c[0])),
                pl.BlockSpec((3 * CONV, lane), lambda g, c: (0, g)),
            ] + [pl.BlockSpec(memory_space=pl.ANY)] * len(old),
            out_specs=[
                out_wide, out_wide, out_wide,
                pl.BlockSpec((rows, heads), lambda g, c: (slot, 0)),
                out_wide, out_wide, out_wide, out_square, out_square,
            ],
            scratch_shapes=[
                pltpu.VMEM((rows + HALO, depth), bf16),
                pltpu.VMEM((3, rows + HALO, lane), f32),
            ],
        ),
        out_shape=[
            whole, whole, whole, jax.ShapeDtypeStruct((length, heads), f32),
            low, low, low, square, square,
        ],
        input_output_aliases={9 + i: i for i in range(len(old))},
        compiler_params=pltpu.CompilerParams(vmem_limit_bytes=60 * 1024 * 1024),
        cost_estimate=pl.CostEstimate(
            flops=flops, bytes_accessed=rows * width * 60, transcendentals=rows * width * 4
        ),
        name="mixer_chunk",
    )(
        chunk, rows_in, halo, weight, beta_weight, table,
        doc_ids.reshape(length, 1), doc_ids.reshape(1, length), conv, *old,
    )


def scan_kernel(
    heads, me_ref, query_ref, key_ref, value_ref, score_ref, inv_ref, beta_ref, table_ref, gain_ref,
    normed_ref, out_ref, fresh_ref, start_ref, state_ref,
):
    tile = pl.program_id(0)
    factor = HEAD_DIM ** (-0.5)
    rows = query_ref.shape[0]

    @pl.when(tile == 0)
    def _():
        state_ref[...] = jnp.zeros_like(state_ref)

    wide = (rows, HEAD_DIM)
    pad = table_ref[:, 3:4]
    from_start = jnp.broadcast_to(table_ref[:, 4:5], wide)
    to_end = jnp.broadcast_to(table_ref[:, 5:6], wide)
    carry = table_ref[rows - 1 : rows, 4:5]
    gain = gain_ref[...]
    for head in range(heads):
        lanes = pl.ds(head * HEAD_DIM, HEAD_DIM)
        beta = sigmoid(beta_ref[:, head : head + 1]) * pad
        query = query_ref[:, lanes]
        key = key_ref[:, lanes]
        state = state_ref[head]
        low_state = state.astype(bf16)
        start_ref[0, head] = low_state
        right = beta * (value_ref[:, lanes].astype(f32) - from_start * mm(key, low_state))
        fresh = mm(inv_ref[head], right).astype(bf16)
        fresh_ref[:, lanes] = fresh
        state_ref[head] = carry * state + mm_tn(key.astype(f32) * to_end, fresh)
        out = factor * (from_start * mm(query, low_state) + mm(score_ref[head], fresh))
        out_ref[:, lanes] = out
        scale = lax.rsqrt(jnp.mean(out * out, axis=1, keepdims=True) + 1e-05)
        normed_ref[:, lanes] = (out * scale * gain).astype(bf16)


def mixer_scan(me, ring, query, key, value, score, inverse, beta_logit, table, gain):
    length, width = query.shape
    heads = width // HEAD_DIM
    rows = length // ring
    wide = pl.BlockSpec((rows, width), lambda i, m: (rotated(i, m[0], ring), 0))
    square = pl.BlockSpec((heads, rows, rows), lambda i, m: (0, rotated(i, m[0], ring), 0))
    flops = 9 * ring * heads * rows * HEAD_DIM * (rows * 2 + HEAD_DIM * 3)
    return pl.pallas_call(
        functools.partial(scan_kernel, heads),
        grid_spec=pltpu.PrefetchScalarGridSpec(
            num_scalar_prefetch=1,
            grid=(ring,),
            in_specs=[
                wide, wide, wide, square, square,
                pl.BlockSpec((rows, heads), lambda i, m: (rotated(i, m[0], ring), 0)),
                pl.BlockSpec((rows, 16), lambda i, m: (i, 0)),
                pl.BlockSpec((1, HEAD_DIM), lambda i, m: (0, 0)),
            ],
            out_specs=[
                wide, wide, wide,
                pl.BlockSpec((1, heads, HEAD_DIM, HEAD_DIM), lambda i, m: (i, 0, 0, 0)),
            ],
            scratch_shapes=[pltpu.VMEM((heads, HEAD_DIM, HEAD_DIM), f32)],
        ),
        out_shape=[
            jax.ShapeDtypeStruct((length, width), bf16),
            jax.ShapeDtypeStruct((length, width), f32),
            jax.ShapeDtypeStruct((length, width), bf16),
            jax.ShapeDtypeStruct((ring, heads, HEAD_DIM, HEAD_DIM), bf16),
        ],
        compiler_params=pltpu.CompilerParams(vmem_limit_bytes=40 * 1024 * 1024),
        cost_estimate=pl.CostEstimate(
            flops=flops, bytes_accessed=length * width * 18, transcendentals=length * heads
        ),
        name="mixer_scan",
    )(me, query, key, value, score, inverse, beta_logit, table, gain.reshape(1, HEAD_DIM))


def backward_kernel(
    heads, me_ref, q_ref, k_ref, v_ref, q_halo_ref, k_halo_ref, v_halo_ref,
    beta_ref, table_ref, doc_col_ref, doc_row_ref, conv_ref, gain_ref,
    out_ref, fresh_ref, score_ref, inv_ref, start_ref, cot_ref,
    dq_ref, dk_ref, dv_ref, dbeta_ref, dconv_ref, dgain_ref, ext_ref, back_ref, state_ref,
):
    step = pl.program_id(0)
    factor = HEAD_DIM ** (-0.5)
    rows, width = q_ref.shape

    @pl.when(step == 0)
    def _():
        state_ref[...] = jnp.zeros_like(state_ref)
        back_ref[:, pl.ds(rows, HALO), :] = jnp.zeros((3, HALO, width), f32)
        dconv_ref[...] = jnp.zeros_like(dconv_ref)
        dgain_ref[...] = jnp.zeros_like(dgain_ref)

    @pl.when(step > 0)
    def _():
        back_ref[:, pl.ds(rows, HALO), :] = back_ref[:, pl.ds(0, HALO), :]

    for part, (ref, halo) in enumerate(
        ((q_ref, q_halo_ref), (k_ref, k_halo_ref), (v_ref, v_halo_ref))
    ):
        ext_ref[part, pl.ds(0, HALO), :] = halo[...].astype(f32)
        ext_ref[part, pl.ds(HALO, rows), :] = ref[...].astype(f32)
    wide = (rows, HEAD_DIM)
    same = [jnp.broadcast_to(table_ref[:, j : j + 1], wide) for j in range(3)]
    after = [jnp.broadcast_to(table_ref[:, 6 + j : 7 + j], wide) for j in range(3)]
    pad = table_ref[:, 3:4]
    from_start = jnp.broadcast_to(table_ref[:, 4:5], wide)
    to_end = jnp.broadcast_to(table_ref[:, 5:6], wide)
    carry = table_ref[rows - 1 : rows, 4:5]
    row = lax.broadcasted_iota(jnp.int32, (rows, rows), 0)
    col = lax.broadcasted_iota(jnp.int32, (rows, rows), 1)
    together = doc_col_ref[...] == doc_row_ref[...]
    below = together & (row > col)
    upto = together & (row >= col)
    gain = gain_ref[...]
    dgain = jnp.zeros((1, HEAD_DIM), f32)
    for head in range(heads):
        lanes = pl.ds(head * HEAD_DIM, HEAD_DIM)
        sums, sigs, acts = [], [], []
        for part in range(3):
            taps = [conv_ref[part * CONV + j : part * CONV + j + 1, lanes] for j in range(CONV)]
            total = conv_sum(ext_ref, part, rows, lanes, taps, same)
            sig = sigmoid(total)
            sums.append(total)
            sigs.append(sig)
            acts.append(total * sig)
        q_scale = lax.rsqrt(jnp.sum(acts[0] * acts[0], axis=1, keepdims=True) + 1e-06)
        k_scale = lax.rsqrt(jnp.sum(acts[1] * acts[1], axis=1, keepdims=True) + 1e-06)
        query_full = acts[0] * q_scale
        key_unit = acts[1] * k_scale
        beta_sig = sigmoid(beta_ref[:, head : head + 1])
        beta = beta_sig * pad
        key_full = key_unit * pad
        key = key_full.astype(bf16)
        query = query_full.astype(bf16)
        value = acts[2]
        out = out_ref[:, lanes]
        cot = cot_ref[:, lanes].astype(f32)
        scale = lax.rsqrt(jnp.mean(out * out, axis=1, keepdims=True) + 1e-05)
        unit = out * scale
        dgain = dgain + jnp.sum(cot * unit, axis=0, keepdims=True)
        gained = cot * gain
        dout = (factor * scale) * (gained - unit * jnp.mean(unit * gained, axis=1, keepdims=True))
        dout_low = dout.astype(bf16)
        dout_first = (dout * from_start).astype(bf16)
        fresh = fresh_ref[:, lanes]
        start = start_ref[0, head]
        dstate = state_ref[head]
        dstate_low = dstate.astype(bf16)
        inverse = inv_ref[head]
        key_end = (key_full * to_end).astype(bf16)
        scores = score_ref[head]
        dfresh = mm_tn(scores, dout_low) + mm(key_end, dstate_low)
        dright = mm_tn(inverse, dfresh)
        dright_low = dright.astype(bf16)
        dscores = jnp.where(upto, mm_nt(dout_low, fresh), 0.0).astype(bf16)
        dquery = mm_nt(dout_first, start) + mm(dscores, key)
        dstrict = jnp.where(below, -mm_nt(dright_low, fresh), 0.0)
        scaled = (dstrict * beta).astype(bf16)
        weighted = (dright * (beta * from_start)).astype(bf16)
        inner_key = mm(dstrict, key)
        start_key = from_start * mm_nt(dright_low, start)
        dkey = (
            mm_tn(dscores, query)
            + to_end * mm_nt(fresh, dstate_low)
            + beta * (inner_key - start_key)
            + mm_tn(scaled, key)
        )
        dbeta = jnp.sum(
            dright * value + (inner_key - start_key) * key_full, axis=1, keepdims=True
        )
        dvalue = beta * dright
        state_ref[head] = (
            carry * dstate + mm_tn(query, dout_first) - mm_tn(key, weighted)
        )
        dbeta_ref[:, head : head + 1] = dbeta * pad * beta_sig * (1.0 - beta_sig)
        dkey = dkey * pad
        dacts = (
            q_scale * (dquery - query_full * jnp.sum(query_full * dquery, axis=1, keepdims=True)),
            k_scale * (dkey - key_unit * jnp.sum(key_unit * dkey, axis=1, keepdims=True)),
            dvalue,
        )
        for part, target in enumerate((dq_ref, dk_ref, dv_ref)):
            sig = sigs[part]
            dsum = dacts[part] * (sig * (1.0 + sums[part] * (1.0 - sig)))
            back_ref[part, pl.ds(0, rows), lanes] = dsum
            taps = [conv_ref[part * CONV + j : part * CONV + j + 1, lanes] for j in range(CONV)]
            dpre = dsum * taps[0]
            dtaps = [jnp.sum(dsum * ext_ref[part, pl.ds(HALO, rows), lanes], axis=0, keepdims=True)]
            for shift in range(1, CONV):
                dpre = dpre + back_ref[part, pl.ds(shift, rows), lanes] * (after[shift - 1] * taps[shift])
                moved = ext_ref[part, pl.ds(HALO - shift, rows), lanes]
                dtaps.append(jnp.sum(dsum * moved * same[shift - 1], axis=0, keepdims=True))
            target[:, lanes] = dpre.astype(bf16)
            for j in range(CONV):
                spot = slice(part * CONV + j, part * CONV + j + 1)
                dconv_ref[spot, lanes] = dconv_ref[spot, lanes] + dtaps[j]
    dgain_ref[...] = dgain_ref[...] + dgain


def mixer_backward(me, ring, pres, beta_logit, table, doc_ids, conv, gain, saved, cot):
    length, width = pres[0].shape
    heads = width // HEAD_DIM
    rows = length // ring
    last = ring - 1

    def spot(i, m):
        return rotated(last - i, m[0], ring)

    def before(i, m):
        return rotated(jnp.maximum(last - i - 1, 0), m[0], ring)

    per = rows // HALO
    wide = pl.BlockSpec((rows, width), lambda i, m: (spot(i, m), 0))
    halo = pl.BlockSpec((HALO, width), lambda i, m: (before(i, m) * per + per - 1, 0))
    square = pl.BlockSpec((heads, rows, rows), lambda i, m: (0, spot(i, m), 0))
    narrow = pl.BlockSpec((rows, heads), lambda i, m: (spot(i, m), 0))
    flops = 10 * ring * heads * rows * HEAD_DIM * (rows * 9 + HEAD_DIM * 6)
    low = jax.ShapeDtypeStruct((length, width), bf16)
    return pl.pallas_call(
        functools.partial(backward_kernel, heads),
        grid_spec=pltpu.PrefetchScalarGridSpec(
            num_scalar_prefetch=1,
            grid=(ring,),
            in_specs=[
                wide, wide, wide, halo, halo, halo, narrow,
                pl.BlockSpec((rows, 16), lambda i, m: (last - i, 0)),
                pl.BlockSpec((rows, 1), lambda i, m: (last - i, 0)),
                pl.BlockSpec((1, rows), lambda i, m: (0, last - i)),
                pl.BlockSpec((3 * CONV, width), lambda i, m: (0, 0)),
                pl.BlockSpec((1, HEAD_DIM), lambda i, m: (0, 0)),
                wide, wide, square, square,
                pl.BlockSpec((1, heads, HEAD_DIM, HEAD_DIM), lambda i, m: (last - i, 0, 0, 0)),
                wide,
            ],
            out_specs=[
                wide, wide, wide, narrow,
                pl.BlockSpec((3 * CONV, width), lambda i, m: (0, 0)),
                pl.BlockSpec((1, HEAD_DIM), lambda i, m: (0, 0)),
            ],
            scratch_shapes=[
                pltpu.VMEM((3, rows + HALO, width), f32),
                pltpu.VMEM((3, rows + HALO, width), f32),
                pltpu.VMEM((heads, HEAD_DIM, HEAD_DIM), f32),
            ],
        ),
        out_shape=[
            low, low, low,
            jax.ShapeDtypeStruct((length, heads), f32),
            jax.ShapeDtypeStruct((3 * CONV, width), f32),
            jax.ShapeDtypeStruct((1, HEAD_DIM), f32),
        ],
        compiler_params=pltpu.CompilerParams(vmem_limit_bytes=40 * 1024 * 1024),
        cost_estimate=pl.CostEstimate(
            flops=flops, bytes_accessed=length * width * 34, transcendentals=length * width * 3
        ),
        name="mixer_backward",
    )(
        me, *pres, *pres, beta_logit, table,
        doc_ids.reshape(length, 1), doc_ids.reshape(1, length), conv, gain.reshape(1, HEAD_DIM),
        *saved, cot,
    )


def spread(place, order):
    mask = 0
    for i, bit in enumerate(order):
        mask = mask | (((place >> (len(order) - 1 - i)) & 1) << bit)
    return mask


def place_of(mask, order):
    place = 0
    for i, bit in enumerate(order):
        place = place | (((mask >> bit) & 1) << (len(order) - 1 - i))
    return place


def pieces_kernel(slots, shared, me_ref, *refs):
    count = 2 + 2 * shared
    lefts = [refs[i * slots : (i + 1) * slots] for i in range(count)]
    at = count * slots
    rights = [refs[at + i * slots : at + (i + 1) * slots] for i in range(2 + shared)]
    outs = refs[at + (2 + shared) * slots :]
    wide = lefts[0][0].shape[1]
    half = wide // 2

    def product(left, right, cols):
        total = None
        for l, r in zip(left, right):
            term = lax.dot_general(
                l[:, cols], r[...], (((0,), (0,)), ((), ())), preferred_element_type=f32
            )
            total = term if total is None else total + term
        return total.astype(bf16)

    for color in range(2):
        out = outs[color]
        out[0, pl.ds(0, wide), :] = product(lefts[color], rights[color], slice(0, wide))
        cols = slice(color * half, (color + 1) * half)
        for i in range(shared):
            spot = pl.ds(wide + i * half, half)
            out[0, spot, :] = product(lefts[2 + 2 * i + color], rights[2 + i], cols)


def grad_pieces(me, orders, first, units):
    slots = len(units[0][0])
    shared = len(units) - 2
    size = 2 ** len(orders[0])
    depth = units[0][0][0][0].shape[1]
    piece = depth // size
    rows = units[0][0][0][1][1]
    cols = units[0][1][0][0].shape[1]

    def left_spec(block, color):
        return pl.BlockSpec(
            (rows, piece), lambda i, m: (block, m[0] ^ spread(i + first, orders[color]))
        )

    def right_spec(block):
        return pl.BlockSpec((rows, cols), lambda i, m: (block, 0), pipeline_mode=pl.Buffered(1))

    arrays, specs = [], []
    for color in range(2):
        for array, (block, _) in units[color][0]:
            arrays.append(array)
            specs.append(left_spec(block, color))
    for unit in units[2:]:
        for color in range(2):
            for array, (block, _) in unit[0]:
                arrays.append(array)
                specs.append(left_spec(block, color))
    for unit in units:
        for array, (block, _) in unit[1]:
            arrays.append(array)
            specs.append(right_spec(block))
    high = piece + shared * (piece // 2)
    out = jax.ShapeDtypeStruct((size // 2, high, cols), bf16)
    flops = 2 * slots * rows * cols * high * size
    return pl.pallas_call(
        functools.partial(pieces_kernel, slots, shared),
        grid_spec=pltpu.PrefetchScalarGridSpec(
            num_scalar_prefetch=1,
            grid=(size // 2,),
            in_specs=specs,
            out_specs=[pl.BlockSpec((1, high, cols), lambda i, m: (i, 0, 0))] * 2,
        ),
        out_shape=[out, out],
        compiler_params=pltpu.CompilerParams(vmem_limit_bytes=40 * 1024 * 1024),
        cost_estimate=pl.CostEstimate(
            flops=flops, bytes_accessed=size * high * cols * 4, transcendentals=0
        ),
        name="grad_pieces",
    )(me, *arrays)


def assemble_kernel(order_core, turned, me_ref, own_a, own_b, got_a, got_b, stack_ref, turned_ref):
    step = pl.program_id(0)
    mine = (((step ^ me_ref[0]) >> order_core) & 1) == 0
    piece = turned_ref.shape[1]
    half = piece // 2
    count = stack_ref.shape[0]

    def pick(own, got, at, high):
        spot = pl.ds(at, high)
        return jnp.where(mine, own[0, spot, :], got[0, spot, :]).astype(f32)

    stack_ref[0] = pick(own_a, got_a, 0, piece)
    stack_ref[1] = pick(own_b, got_b, 0, piece)
    for i in range(count - 2 + 1):
        at = piece + i * half
        top = pick(own_a, got_a, at, half)
        low = pick(own_b, got_b, at, half)
        if i < count - 2:
            stack_ref[2 + i, pl.ds(0, half), :] = top
            stack_ref[2 + i, pl.ds(half, half), :] = low
        else:
            turned_ref[...] = jnp.concatenate([top, low], axis=0).T


def assemble(me, orders, own, got, count):
    places, high, cols = own[0].shape
    size = 2 * places
    piece = 2 * high // (count + 1)
    depth = size * piece

    def spec(color):
        return pl.BlockSpec(
            (1, high, cols), lambda a, m: (place_of(a ^ m[0], orders[color]) & (places - 1), 0, 0)
        )

    return pl.pallas_call(
        functools.partial(assemble_kernel, orders[0][0], True),
        grid_spec=pltpu.PrefetchScalarGridSpec(
            num_scalar_prefetch=1,
            grid=(size,),
            in_specs=[spec(0), spec(1), spec(0), spec(1)],
            out_specs=[
                pl.BlockSpec((count, piece, cols), lambda a, m: (0, a, 0)),
                pl.BlockSpec((cols, piece), lambda a, m: (0, a)),
            ],
        ),
        out_shape=[
            jax.ShapeDtypeStruct((count, depth, cols), f32),
            jax.ShapeDtypeStruct((cols, depth), f32),
        ],
        compiler_params=pltpu.CompilerParams(vmem_limit_bytes=40 * 1024 * 1024),
        cost_estimate=pl.CostEstimate(
            flops=0, bytes_accessed=size * high * cols * 20, transcendentals=0
        ),
        name="assemble",
    )(me, *own, *got)


def dot_f32(a, b):
    return jnp.dot(a, b, preferred_element_type=f32)


def dot_nt(a, b):
    return lax.dot_general(a, b, (((1,), (1,)), ((), ())), preferred_element_type=f32)


def dot_tn(a, b):
    return lax.dot_general(a, b, (((0,), (0,)), ((), ())), preferred_element_type=f32)


def rms_forward(rows, gain):
    scale = lax.rsqrt(jnp.mean(rows * rows, axis=-1, keepdims=True) + 1e-06)
    return (rows * scale * gain).astype(bf16), scale


def rms_backward(rows, scale, gain, grad):
    scaled = grad * gain
    mean = jnp.mean(scaled * rows, axis=-1, keepdims=True)
    gain_grad = jnp.sum(grad * rows * scale, axis=0)
    return scale * scaled - (scale * scale * scale) * rows * mean, gain_grad


def after(value, *others):
    return lax.optimization_barrier((value, *others))[0]


def bits_of(count):
    return [b for b in range(count.bit_length() - 1)]


def add_low(a, b):
    return (a.astype(f32) + b.astype(f32)).astype(bf16)


class Order:
    def __init__(self):
        self.last = []

    def wait(self, *values):
        flat, tree = jax.tree.flatten(values)
        held = lax.optimization_barrier((tuple(flat), tuple(self.last)))[0]
        out = jax.tree.unflatten(tree, held)
        return out if len(out) > 1 else out[0]

    def done(self, *values):
        self.last = jax.tree.leaves(values)
        return values if len(values) > 1 else values[0]


class Ring:
    def __init__(self, size):
        self.size = size
        self.me = lax.axis_index("heads")

    def back(self, value):
        return lax.ppermute(value, "heads", [(i, (i - 1) % self.size) for i in range(self.size)])

    def shift(self, value, by):
        return lax.ppermute(value, "heads", [(i, (i + by) % self.size) for i in range(self.size)])

    def small(self, vector):
        for bit in bits_of(self.size):
            moved = lax.ppermute(vector, "heads", [(i, i ^ (1 << bit)) for i in range(self.size)])
            vector = vector + moved
        return vector

    def gather(self, rows):
        slots = [rows]
        for _ in range(self.size - 1):
            slots.append(self.back(slots[-1]))
        return slots


def spots(arrays):
    return [(array, (0, array.shape[0])) for array in arrays]


def cuts(array, size):
    return [(array, (k, array.shape[0] // size)) for k in range(size)]


class Groups:
    def __init__(self, size):
        self.size = size
        self.bits = bits_of(size)
        self.me = lax.axis_index("dp")

    def swap(self, value, bit):
        return lax.ppermute(value, "dp", [(i, i ^ (1 << bit)) for i in range(self.size)])

    def orders(self):
        first, rest = self.bits[:1], self.bits[1:]
        return first + rest, first + rest[::-1]

    def swap_all(self, values, step):
        return [self.swap(value, self.orders()[color][step]) for color, value in enumerate(values)]

    def narrow(self, keeps, moved):
        half = keeps[0].shape[0] // 2
        if half:
            sends = [add_low(k[half:], m[half:]) for k, m in zip(keeps, moved)]
        else:
            sends, half = [], 1
        return sends, [add_low(k[:half], m[:half]) for k, m in zip(keeps, moved)]

    def widen(self, keeps, moved):
        return [jnp.concatenate([k, m]) for k, m in zip(keeps, moved)]

    def small(self, vector):
        for bit in self.bits:
            vector = vector + self.swap(vector, bit)
        return vector


class Reduction:
    def __init__(self, groups, order, units, count):
        self.groups, self.order, self.count = groups, order, count
        self.me = groups.me.astype(jnp.int32).reshape(1)
        self.units = units
        self.at = 0
        self.steps = len(groups.bits)

    def part(self, first):
        units = [(list(left), list(right)) for left, right in self.units]
        array, spot = units[0][1][0]
        units[0][1][0] = (self.order.wait(array), spot)
        return self.order.done(*grad_pieces(self.me, self.groups.orders(), first, units))

    def send(self):
        self.moved = self.groups.swap_all(self.part(self.groups.size // 2), 0)

    def keep(self):
        self.keeps = list(self.part(0))

    def left(self):
        return 2 * self.steps - 1 - self.at

    def advance(self):
        moved = self.order.wait(self.moved)
        if self.at < self.steps:
            sends, self.keeps = self.groups.narrow(self.keeps, moved)
            self.order.done(self.keeps)
            step = min(self.at + 1, self.steps - 1)
            self.moved = self.groups.swap_all(sends or self.keeps, step)
        else:
            self.keeps = self.groups.widen(self.keeps, moved)
            self.order.done(self.keeps)
            self.moved = self.groups.swap_all(self.keeps, 2 * self.steps - 2 - self.at)
        self.at += 1

    def finish(self):
        while self.left():
            self.advance()
        moved = self.order.wait(self.moved)
        return self.order.done(*assemble(self.me, self.groups.orders(), self.keeps, moved, self.count))


def shards(
    heads_size,
    dp_size,
    block_input,
    doc_ids,
    pad_mask,
    first_gain,
    qkv_weight,
    beta_weight,
    conv_weight,
    out_gain,
    out_weight,
    second_gain,
    gate_up_weight,
    down_weight,
    cotangent,
):
    ring = Ring(heads_size)
    groups = Groups(dp_size)
    order = Order()
    size = heads_size
    steps = len(groups.bits)
    local_rows, model_width = block_input.shape
    width = qkv_weight.shape[2]
    me = ring.me.astype(jnp.int32)
    me_one = me.reshape(1)
    pad_float = pad_mask.astype(f32)
    pad_rows = lax.dynamic_slice_in_dim(pad_float, me * local_rows, local_rows, 0)
    rows_float = block_input.astype(f32)
    first_float = first_gain.astype(f32)
    second_float = second_gain.astype(f32)
    conv_float = conv_weight.astype(f32).reshape(3 * CONV, width)
    gain_float = out_gain.astype(f32)

    share = out_weight.shape[0] // dp_size
    own_share = lax.dynamic_slice_in_dim(out_weight, groups.me * share, share, 0)
    shares = lax.all_gather(own_share, "heads", axis=0)
    halo_raw = ring.shift(block_input[local_rows - HALO :], 1)
    halo_rows, _ = rms_forward(halo_raw.astype(f32), first_float)
    xn_first, first_scale = rms_forward(rows_float, first_float)
    first_slots = ring.gather(after(xn_first, halo_rows))
    grad_rows = cotangent.astype(f32) * pad_rows[:, None]
    grad_low = grad_rows.astype(bf16)
    table = token_table(doc_ids, pad_float, local_rows)
    old = []
    for k in range(size):
        chunk = lax.rem(me + k, size).reshape(1)
        halo, halo_block = (halo_rows, 0) if k == 0 else (first_slots[k - 1], local_rows // HALO - 1)
        old = mixer_chunk(
            k, chunk, first_slots[k], halo, halo_block, qkv_weight, beta_weight, table, doc_ids,
            conv_float, old,
        )
        if k == 1:
            out_all_heads = lax.all_gather(after(shares, old[3]), "dp", axis=1, tiled=True)
        if k == size - 2:
            grad_all = lax.all_gather(after(grad_low, first_slots[-1], old[3]), "heads", axis=0)
    *pre_all, beta_all, query, key, value, score, inverse = old

    normed, out_all, fresh, starts = mixer_scan(
        me_one, size, query, key, value, score, inverse, beta_all, table, gain_float
    )
    saved = (out_all, fresh, score, inverse, starts)
    blocks = [normed[k * local_rows : (k + 1) * local_rows] for k in range(size)]
    moved = [ring.shift(blocks[k], k) for k in range(1, size)]
    mixed = dot_f32(blocks[0], out_weight)
    for k in range(1, size):
        source = lax.rem(me - k + size, size)
        weight = lax.dynamic_index_in_dim(out_all_heads, source, 0, keepdims=False)
        mixed = mixed + dot_f32(moved[k - 1], weight)
    hidden_one = rows_float + mixed
    xn_second, second_scale = rms_forward(hidden_one, second_float)

    second_slots = ring.gather(xn_second)
    grad_slots, hiddens, gates, ups = [], [], [], []
    total = moving_sum = None
    for k in range(size):
        source = lax.rem(me + k, size)
        if k > 2:
            total = add_low(back, moving_sum)
            moving_sum = ring.back(total)
            second_slots[k] = after(second_slots[k], total)
        if k:
            arrived = after(grad_all, second_slots[k])
            grad_slots.append(lax.dynamic_index_in_dim(arrived, source, 0, keepdims=False))
        else:
            grad_slots.append(grad_low)
        gate = dot_f32(second_slots[k], gate_up_weight[0])
        up = dot_f32(second_slots[k], gate_up_weight[1])
        grad_hidden = dot_nt(grad_slots[k], down_weight)
        sig = sigmoid(gate)
        swish = gate * sig
        hiddens.append((swish * up).astype(bf16))
        gates.append((grad_hidden * up * sig * (1.0 + gate * (1.0 - sig))).astype(bf16))
        ups.append((grad_hidden * swish).astype(bf16))
        back = dot_nt(gates[k], gate_up_weight[0]) + dot_nt(ups[k], gate_up_weight[1])
        if k == 0:
            own_back = back
        elif k == 1:
            moving_sum = ring.back(back.astype(bf16))
    total = add_low(back, moving_sum)
    moving_sum = ring.back(total)
    order.done(total)

    ffn_units = [
        (spots(second_slots), spots(gates)),
        (spots(second_slots), spots(ups)),
        (spots(grad_slots), spots(hiddens)),
    ]
    ffn = Reduction(groups, order, ffn_units, 2)
    ffn.send()
    ffn.keep()
    ffn.advance()
    grad_xn_second = own_back + order.wait(moving_sum).astype(f32)
    grad_part, second_gain_grad = rms_backward(hidden_one, second_scale, second_float, grad_xn_second)
    grad_h1 = grad_rows + grad_part
    mid_slots = [order.done(grad_h1.astype(bf16))]
    downs, normeds = [], []
    for k in range(size):
        if k + 1 < size:
            moving = ring.back(mid_slots[k])
        if k == 0:
            downs = [dot_f32(order.wait(hidden), down_weight) for hidden in hiddens]
            order.done(downs)
        if k + 2 == size:
            ffn.advance()
        normeds.append(order.done(dot_nt(order.wait(mid_slots[k]), out_weight).astype(bf16)))
        if k + 1 < size:
            mid_slots.append(order.wait(moving))
            order.done(mid_slots[-1])
    ffn.advance()
    down_moving = ring.back(order.wait(downs[1 % size].astype(bf16)))
    *grad_pres, grad_logit, conv_part, out_gain_part = mixer_backward(
        me_one, size, pre_all, beta_all, table, doc_ids, conv_float, gain_float, saved,
        order.wait(jnp.concatenate(normeds)),
    )
    grad_logit = order.done(grad_logit.astype(bf16), grad_pres[0])[0]
    down_total = order.done(add_low(downs[2 % size], order.wait(down_moving)))

    def first_partial(k):
        rows = slice(k * local_rows, (k + 1) * local_rows)
        total = dot_nt(order.wait(grad_logit[rows]), beta_weight)
        for i in range(3):
            total = total + dot_nt(order.wait(grad_pres[i][rows]), qkv_weight[i])
        return total

    def gain_share(k, share):
        return jnp.sum(share * first_slots[k].astype(f32), axis=0)

    partial = first_partial(1 % size)
    first_gain_part = gain_share(1 % size, partial)
    total = order.done(partial.astype(bf16))
    moving_sum = ring.back(total)
    ffn.advance()
    qkv = Reduction(
        groups,
        order,
        [
            (spots(first_slots), cuts(grad_pres[0], size)),
            (spots(first_slots), cuts(grad_pres[1], size)),
            (spots(first_slots), cuts(grad_pres[2], size)),
            (spots(mid_slots), cuts(normed, size)),
        ],
        3,
    )
    qkv.send()
    qkv.keep()
    qkv.advance()
    partial = order.done(first_partial(2 % size))
    for k in range(2, size):
        total = order.done(add_low(partial, order.wait(moving_sum)))
        moving_sum = ring.back(total)
        first_gain_part = first_gain_part + gain_share(k, partial)
        partial = order.done(first_partial((k + 1) % size))
        if k == 2:
            while ffn.left():
                ffn.advance()
    first_gain_part = (first_gain_part + gain_share(0, partial)) / first_float
    beta_part = 0.0
    late_logit = order.wait(grad_logit)
    for k in range(size):
        beta_part = beta_part + dot_tn(first_slots[k], late_logit[k * local_rows : (k + 1) * local_rows])
    tiny = (beta_part, conv_part, first_gain_part, second_gain_grad, out_gain_part)
    small = jnp.concatenate([v.reshape(-1) for v in tiny])
    count = beta_part.size
    gains_at = count + conv_part.size

    def hop(vector, bit):
        return order.done(vector + order.wait(groups.swap(vector, bit)))

    qkv.advance()
    small = hop(small, 0)
    grad_xn_first = partial + order.wait(moving_sum).astype(f32)
    grad_x_part, _ = rms_backward(rows_float, first_scale, first_float, grad_xn_first)
    input_grad = order.done(grad_h1 + grad_x_part)
    down_moving = ring.back(order.wait(down_total))
    qkv.advance()
    small = hop(small, 1)
    gate_up_grad, down_grad = ffn.finish()
    qkv.advance()
    for bit in groups.bits[2:]:
        small = hop(small, bit)
    for k in range(3, size):
        down_total = order.done(add_low(downs[k], order.wait(down_moving)))
        down_moving = ring.back(down_total)
    output = hidden_one + downs[0] + order.wait(down_moving).astype(f32)
    block_output = order.done(output.astype(bf16))
    while qkv.left():
        qkv.advance()
    beta_grad = small[:count].reshape(beta_part.shape)
    conv_grad = small[count:gains_at].reshape(3, CONV, width)
    gains = small[gains_at:]
    for bit in bits_of(size):
        moved = lax.ppermute(gains, "heads", [(i, i ^ (1 << bit)) for i in range(size)])
        gains = order.done(gains + order.wait(moved))
    qkv_grad, out_grad = qkv.finish()
    return (
        block_output,
        input_grad,
        gains[:model_width],
        qkv_grad,
        beta_grad,
        conv_grad,
        gains[2 * model_width :],
        out_grad,
        gains[model_width : 2 * model_width],
        gate_up_grad,
        down_grad,
    )


def solution(mesh):
    rows = P(("dp", "heads"), None)
    last = P(None, None, "heads")
    return jax.shard_map(
        functools.partial(shards, mesh.shape["heads"], mesh.shape["dp"]),
        mesh=mesh,
        in_specs=(
            rows, P("dp"), P("dp"), P(), last, P(None, "heads"), last, P(), P("heads", None), P(),
            last, P("heads", None), rows,
        ),
        out_specs=(
            rows, rows, P(), last, P(None, "heads"), last, P(), P("heads", None), P(), last,
            P("heads", None),
        ),
        check_vma=False,
    )
```

```python
import functools
import jax
import jax.numpy as jnp
from jax import lax
from jax.experimental import pallas as pl
from jax.experimental.pallas import tpu as pltpu
from jax.sharding import PartitionSpec as P

HEAD_DIM = 128
CONV = 4
HALO = 16
f32 = jnp.float32
bf16 = jnp.bfloat16


def mm(a, b):
    return jnp.dot(a.astype(bf16), b.astype(bf16), preferred_element_type=f32)


def mm_nt(a, b):
    return lax.dot_general(
        a.astype(bf16), b.astype(bf16), (((1,), (1,)), ((), ())), preferred_element_type=f32
    )


def mm_tn(a, b):
    return lax.dot_general(
        a.astype(bf16), b.astype(bf16), (((0,), (0,)), ((), ())), preferred_element_type=f32
    )


def token_table(doc_ids, pad_float, tile):
    length = doc_ids.shape[0]
    minus = jnp.full((tile,), -1, jnp.int32)
    padded = jnp.concatenate([minus, doc_ids, minus])

    def same(shift):
        moved = lax.slice_in_dim(padded, tile - shift, tile - shift + length, axis=0)
        return (moved == doc_ids).astype(f32)

    tiles = doc_ids.reshape(length // tile, tile)
    ends = tiles[:, -1]
    before = jnp.concatenate([jnp.full((1,), -1, jnp.int32), ends[:-1]])
    from_start = (tiles == before[:, None]).astype(f32).reshape(length)
    to_end = (tiles == ends[:, None]).astype(f32).reshape(length)
    columns = [same(1), same(2), same(3), pad_float, from_start, to_end, same(-1), same(-2), same(-3)]
    columns += [jnp.zeros((length,), f32)] * (16 - len(columns))
    return jnp.stack(columns, axis=1)


def sigmoid(x):
    return 1.0 / (1.0 + jnp.exp(-x))


def block_inverse(strict, apart):
    size = strict.shape[0]
    zero = jnp.zeros_like(strict)
    inverse = jnp.where(apart == 0, 1.0, jnp.where(apart == 1, -strict, zero))
    low = strict.astype(bf16)
    low_zero = jnp.zeros_like(low)
    step = 2
    while step < size:
        part = jnp.where((apart >= step) & (apart < 2 * step), low, low_zero)
        held = inverse.astype(bf16)
        inverse = inverse - mm(held, mm(part, held))
        step *= 2
    return inverse


def unit_inverse(strict):
    size = strict.shape[0]
    half = min(size, 128)
    row = lax.broadcasted_iota(jnp.int32, (half, half), 0)
    col = lax.broadcasted_iota(jnp.int32, (half, half), 1)
    apart = row ^ col
    if size == half:
        return block_inverse(strict, apart)
    top = strict[:half, :half]
    bottom = strict[half:, half:]
    top = block_inverse(top, apart)
    bottom = block_inverse(bottom, apart)
    cross = -mm(bottom, mm(strict[half:, :half], top))
    return jnp.concatenate(
        [jnp.concatenate([top, jnp.zeros_like(top)], axis=1), jnp.concatenate([cross, bottom], axis=1)],
        axis=0,
    )


def conv_sum(ext_ref, part, rows, lanes, taps, same):
    total = ext_ref[part, pl.ds(HALO, rows), lanes] * taps[0]
    for shift in range(1, CONV):
        total = total + ext_ref[part, pl.ds(HALO - shift, rows), lanes] * taps[shift] * same[shift - 1]
    return total


def rotated(tile, me, ring):
    return lax.rem(tile - me + ring, ring)


def chunk_kernel(
    heads, old, where_ref, x_ref, x_halo_ref, weight_ref, beta_weight_ref,
    table_ref, doc_col_ref, doc_row_ref, conv_ref, *rest,
):
    outs = rest[old:]
    (q_pre_ref, k_pre_ref, v_pre_ref, beta_out_ref,
     query_ref, key_ref, value_ref, score_ref, inv_ref, x_ext_ref, ext_ref) = outs
    group = pl.program_id(0)
    rows = x_ref.shape[0]

    @pl.when(group == 0)
    def _():
        x_ext_ref[pl.ds(0, HALO), :] = x_halo_ref[...]
        x_ext_ref[pl.ds(HALO, rows), :] = x_ref[...]
        beta_out_ref[...] = jnp.dot(x_ref[...], beta_weight_ref[...], preferred_element_type=f32)

    for part, copy in enumerate((q_pre_ref, k_pre_ref, v_pre_ref)):
        pre = jnp.dot(x_ext_ref[...], weight_ref[part], preferred_element_type=f32)
        ext_ref[part] = pre
        copy[...] = pre[HALO:]
    wide = (rows, HEAD_DIM)
    same = [jnp.broadcast_to(table_ref[:, j : j + 1], wide) for j in range(3)]
    pad = table_ref[:, 3:4]
    row = lax.broadcasted_iota(jnp.int32, (rows, rows), 0)
    col = lax.broadcasted_iota(jnp.int32, (rows, rows), 1)
    together = doc_col_ref[...] == doc_row_ref[...]
    below = together & (row > col)
    upto = together & (row >= col)
    betas = sigmoid(beta_out_ref[...]) * pad
    lane = lax.broadcasted_iota(jnp.int32, betas.shape, 1)
    for head in range(heads):
        lanes = pl.ds(head * HEAD_DIM, HEAD_DIM)
        acts = []
        for part in range(3):
            taps = [conv_ref[part * CONV + j : part * CONV + j + 1, lanes] for j in range(CONV)]
            total = conv_sum(ext_ref, part, rows, lanes, taps, same)
            acts.append(total * sigmoid(total))
        query = acts[0] * lax.rsqrt(jnp.sum(acts[0] * acts[0], axis=1, keepdims=True) + 1e-06)
        key = acts[1] * (lax.rsqrt(jnp.sum(acts[1] * acts[1], axis=1, keepdims=True) + 1e-06) * pad)
        beta = jnp.sum(jnp.where(lane == group * heads + head, betas, 0.0), axis=1, keepdims=True)
        key = key.astype(bf16)
        query = query.astype(bf16)
        query_ref[:, lanes] = query
        key_ref[:, lanes] = key
        value_ref[:, lanes] = acts[2].astype(bf16)
        strict = jnp.where(below, mm_nt(key, key) * beta, 0.0)
        inv_ref[head] = unit_inverse(strict).astype(bf16)
        score_ref[head] = jnp.where(upto, mm_nt(query, key), 0.0).astype(bf16)


def mixer_chunk(slot, chunk, rows_in, halo, halo_block, weight, beta_weight, table, doc_ids, conv, old):
    rows, depth = rows_in.shape
    width = weight.shape[2]
    heads = width // HEAD_DIM
    length = doc_ids.shape[0]
    per = 2 if heads % 2 == 0 else 1
    lane = per * HEAD_DIM
    out_wide = pl.BlockSpec((rows, lane), lambda g, c: (slot, g))
    out_square = pl.BlockSpec((per, rows, rows), lambda g, c: (g, slot, 0))
    whole = jax.ShapeDtypeStruct((length, width), f32)
    low = jax.ShapeDtypeStruct((length, width), bf16)
    square = jax.ShapeDtypeStruct((heads, length, rows), bf16)
    flops = 16 * heads * rows * (rows * (rows * 8 + HEAD_DIM * 2) + 3 * depth * HEAD_DIM)
    return pl.pallas_call(
        functools.partial(chunk_kernel, per, len(old)),
        grid_spec=pltpu.PrefetchScalarGridSpec(
            num_scalar_prefetch=1,
            grid=(heads // per,),
            in_specs=[
                pl.BlockSpec((rows, depth), lambda g, c: (0, 0)),
                pl.BlockSpec((HALO, depth), lambda g, c: (halo_block, 0)),
                pl.BlockSpec((3, depth, lane), lambda g, c: (0, 0, g)),
                pl.BlockSpec((depth, heads), lambda g, c: (0, 0)),
                pl.BlockSpec((rows, 16), lambda g, c: (c[0], 0)),
                pl.BlockSpec((rows, 1), lambda g, c: (c[0], 0)),
                pl.BlockSpec((1, rows), lambda g, c: (0, c[0])),
                pl.BlockSpec((3 * CONV, lane), lambda g, c: (0, g)),
            ] + [pl.BlockSpec(memory_space=pl.ANY)] * len(old),
            out_specs=[
                out_wide, out_wide, out_wide,
                pl.BlockSpec((rows, heads), lambda g, c: (slot, 0)),
                out_wide, out_wide, out_wide, out_square, out_square,
            ],
            scratch_shapes=[
                pltpu.VMEM((rows + HALO, depth), bf16),
                pltpu.VMEM((3, rows + HALO, lane), f32),
            ],
        ),
        out_shape=[
            whole, whole, whole, jax.ShapeDtypeStruct((length, heads), f32),
            low, low, low, square, square,
        ],
        input_output_aliases={9 + i: i for i in range(len(old))},
        compiler_params=pltpu.CompilerParams(vmem_limit_bytes=60 * 1024 * 1024),
        cost_estimate=pl.CostEstimate(
            flops=flops, bytes_accessed=rows * width * 60, transcendentals=rows * width * 4
        ),
        name="mixer_chunk",
    )(
        chunk, rows_in, halo, weight, beta_weight, table,
        doc_ids.reshape(length, 1), doc_ids.reshape(1, length), conv, *old,
    )


def scan_kernel(
    heads, me_ref, query_ref, key_ref, value_ref, score_ref, inv_ref, beta_ref, table_ref, gain_ref,
    normed_ref, out_ref, fresh_ref, start_ref, state_ref,
):
    tile = pl.program_id(0)
    factor = HEAD_DIM ** (-0.5)
    rows = query_ref.shape[0]

    @pl.when(tile == 0)
    def _():
        state_ref[...] = jnp.zeros_like(state_ref)

    wide = (rows, HEAD_DIM)
    pad = table_ref[:, 3:4]
    from_start = jnp.broadcast_to(table_ref[:, 4:5], wide)
    to_end = jnp.broadcast_to(table_ref[:, 5:6], wide)
    carry = table_ref[rows - 1 : rows, 4:5]
    gain = gain_ref[...]
    for head in range(heads):
        lanes = pl.ds(head * HEAD_DIM, HEAD_DIM)
        beta = sigmoid(beta_ref[:, head : head + 1]) * pad
        query = query_ref[:, lanes]
        key = key_ref[:, lanes]
        state = state_ref[head]
        low_state = state.astype(bf16)
        start_ref[0, head] = low_state
        right = beta * (value_ref[:, lanes].astype(f32) - from_start * mm(key, low_state))
        fresh = mm(inv_ref[head], right).astype(bf16)
        fresh_ref[:, lanes] = fresh
        state_ref[head] = carry * state + mm_tn(key.astype(f32) * to_end, fresh)
        out = factor * (from_start * mm(query, low_state) + mm(score_ref[head], fresh))
        out_ref[:, lanes] = out
        scale = lax.rsqrt(jnp.mean(out * out, axis=1, keepdims=True) + 1e-05)
        normed_ref[:, lanes] = (out * scale * gain).astype(bf16)


def mixer_scan(me, ring, query, key, value, score, inverse, beta_logit, table, gain):
    length, width = query.shape
    heads = width // HEAD_DIM
    rows = length // ring
    wide = pl.BlockSpec((rows, width), lambda i, m: (rotated(i, m[0], ring), 0))
    square = pl.BlockSpec((heads, rows, rows), lambda i, m: (0, rotated(i, m[0], ring), 0))
    flops = 9 * ring * heads * rows * HEAD_DIM * (rows * 2 + HEAD_DIM * 3)
    return pl.pallas_call(
        functools.partial(scan_kernel, heads),
        grid_spec=pltpu.PrefetchScalarGridSpec(
            num_scalar_prefetch=1,
            grid=(ring,),
            in_specs=[
                wide, wide, wide, square, square,
                pl.BlockSpec((rows, heads), lambda i, m: (rotated(i, m[0], ring), 0)),
                pl.BlockSpec((rows, 16), lambda i, m: (i, 0)),
                pl.BlockSpec((1, HEAD_DIM), lambda i, m: (0, 0)),
            ],
            out_specs=[
                wide, wide, wide,
                pl.BlockSpec((1, heads, HEAD_DIM, HEAD_DIM), lambda i, m: (i, 0, 0, 0)),
            ],
            scratch_shapes=[pltpu.VMEM((heads, HEAD_DIM, HEAD_DIM), f32)],
        ),
        out_shape=[
            jax.ShapeDtypeStruct((length, width), bf16),
            jax.ShapeDtypeStruct((length, width), f32),
            jax.ShapeDtypeStruct((length, width), bf16),
            jax.ShapeDtypeStruct((ring, heads, HEAD_DIM, HEAD_DIM), bf16),
        ],
        compiler_params=pltpu.CompilerParams(vmem_limit_bytes=40 * 1024 * 1024),
        cost_estimate=pl.CostEstimate(
            flops=flops, bytes_accessed=length * width * 18, transcendentals=length * heads
        ),
        name="mixer_scan",
    )(me, query, key, value, score, inverse, beta_logit, table, gain.reshape(1, HEAD_DIM))


def backward_kernel(
    heads, me_ref, q_ref, k_ref, v_ref, q_halo_ref, k_halo_ref, v_halo_ref,
    beta_ref, table_ref, doc_col_ref, doc_row_ref, conv_ref, gain_ref,
    out_ref, fresh_ref, score_ref, inv_ref, start_ref, cot_ref,
    dq_ref, dk_ref, dv_ref, dbeta_ref, dconv_ref, dgain_ref, ext_ref, back_ref, state_ref,
):
    step = pl.program_id(0)
    factor = HEAD_DIM ** (-0.5)
    rows, width = q_ref.shape

    @pl.when(step == 0)
    def _():
        state_ref[...] = jnp.zeros_like(state_ref)
        back_ref[:, pl.ds(rows, HALO), :] = jnp.zeros((3, HALO, width), f32)
        dconv_ref[...] = jnp.zeros_like(dconv_ref)
        dgain_ref[...] = jnp.zeros_like(dgain_ref)

    @pl.when(step > 0)
    def _():
        back_ref[:, pl.ds(rows, HALO), :] = back_ref[:, pl.ds(0, HALO), :]

    for part, (ref, halo) in enumerate(
        ((q_ref, q_halo_ref), (k_ref, k_halo_ref), (v_ref, v_halo_ref))
    ):
        ext_ref[part, pl.ds(0, HALO), :] = halo[...].astype(f32)
        ext_ref[part, pl.ds(HALO, rows), :] = ref[...].astype(f32)
    wide = (rows, HEAD_DIM)
    same = [jnp.broadcast_to(table_ref[:, j : j + 1], wide) for j in range(3)]
    after = [jnp.broadcast_to(table_ref[:, 6 + j : 7 + j], wide) for j in range(3)]
    pad = table_ref[:, 3:4]
    from_start = jnp.broadcast_to(table_ref[:, 4:5], wide)
    to_end = jnp.broadcast_to(table_ref[:, 5:6], wide)
    carry = table_ref[rows - 1 : rows, 4:5]
    row = lax.broadcasted_iota(jnp.int32, (rows, rows), 0)
    col = lax.broadcasted_iota(jnp.int32, (rows, rows), 1)
    together = doc_col_ref[...] == doc_row_ref[...]
    below = together & (row > col)
    upto = together & (row >= col)
    gain = gain_ref[...]
    dgain = jnp.zeros((1, HEAD_DIM), f32)
    for head in range(heads):
        lanes = pl.ds(head * HEAD_DIM, HEAD_DIM)
        sums, sigs, acts = [], [], []
        for part in range(3):
            taps = [conv_ref[part * CONV + j : part * CONV + j + 1, lanes] for j in range(CONV)]
            total = conv_sum(ext_ref, part, rows, lanes, taps, same)
            sig = sigmoid(total)
            sums.append(total)
            sigs.append(sig)
            acts.append(total * sig)
        q_scale = lax.rsqrt(jnp.sum(acts[0] * acts[0], axis=1, keepdims=True) + 1e-06)
        k_scale = lax.rsqrt(jnp.sum(acts[1] * acts[1], axis=1, keepdims=True) + 1e-06)
        query_full = acts[0] * q_scale
        key_unit = acts[1] * k_scale
        beta_sig = sigmoid(beta_ref[:, head : head + 1])
        beta = beta_sig * pad
        key_full = key_unit * pad
        key = key_full.astype(bf16)
        query = query_full.astype(bf16)
        value = acts[2]
        out = out_ref[:, lanes]
        cot = cot_ref[:, lanes].astype(f32)
        scale = lax.rsqrt(jnp.mean(out * out, axis=1, keepdims=True) + 1e-05)
        unit = out * scale
        dgain = dgain + jnp.sum(cot * unit, axis=0, keepdims=True)
        gained = cot * gain
        dout = (factor * scale) * (gained - unit * jnp.mean(unit * gained, axis=1, keepdims=True))
        dout_low = dout.astype(bf16)
        dout_first = (dout * from_start).astype(bf16)
        fresh = fresh_ref[:, lanes]
        start = start_ref[0, head]
        dstate = state_ref[head]
        dstate_low = dstate.astype(bf16)
        inverse = inv_ref[head]
        key_end = (key_full * to_end).astype(bf16)
        scores = score_ref[head]
        dfresh = mm_tn(scores, dout_low) + mm(key_end, dstate_low)
        dright = mm_tn(inverse, dfresh)
        dright_low = dright.astype(bf16)
        dscores = jnp.where(upto, mm_nt(dout_low, fresh), 0.0).astype(bf16)
        dquery = mm_nt(dout_first, start) + mm(dscores, key)
        dstrict = jnp.where(below, -mm_nt(dright_low, fresh), 0.0)
        scaled = (dstrict * beta).astype(bf16)
        weighted = (dright * (beta * from_start)).astype(bf16)
        inner_key = mm(dstrict, key)
        start_key = from_start * mm_nt(dright_low, start)
        dkey = (
            mm_tn(dscores, query)
            + to_end * mm_nt(fresh, dstate_low)
            + beta * (inner_key - start_key)
            + mm_tn(scaled, key)
        )
        dbeta = jnp.sum(
            dright * value + (inner_key - start_key) * key_full, axis=1, keepdims=True
        )
        dvalue = beta * dright
        state_ref[head] = (
            carry * dstate + mm_tn(query, dout_first) - mm_tn(key, weighted)
        )
        dbeta_ref[:, head : head + 1] = dbeta * pad * beta_sig * (1.0 - beta_sig)
        dkey = dkey * pad
        dacts = (
            q_scale * (dquery - query_full * jnp.sum(query_full * dquery, axis=1, keepdims=True)),
            k_scale * (dkey - key_unit * jnp.sum(key_unit * dkey, axis=1, keepdims=True)),
            dvalue,
        )
        for part, target in enumerate((dq_ref, dk_ref, dv_ref)):
            sig = sigs[part]
            dsum = dacts[part] * (sig * (1.0 + sums[part] * (1.0 - sig)))
            back_ref[part, pl.ds(0, rows), lanes] = dsum
            taps = [conv_ref[part * CONV + j : part * CONV + j + 1, lanes] for j in range(CONV)]
            dpre = dsum * taps[0]
            dtaps = [jnp.sum(dsum * ext_ref[part, pl.ds(HALO, rows), lanes], axis=0, keepdims=True)]
            for shift in range(1, CONV):
                dpre = dpre + back_ref[part, pl.ds(shift, rows), lanes] * (after[shift - 1] * taps[shift])
                moved = ext_ref[part, pl.ds(HALO - shift, rows), lanes]
                dtaps.append(jnp.sum(dsum * moved * same[shift - 1], axis=0, keepdims=True))
            target[:, lanes] = dpre.astype(bf16)
            for j in range(CONV):
                spot = slice(part * CONV + j, part * CONV + j + 1)
                dconv_ref[spot, lanes] = dconv_ref[spot, lanes] + dtaps[j]
    dgain_ref[...] = dgain_ref[...] + dgain


def mixer_backward(me, ring, pres, beta_logit, table, doc_ids, conv, gain, saved, cot):
    length, width = pres[0].shape
    heads = width // HEAD_DIM
    rows = length // ring
    last = ring - 1

    def spot(i, m):
        return rotated(last - i, m[0], ring)

    def before(i, m):
        return rotated(jnp.maximum(last - i - 1, 0), m[0], ring)

    per = rows // HALO
    wide = pl.BlockSpec((rows, width), lambda i, m: (spot(i, m), 0))
    halo = pl.BlockSpec((HALO, width), lambda i, m: (before(i, m) * per + per - 1, 0))
    square = pl.BlockSpec((heads, rows, rows), lambda i, m: (0, spot(i, m), 0))
    narrow = pl.BlockSpec((rows, heads), lambda i, m: (spot(i, m), 0))
    flops = 10 * ring * heads * rows * HEAD_DIM * (rows * 9 + HEAD_DIM * 6)
    low = jax.ShapeDtypeStruct((length, width), bf16)
    return pl.pallas_call(
        functools.partial(backward_kernel, heads),
        grid_spec=pltpu.PrefetchScalarGridSpec(
            num_scalar_prefetch=1,
            grid=(ring,),
            in_specs=[
                wide, wide, wide, halo, halo, halo, narrow,
                pl.BlockSpec((rows, 16), lambda i, m: (last - i, 0)),
                pl.BlockSpec((rows, 1), lambda i, m: (last - i, 0)),
                pl.BlockSpec((1, rows), lambda i, m: (0, last - i)),
                pl.BlockSpec((3 * CONV, width), lambda i, m: (0, 0)),
                pl.BlockSpec((1, HEAD_DIM), lambda i, m: (0, 0)),
                wide, wide, square, square,
                pl.BlockSpec((1, heads, HEAD_DIM, HEAD_DIM), lambda i, m: (last - i, 0, 0, 0)),
                wide,
            ],
            out_specs=[
                wide, wide, wide, narrow,
                pl.BlockSpec((3 * CONV, width), lambda i, m: (0, 0)),
                pl.BlockSpec((1, HEAD_DIM), lambda i, m: (0, 0)),
            ],
            scratch_shapes=[
                pltpu.VMEM((3, rows + HALO, width), f32),
                pltpu.VMEM((3, rows + HALO, width), f32),
                pltpu.VMEM((heads, HEAD_DIM, HEAD_DIM), f32),
            ],
        ),
        out_shape=[
            low, low, low,
            jax.ShapeDtypeStruct((length, heads), f32),
            jax.ShapeDtypeStruct((3 * CONV, width), f32),
            jax.ShapeDtypeStruct((1, HEAD_DIM), f32),
        ],
        compiler_params=pltpu.CompilerParams(vmem_limit_bytes=40 * 1024 * 1024),
        cost_estimate=pl.CostEstimate(
            flops=flops, bytes_accessed=length * width * 34, transcendentals=length * width * 3
        ),
        name="mixer_backward",
    )(
        me, *pres, *pres, beta_logit, table,
        doc_ids.reshape(length, 1), doc_ids.reshape(1, length), conv, gain.reshape(1, HEAD_DIM),
        *saved, cot,
    )


def spread(place, order):
    mask = 0
    for i, bit in enumerate(order):
        mask = mask | (((place >> (len(order) - 1 - i)) & 1) << bit)
    return mask


def place_of(mask, order):
    place = 0
    for i, bit in enumerate(order):
        place = place | (((mask >> bit) & 1) << (len(order) - 1 - i))
    return place


def pieces_kernel(slots, shared, me_ref, *refs):
    count = 2 + 2 * shared
    lefts = [refs[i * slots : (i + 1) * slots] for i in range(count)]
    at = count * slots
    rights = [refs[at + i * slots : at + (i + 1) * slots] for i in range(2 + shared)]
    outs = refs[at + (2 + shared) * slots :]
    wide = lefts[0][0].shape[1]
    half = wide // 2

    def product(left, right, cols):
        total = None
        for l, r in zip(left, right):
            term = lax.dot_general(
                l[:, cols], r[...], (((0,), (0,)), ((), ())), preferred_element_type=f32
            )
            total = term if total is None else total + term
        return total.astype(bf16)

    for color in range(2):
        out = outs[color]
        out[0, pl.ds(0, wide), :] = product(lefts[color], rights[color], slice(0, wide))
        cols = slice(color * half, (color + 1) * half)
        for i in range(shared):
            spot = pl.ds(wide + i * half, half)
            out[0, spot, :] = product(lefts[2 + 2 * i + color], rights[2 + i], cols)


def grad_pieces(me, orders, first, units):
    slots = len(units[0][0])
    shared = len(units) - 2
    size = 2 ** len(orders[0])
    depth = units[0][0][0][0].shape[1]
    piece = depth // size
    rows = units[0][0][0][1][1]
    cols = units[0][1][0][0].shape[1]

    def left_spec(block, color):
        return pl.BlockSpec(
            (rows, piece), lambda i, m: (block, m[0] ^ spread(i + first, orders[color]))
        )

    def right_spec(block):
        return pl.BlockSpec((rows, cols), lambda i, m: (block, 0), pipeline_mode=pl.Buffered(1))

    arrays, specs = [], []
    for color in range(2):
        for array, (block, _) in units[color][0]:
            arrays.append(array)
            specs.append(left_spec(block, color))
    for unit in units[2:]:
        for color in range(2):
            for array, (block, _) in unit[0]:
                arrays.append(array)
                specs.append(left_spec(block, color))
    for unit in units:
        for array, (block, _) in unit[1]:
            arrays.append(array)
            specs.append(right_spec(block))
    high = piece + shared * (piece // 2)
    out = jax.ShapeDtypeStruct((size // 2, high, cols), bf16)
    flops = 2 * slots * rows * cols * high * size
    return pl.pallas_call(
        functools.partial(pieces_kernel, slots, shared),
        grid_spec=pltpu.PrefetchScalarGridSpec(
            num_scalar_prefetch=1,
            grid=(size // 2,),
            in_specs=specs,
            out_specs=[pl.BlockSpec((1, high, cols), lambda i, m: (i, 0, 0))] * 2,
        ),
        out_shape=[out, out],
        compiler_params=pltpu.CompilerParams(vmem_limit_bytes=40 * 1024 * 1024),
        cost_estimate=pl.CostEstimate(
            flops=flops, bytes_accessed=size * high * cols * 4, transcendentals=0
        ),
        name="grad_pieces",
    )(me, *arrays)


def assemble_kernel(order_core, turned, me_ref, own_a, own_b, got_a, got_b, stack_ref, turned_ref):
    step = pl.program_id(0)
    mine = (((step ^ me_ref[0]) >> order_core) & 1) == 0
    piece = turned_ref.shape[1]
    half = piece // 2
    count = stack_ref.shape[0]

    def pick(own, got, at, high):
        spot = pl.ds(at, high)
        return jnp.where(mine, own[0, spot, :], got[0, spot, :]).astype(f32)

    stack_ref[0] = pick(own_a, got_a, 0, piece)
    stack_ref[1] = pick(own_b, got_b, 0, piece)
    for i in range(count - 2 + 1):
        at = piece + i * half
        top = pick(own_a, got_a, at, half)
        low = pick(own_b, got_b, at, half)
        if i < count - 2:
            stack_ref[2 + i, pl.ds(0, half), :] = top
            stack_ref[2 + i, pl.ds(half, half), :] = low
        else:
            turned_ref[...] = jnp.concatenate([top, low], axis=0).T


def assemble(me, orders, own, got, count):
    places, high, cols = own[0].shape
    size = 2 * places
    piece = 2 * high // (count + 1)
    depth = size * piece

    def spec(color):
        return pl.BlockSpec(
            (1, high, cols), lambda a, m: (place_of(a ^ m[0], orders[color]) & (places - 1), 0, 0)
        )

    return pl.pallas_call(
        functools.partial(assemble_kernel, orders[0][0], True),
        grid_spec=pltpu.PrefetchScalarGridSpec(
            num_scalar_prefetch=1,
            grid=(size,),
            in_specs=[spec(0), spec(1), spec(0), spec(1)],
            out_specs=[
                pl.BlockSpec((count, piece, cols), lambda a, m: (0, a, 0)),
                pl.BlockSpec((cols, piece), lambda a, m: (0, a)),
            ],
        ),
        out_shape=[
            jax.ShapeDtypeStruct((count, depth, cols), f32),
            jax.ShapeDtypeStruct((cols, depth), f32),
        ],
        compiler_params=pltpu.CompilerParams(vmem_limit_bytes=40 * 1024 * 1024),
        cost_estimate=pl.CostEstimate(
            flops=0, bytes_accessed=size * high * cols * 20, transcendentals=0
        ),
        name="assemble",
    )(me, *own, *got)


def dot_f32(a, b):
    return jnp.dot(a, b, preferred_element_type=f32)


def dot_nt(a, b):
    return lax.dot_general(a, b, (((1,), (1,)), ((), ())), preferred_element_type=f32)


def dot_tn(a, b):
    return lax.dot_general(a, b, (((0,), (0,)), ((), ())), preferred_element_type=f32)


def rms_forward(rows, gain):
    scale = lax.rsqrt(jnp.mean(rows * rows, axis=-1, keepdims=True) + 1e-06)
    return (rows * scale * gain).astype(bf16), scale


def rms_backward(rows, scale, gain, grad):
    scaled = grad * gain
    mean = jnp.mean(scaled * rows, axis=-1, keepdims=True)
    gain_grad = jnp.sum(grad * rows * scale, axis=0)
    return scale * scaled - (scale * scale * scale) * rows * mean, gain_grad


def after(value, *others):
    return lax.optimization_barrier((value, *others))[0]


def bits_of(count):
    return [b for b in range(count.bit_length() - 1)]


def add_low(a, b):
    return (a.astype(f32) + b.astype(f32)).astype(bf16)


class Order:
    def __init__(self):
        self.last = []

    def wait(self, *values):
        flat, tree = jax.tree.flatten(values)
        held = lax.optimization_barrier((tuple(flat), tuple(self.last)))[0]
        out = jax.tree.unflatten(tree, held)
        return out if len(out) > 1 else out[0]

    def done(self, *values):
        self.last = jax.tree.leaves(values)
        return values if len(values) > 1 else values[0]


class Ring:
    def __init__(self, size):
        self.size = size
        self.me = lax.axis_index("heads")

    def back(self, value):
        return lax.ppermute(value, "heads", [(i, (i - 1) % self.size) for i in range(self.size)])

    def shift(self, value, by):
        return lax.ppermute(value, "heads", [(i, (i + by) % self.size) for i in range(self.size)])

    def small(self, vector):
        for bit in bits_of(self.size):
            moved = lax.ppermute(vector, "heads", [(i, i ^ (1 << bit)) for i in range(self.size)])
            vector = vector + moved
        return vector

    def gather(self, rows):
        slots = [rows]
        for _ in range(self.size - 1):
            slots.append(self.back(slots[-1]))
        return slots


def spots(arrays):
    return [(array, (0, array.shape[0])) for array in arrays]


def cuts(array, size):
    return [(array, (k, array.shape[0] // size)) for k in range(size)]


class Groups:
    def __init__(self, size):
        self.size = size
        self.bits = bits_of(size)
        self.me = lax.axis_index("dp")

    def swap(self, value, bit):
        return lax.ppermute(value, "dp", [(i, i ^ (1 << bit)) for i in range(self.size)])

    def orders(self):
        first, rest = self.bits[:1], self.bits[1:]
        return first + rest, first + rest[::-1]

    def swap_all(self, values, step):
        return [self.swap(value, self.orders()[color][step]) for color, value in enumerate(values)]

    def narrow(self, keeps, moved):
        half = keeps[0].shape[0] // 2
        if half:
            sends = [add_low(k[half:], m[half:]) for k, m in zip(keeps, moved)]
        else:
            sends, half = [], 1
        return sends, [add_low(k[:half], m[:half]) for k, m in zip(keeps, moved)]

    def widen(self, keeps, moved):
        return [jnp.concatenate([k, m]) for k, m in zip(keeps, moved)]

    def small(self, vector):
        for bit in self.bits:
            vector = vector + self.swap(vector, bit)
        return vector


class Reduction:
    def __init__(self, groups, order, units, count):
        self.groups, self.order, self.count = groups, order, count
        self.me = groups.me.astype(jnp.int32).reshape(1)
        self.units = units
        self.at = 0
        self.steps = len(groups.bits)

    def part(self, first):
        units = [(list(left), list(right)) for left, right in self.units]
        array, spot = units[0][1][0]
        units[0][1][0] = (self.order.wait(array), spot)
        return self.order.done(*grad_pieces(self.me, self.groups.orders(), first, units))

    def send(self):
        self.moved = self.groups.swap_all(self.part(self.groups.size // 2), 0)

    def keep(self):
        self.keeps = list(self.part(0))

    def left(self):
        return 2 * self.steps - 1 - self.at

    def advance(self):
        moved = self.order.wait(self.moved)
        if self.at < self.steps:
            sends, self.keeps = self.groups.narrow(self.keeps, moved)
            self.order.done(self.keeps)
            step = min(self.at + 1, self.steps - 1)
            self.moved = self.groups.swap_all(sends or self.keeps, step)
        else:
            self.keeps = self.groups.widen(self.keeps, moved)
            self.order.done(self.keeps)
            self.moved = self.groups.swap_all(self.keeps, 2 * self.steps - 2 - self.at)
        self.at += 1

    def finish(self):
        while self.left():
            self.advance()
        moved = self.order.wait(self.moved)
        return self.order.done(*assemble(self.me, self.groups.orders(), self.keeps, moved, self.count))


def shards(
    heads_size,
    dp_size,
    block_input,
    doc_ids,
    pad_mask,
    first_gain,
    qkv_weight,
    beta_weight,
    conv_weight,
    out_gain,
    out_weight,
    second_gain,
    gate_up_weight,
    down_weight,
    cotangent,
):
    ring = Ring(heads_size)
    groups = Groups(dp_size)
    order = Order()
    size = heads_size
    steps = len(groups.bits)
    local_rows, model_width = block_input.shape
    width = qkv_weight.shape[2]
    me = ring.me.astype(jnp.int32)
    me_one = me.reshape(1)
    pad_float = pad_mask.astype(f32)
    pad_rows = lax.dynamic_slice_in_dim(pad_float, me * local_rows, local_rows, 0)
    rows_float = block_input.astype(f32)
    first_float = first_gain.astype(f32)
    second_float = second_gain.astype(f32)
    conv_float = conv_weight.astype(f32).reshape(3 * CONV, width)
    gain_float = out_gain.astype(f32)

    share = out_weight.shape[0] // dp_size
    own_share = lax.dynamic_slice_in_dim(out_weight, groups.me * share, share, 0)
    shares = lax.all_gather(own_share, "heads", axis=0)
    halo_raw = ring.shift(block_input[local_rows - HALO :], 1)
    halo_rows, _ = rms_forward(halo_raw.astype(f32), first_float)
    xn_first, first_scale = rms_forward(rows_float, first_float)
    first_slots = ring.gather(after(xn_first, halo_rows))
    grad_rows = cotangent.astype(f32) * pad_rows[:, None]
    grad_low = grad_rows.astype(bf16)
    table = token_table(doc_ids, pad_float, local_rows)
    old = []
    for k in range(size):
        chunk = lax.rem(me + k, size).reshape(1)
        halo, halo_block = (halo_rows, 0) if k == 0 else (first_slots[k - 1], local_rows // HALO - 1)
        old = mixer_chunk(
            k, chunk, first_slots[k], halo, halo_block, qkv_weight, beta_weight, table, doc_ids,
            conv_float, old,
        )
        if k == 1:
            out_all_heads = lax.all_gather(after(shares, old[3]), "dp", axis=1, tiled=True)
        if k == size - 2:
            grad_all = lax.all_gather(after(grad_low, first_slots[-1], old[3]), "heads", axis=0)
    *pre_all, beta_all, query, key, value, score, inverse = old

    normed, out_all, fresh, starts = mixer_scan(
        me_one, size, query, key, value, score, inverse, beta_all, table, gain_float
    )
    saved = (out_all, fresh, score, inverse, starts)
    blocks = [normed[k * local_rows : (k + 1) * local_rows] for k in range(size)]
    moved = [ring.shift(blocks[k], k) for k in range(1, size)]
    mixed = dot_f32(blocks[0], out_weight)
    for k in range(1, size):
        source = lax.rem(me - k + size, size)
        weight = lax.dynamic_index_in_dim(out_all_heads, source, 0, keepdims=False)
        mixed = mixed + dot_f32(moved[k - 1], weight)
    hidden_one = rows_float + mixed
    xn_second, second_scale = rms_forward(hidden_one, second_float)

    second_slots = ring.gather(xn_second)
    grad_slots, hiddens, gates, ups = [], [], [], []
    total = moving_sum = None
    for k in range(size):
        source = lax.rem(me + k, size)
        if k > 2:
            total = add_low(back, moving_sum)
            moving_sum = ring.back(total)
            second_slots[k] = after(second_slots[k], total)
        if k:
            arrived = after(grad_all, second_slots[k])
            grad_slots.append(lax.dynamic_index_in_dim(arrived, source, 0, keepdims=False))
        else:
            grad_slots.append(grad_low)
        gate = dot_f32(second_slots[k], gate_up_weight[0])
        up = dot_f32(second_slots[k], gate_up_weight[1])
        grad_hidden = dot_nt(grad_slots[k], down_weight)
        sig = sigmoid(gate)
        swish = gate * sig
        hiddens.append((swish * up).astype(bf16))
        gates.append((grad_hidden * up * sig * (1.0 + gate * (1.0 - sig))).astype(bf16))
        ups.append((grad_hidden * swish).astype(bf16))
        back = dot_nt(gates[k], gate_up_weight[0]) + dot_nt(ups[k], gate_up_weight[1])
        if k == 0:
            own_back = back
        elif k == 1:
            moving_sum = ring.back(back.astype(bf16))
    total = add_low(back, moving_sum)
    moving_sum = ring.back(total)
    order.done(total)

    ffn_units = [
        (spots(second_slots), spots(gates)),
        (spots(second_slots), spots(ups)),
        (spots(grad_slots), spots(hiddens)),
    ]
    ffn = Reduction(groups, order, ffn_units, 2)
    ffn.send()
    ffn.keep()
    ffn.advance()
    grad_xn_second = own_back + order.wait(moving_sum).astype(f32)
    grad_part, second_gain_grad = rms_backward(hidden_one, second_scale, second_float, grad_xn_second)
    grad_h1 = grad_rows + grad_part
    mid_slots = [order.done(grad_h1.astype(bf16))]
    downs, normeds = [], []
    for k in range(size):
        if k + 1 < size:
            moving = ring.back(mid_slots[k])
        if k == 0:
            downs = [dot_f32(order.wait(hidden), down_weight) for hidden in hiddens]
            order.done(downs)
        if k + 2 == size:
            ffn.advance()
        normeds.append(order.done(dot_nt(order.wait(mid_slots[k]), out_weight).astype(bf16)))
        if k + 1 < size:
            mid_slots.append(order.wait(moving))
            order.done(mid_slots[-1])
    ffn.advance()
    down_moving = ring.back(order.wait(downs[1 % size].astype(bf16)))
    *grad_pres, grad_logit, conv_part, out_gain_part = mixer_backward(
        me_one, size, pre_all, beta_all, table, doc_ids, conv_float, gain_float, saved,
        order.wait(jnp.concatenate(normeds)),
    )
    grad_logit = order.done(grad_logit.astype(bf16), grad_pres[0])[0]
    down_total = order.done(add_low(downs[2 % size], order.wait(down_moving)))

    def first_partial(k):
        rows = slice(k * local_rows, (k + 1) * local_rows)
        total = dot_nt(order.wait(grad_logit[rows]), beta_weight)
        for i in range(3):
            total = total + dot_nt(order.wait(grad_pres[i][rows]), qkv_weight[i])
        return total

    def gain_share(k, share):
        return jnp.sum(share * first_slots[k].astype(f32), axis=0)

    partial = first_partial(1 % size)
    first_gain_part = gain_share(1 % size, partial)
    total = order.done(partial.astype(bf16))
    moving_sum = ring.back(total)
    ffn.advance()
    qkv = Reduction(
        groups,
        order,
        [
            (spots(first_slots), cuts(grad_pres[0], size)),
            (spots(first_slots), cuts(grad_pres[1], size)),
            (spots(first_slots), cuts(grad_pres[2], size)),
            (spots(mid_slots), cuts(normed, size)),
        ],
        3,
    )
    qkv.send()
    qkv.keep()
    qkv.advance()
    partial = order.done(first_partial(2 % size))
    for k in range(2, size):
        total = order.done(add_low(partial, order.wait(moving_sum)))
        moving_sum = ring.back(total)
        first_gain_part = first_gain_part + gain_share(k, partial)
        partial = order.done(first_partial((k + 1) % size))
        if k == 2:
            while ffn.left():
                ffn.advance()
    first_gain_part = (first_gain_part + gain_share(0, partial)) / first_float
    beta_part = 0.0
    late_logit = order.wait(grad_logit)
    for k in range(size):
        beta_part = beta_part + dot_tn(first_slots[k], late_logit[k * local_rows : (k + 1) * local_rows])
    tiny = (beta_part, conv_part, first_gain_part, second_gain_grad, out_gain_part)
    small = jnp.concatenate([v.reshape(-1) for v in tiny])
    count = beta_part.size
    gains_at = count + conv_part.size

    def hop(vector, bit):
        return order.done(vector + order.wait(groups.swap(vector, bit)))

    qkv.advance()
    small = hop(small, 0)
    grad_xn_first = partial + order.wait(moving_sum).astype(f32)
    grad_x_part, _ = rms_backward(rows_float, first_scale, first_float, grad_xn_first)
    input_grad = order.done(grad_h1 + grad_x_part)
    down_moving = ring.back(order.wait(down_total))
    qkv.advance()
    small = hop(small, 1)
    qkv.advance()
    gate_up_grad, down_grad = ffn.finish()
    for bit in groups.bits[2:]:
        small = hop(small, bit)
    for k in range(3, size):
        down_total = order.done(add_low(downs[k], order.wait(down_moving)))
        down_moving = ring.back(down_total)
    while qkv.left():
        qkv.advance()
    beta_grad = small[:count].reshape(beta_part.shape)
    conv_grad = small[count:gains_at].reshape(3, CONV, width)
    gains = small[gains_at:]
    for bit in bits_of(size):
        moved = lax.ppermute(gains, "heads", [(i, i ^ (1 << bit)) for i in range(size)])
        gains = order.done(gains + order.wait(moved))
    qkv_grad, out_grad = qkv.finish()
    output = hidden_one + downs[0] + order.wait(down_moving).astype(f32)
    block_output = order.done(output.astype(bf16))
    return (
        block_output,
        input_grad,
        gains[:model_width],
        qkv_grad,
        beta_grad,
        conv_grad,
        gains[2 * model_width :],
        out_grad,
        gains[model_width : 2 * model_width],
        gate_up_grad,
        down_grad,
    )


def solution(mesh):
    rows = P(("dp", "heads"), None)
    last = P(None, None, "heads")
    return jax.shard_map(
        functools.partial(shards, mesh.shape["heads"], mesh.shape["dp"]),
        mesh=mesh,
        in_specs=(
            rows, P("dp"), P("dp"), P(), last, P(None, "heads"), last, P(), P("heads", None), P(),
            last, P("heads", None), rows,
        ),
        out_specs=(
            rows, rows, P(), last, P(None, "heads"), last, P(), P("heads", None), P(), last,
            P("heads", None),
        ),
        check_vma=False,
    )
```
